32 devices in a mesh: win: 8 (over z, x), fsdp: 4 (over y, core).
Axes of the slice: x: 2, y: 2, z: 4, core: 2. Of those that a mesh axis runs over, the one named last changes fastest.
Arguments:
- tokens: bfloat16 [4, 56, 14, 1344], P('fsdp', 'win'), may hold values from -6 to 6
- cotangent: bfloat16 [4, 56, 14, 1344], P('fsdp', 'win'), may hold values from -6 to 6
- crop_ids: int32 [4, 56], P('fsdp'), may hold values from 0 to 1, never falling along the last dimension, each value on 1 to 35 neighbouring positions
- params: float32 [2, 124928], P(None, 'fsdp'), may hold values from -5 to 5
- first_moment: float32 [2, 124928], P(None, 'fsdp'), may hold values from -1 to 1
- second_moment: float32 [2, 124928], P(None, 'fsdp'), may hold values from 0 to 1
Outputs:
- block_out: bfloat16 [4, 56, 14, 1344], P('fsdp', 'win')
- input_grad: bfloat16 [4, 56, 14, 1344], P('fsdp', 'win')
- grad_norm: float32 [], replicated
- new_params: float32 [2, 124928], P(None, 'fsdp')
- new_first: float32 [2, 124928], P(None, 'fsdp')
- new_second: float32 [2, 124928], P(None, 'fsdp')
- params_copy: bfloat16 [2, 124928], P(None, 'fsdp')
The draws below stay inside these ranges and needn't reach their ends.
Inputs may be any that keep to these rules, and one draw needn't show every extreme that they name: `crop_ids`: each row numbers 2 crops along the first dimension: 0 at the start, never falling, rising by one at each crop's end, each crop 1 to 35 slices long.
All inputs are finite; a program needn't handle non-finite values.
Results may differ from the reference program's by a relative error of at most 0.019.
Values may be sent and summed in bfloat16 or wider, within the bound.
A program may use at most 256 MiB of HBM per device.

```python
import math
import jax
import jax.numpy as jnp
import numpy as np
from jax import lax

C = 96
HEADS = 6
HEAD = 16
HID = 384
WS = 7
SHIFT = 3
TABLE = 2197
SY = 14
SZ = 14
NX = 56
VOLS = 4
CROPS = 2
CROP_MOST = 35
BP = 124926
BPAD = 124928
STEP = 5


CLIP_LIMIT = 1.0


def kind_list():
    lengths = [3 * C * C, C * C, C * HID, HID * C, TABLE * HEADS, C, C, C, C, C, C, C, HID, C]
    kinds = [0, 1, 2, 3, 4, 5, 6, 6, 6, 6, 5, 6, 6, 6]
    pieces = [jnp.full((extent,), kind_one, jnp.int32) for extent, kind_one in zip(lengths, kinds)]
    pieces.append(jnp.full((BPAD - BP,), 7, jnp.int32))
    return jnp.concatenate(pieces)


def gradient_scale():
    factor = jnp.take(jnp.array([1.0, 1.0, 1.0, 1.0, 3.0, 3.0, 3.0, 1.0], jnp.float32), kind_list())
    return factor * CLIP_LIMIT * (2.0 * BP) ** (-0.5)


def draw_params(key, part):
    kinds = kind_list()
    spreads = jnp.array([C ** (-0.5), max(C // 16, 1) ** (-0.5), C ** (-0.5), HID ** (-0.5), 1.0, 0.0, 0.3, 0.02], jnp.float32)
    spread_all = jnp.take(spreads, kinds)
    normal_part = jnp.clip(jax.random.normal(jax.random.fold_in(key, 11), (2, BPAD), jnp.float32), -5.0, 5.0)
    uniform_part = jax.random.uniform(jax.random.fold_in(key, 12), (2, BPAD), jnp.float32, 0.6, 1.4)
    return jnp.where(kinds == 5, uniform_part, normal_part * spread_all)


def draw_first_moment(key, part):
    normal_part = jnp.clip(jax.random.normal(jax.random.fold_in(key, 21), (2, BPAD), jnp.float32), -5.0, 5.0)
    return normal_part * 0.6 * (0.1 / 0.9) * gradient_scale()


def draw_second_moment(key, part):
    factor = jnp.exp(jax.random.uniform(jax.random.fold_in(key, 31), (2, BPAD), jnp.float32, 0.0, math.log(4.0)))
    scale_all = gradient_scale()
    return factor * (0.001 / 0.999) * scale_all * scale_all


def level_of(own_key, shape, shards, smallest, high):
    def one(dim, parts):
        draws = jax.random.uniform(jax.random.fold_in(jax.random.fold_in(own_key, 6), dim), (parts,), jnp.float32, smallest / len(shards), high / len(shards))
        return jnp.repeat(jnp.exp(draws), shape[dim] // parts).reshape((-1,) + (1,) * (len(shape) - dim - 1))

    gain = one(*shards[0])
    for cut in shards[1:]:
        gain = gain * one(*cut)
    return gain


def length_profile(number_of, total, bound, slope):
    weights = [(1 << 20) // math.isqrt(rank ** slope) + 1 for rank in range(2, number_of + 1)]
    surplus, counts = total - bound - (number_of - 1), [1] * (number_of - 1)
    while surplus > 0:
        movable = [i for i in range(number_of - 1) if counts[i] < bound]
        pool, budget = sum([weights[i] for i in movable]), surplus
        for i in movable:
            more = min(bound - counts[i], max(1, budget * weights[i] // pool), surplus)
            counts[i] = counts[i] + more
            surplus = surplus - more
    return np.array([bound] + counts)


def ragged(own_key, number_of, total, most, skew):
    if number_of == 2:
        one = jax.random.randint(own_key, (), max(1, total - most), min(most, total - 1) + 1)
        return jnp.stack([one, total - one])
    sizes = jnp.asarray(length_profile(number_of, total, most, skew), jnp.int32)
    couples = (number_of - 1) // 2
    source_of, receiver = sizes[1:1 + 2 * couples:2], sizes[2:2 + 2 * couples:2]
    margin = jnp.minimum(source_of - 1, most - receiver)
    moved = jax.random.randint(jax.random.fold_in(own_key, 1), (couples,), 0, 1 << 20) % (margin + 1)
    sizes = sizes.at[1:1 + 2 * couples:2].set(source_of - moved).at[2:2 + 2 * couples:2].set(receiver + moved)
    return sizes[jax.random.permutation(jax.random.fold_in(own_key, 2), number_of)]


def centred(rng, shape, spread, bound, split=(), kind=jnp.bfloat16):
    values = jax.random.normal(rng, shape, jnp.float32) * spread
    if len(split) > 0:
        values = level_of(rng, shape, split, -0.22, 0.18) * values
    return jnp.clip(values, min=-bound, max=bound).astype(kind)


def setup_inputs(seed: int = 0) -> dict:
    splits = jax.random.split(jax.random.key(seed), 7)
    tokens = centred(splits[0], (VOLS, NX, SY, SZ * C), 1.0, 6.0, ((0, 4), (1, 8)))
    cotangent = centred(splits[1], (VOLS, NX, SY, SZ * C), 1.0, 6.0, ((0, 4), (1, 8)))
    crop_ids = jax.vmap(lambda own: jnp.searchsorted(jnp.cumsum(ragged(own, CROPS, NX, CROP_MOST, 1)), jnp.arange(NX), side="right"))(jax.random.split(splits[2], VOLS)).reshape((VOLS, NX)).astype(jnp.int32)
    params = draw_params(jax.random.fold_in(splits[6], 71), 0)
    first_moment = draw_first_moment(jax.random.fold_in(splits[6], 71), 0)
    second_moment = draw_second_moment(jax.random.fold_in(splits[6], 71), 0)
    return dict(tokens=tokens, cotangent=cotangent, crop_ids=crop_ids, params=params, first_moment=first_moment, second_moment=second_moment)


@jax.custom_vjp
def low(v):
    return lax.optimization_barrier(v.astype(jnp.bfloat16)).astype(jnp.float32)

@jax.custom_vjp
def low_back(v):
    return v

def low_keep(v):
    return (low(v), None)

def low_pass(kept, grad):
    return (grad,)

def back_keep(v):
    return (v, None)

def back_low(kept, grad):
    return (low(grad),)
low.defvjp(low_keep, low_pass)
low_back.defvjp(back_keep, back_low)
EPS_NORM = 1e-05
CLIP_LIMIT = 1.0
LEARN_RATE = 0.4
BETA_FIRST = 0.9
BETA_SECOND = 0.999
WEIGHT_DECAY = 0.05
EPS_ADAM = 1e-08
MASK_FILL = -1e+30
HIGHEST = lax.Precision.HIGHEST

def round_both(values):
    return low(low_back(values))

def piece_sizes():
    return [C * 3 * C, C * C, C * HID, HID * C, TABLE * HEADS, C, C, C, C, C, C, C, HID, C]

def split_block(flat_row):
    shapes = [(C, 3 * C), (C, C), (C, HID), (HID, C), (TABLE, HEADS), (C,), (C,), (C,), (C,), (C,), (C,), (C,), (HID,), (C,)]
    pieces = []
    offset = 0
    for extent, shape_one in zip(piece_sizes(), shapes):
        pieces.append(flat_row[offset:offset + extent].reshape(shape_one))
        offset = offset + extent
    return pieces

def relative_index():
    spots_all = jnp.arange(WS ** 3)
    coord_a = spots_all // (WS * WS)
    coord_b = spots_all // WS % WS
    coord_c = spots_all % WS
    table_span = 2 * WS - 1

    def differ(coord_one):
        return coord_one[:, None] - coord_one[None, :] + WS - 1
    return (differ(coord_a) * table_span + differ(coord_b)) * table_span + differ(coord_c)

def region_labels(extent):
    spots_all = jnp.arange(extent)
    return (spots_all >= extent - WS).astype(jnp.int32) + (spots_all >= extent - SHIFT).astype(jnp.int32)

def to_windows(values):
    extent_x, extent_y, extent_z = values.shape[:3]
    trailing = values.shape[3:]
    blocked = values.reshape((extent_x // WS, WS, extent_y // WS, WS, extent_z // WS, WS) + trailing)
    axes_order = (0, 2, 4, 1, 3, 5) + tuple(range(6, 6 + len(trailing)))
    return blocked.transpose(axes_order).reshape((-1, WS ** 3) + trailing)

def from_windows(windows, extent_x, extent_y, extent_z):
    trailing = windows.shape[2:]
    blocked = windows.reshape((extent_x // WS, extent_y // WS, extent_z // WS, WS, WS, WS) + trailing)
    axes_order = (0, 3, 1, 4, 2, 5) + tuple(range(6, 6 + len(trailing)))
    return blocked.transpose(axes_order).reshape((extent_x, extent_y, extent_z) + trailing)

def layer_norm(values, gain_row, bias_row):
    centered = values - lax.optimization_barrier(jnp.mean(values, axis=-1, keepdims=True))
    variance = lax.optimization_barrier(jnp.mean(centered * centered, axis=-1, keepdims=True))
    return centered * lax.rsqrt(variance + EPS_NORM) * gain_row + bias_row

def window_attention(normed_wins, label_wins, w_qkv, bias_all, table_bias):
    window_count = normed_wins.shape[0]
    group_size = math.gcd(window_count, 8)
    stacked = normed_wins.reshape(window_count // group_size, group_size, WS ** 3, C)
    label_stack = label_wins.reshape(window_count // group_size, group_size, WS ** 3)

    def one_group(inputs):
        block_normed, block_labels = inputs
        qkv = round_both(jnp.einsum('wtc,cf->wtf', block_normed, w_qkv, precision=HIGHEST) + bias_all)
        split_qkv = qkv.reshape(group_size, WS ** 3, 3, HEADS, HEAD)
        queries = split_qkv[:, :, 0]
        key_rows = split_qkv[:, :, 1]
        value_rows = split_qkv[:, :, 2]
        scores = HEAD ** (-0.5) * jnp.einsum('wqhd,wkhd->whqk', queries, key_rows, precision=HIGHEST) + table_bias[None]
        scores = low_back(scores)
        allowed = (block_labels[:, :, None] == block_labels[:, None, :])[:, None]
        soft_weights = jax.nn.softmax(jnp.where(allowed, scores, MASK_FILL), axis=-1)
        attended = jnp.einsum('whqk,wkhd->wqhd', low(soft_weights), value_rows, precision=HIGHEST)
        return round_both(attended.reshape(group_size, WS ** 3, C))
    result = lax.map(jax.checkpoint(one_group), (stacked, label_stack))
    return result.reshape(window_count, WS ** 3, C)

def swin_block(cell_values, labels, weights, rel_index, shifted):
    w_qkv, w_proj, w_one, w_two, bias_table, gain_one, bias_one, bias_query, bias_value, bias_proj, gain_two, bias_two, bias_hidden, bias_out = weights
    extent_x, extent_y, extent_z = cell_values.shape[:3]
    normed = low(layer_norm(cell_values, gain_one, bias_one))
    if shifted:
        normed = jnp.roll(low_back(normed), (-SHIFT, -SHIFT, -SHIFT), axis=(0, 1, 2))
    windows = to_windows(normed)
    label_wins = to_windows(labels)
    bias_all = jnp.concatenate([bias_query, jnp.zeros_like(bias_query), bias_value])
    table_bias = bias_table[rel_index].transpose(2, 0, 1)
    attended = from_windows(window_attention(windows, label_wins, w_qkv, bias_all, table_bias), extent_x, extent_y, extent_z)
    if shifted:
        attended = jnp.roll(attended, (SHIFT, SHIFT, SHIFT), axis=(0, 1, 2))
    branch = round_both(jnp.einsum('xyzc,cf->xyzf', attended, w_proj, precision=HIGHEST) + bias_proj)
    middle = cell_values + branch
    normed_two = low(layer_norm(middle, gain_two, bias_two))
    hidden = low_back(jnp.einsum('xyzc,cf->xyzf', normed_two, w_one, precision=HIGHEST) + bias_hidden)
    active = low(jax.nn.gelu(hidden, approximate=False))
    result = low_back(jnp.einsum('xyzf,fc->xyzc', active, w_two, precision=HIGHEST) + bias_out)
    return middle + result

def forward_all(flat_both, grids, crop_ids):
    first_weights = split_block(low(flat_both[0]))
    second_weights = split_block(low(flat_both[1]))
    rel_index = relative_index()

    def one_volume(inputs):
        cell_values, crop_row = inputs
        labels_plain = jnp.broadcast_to(9 * crop_row[:, None, None], (NX, SY, SZ))
        first = swin_block(cell_values, labels_plain, first_weights, rel_index, False)
        crop_rolled = jnp.roll(crop_row, -SHIFT)
        labels_shift = 9 * crop_rolled[:, None, None] + 3 * region_labels(SY)[None, :, None] + region_labels(SZ)[None, None, :]
        return swin_block(first, labels_shift, second_weights, rel_index, True)
    return lax.map(jax.checkpoint(one_volume), (grids, crop_ids))

def reference(tokens, cotangent, crop_ids, params, first_moment, second_moment):
    grids = tokens.astype(jnp.float32).reshape(VOLS, NX, SY, SZ, C)
    outputs, pullback = jax.vjp(lambda flat_both, cell_grids: forward_all(flat_both, cell_grids, crop_ids), params, grids)
    grad_params, grad_grids = pullback(cotangent.astype(jnp.float32).reshape(VOLS, NX, SY, SZ, C))
    block_out = outputs.reshape(VOLS, NX, SY, SZ * C).astype(jnp.bfloat16)
    input_grad = grad_grids.reshape(VOLS, NX, SY, SZ * C).astype(jnp.bfloat16)
    grad_norm = jnp.sqrt(jnp.sum(grad_params * grad_params))
    clipped = grad_params * jnp.minimum(1.0, CLIP_LIMIT / (grad_norm + 1e-06))
    new_first = BETA_FIRST * first_moment + (1.0 - BETA_FIRST) * clipped
    new_second = BETA_SECOND * second_moment + (1.0 - BETA_SECOND) * clipped * clipped
    first_hat = new_first / (1.0 - BETA_FIRST ** STEP)
    second_hat = new_second / (1.0 - BETA_SECOND ** STEP)
    new_params = params - LEARN_RATE * (first_hat / (jnp.sqrt(second_hat) + EPS_ADAM) + WEIGHT_DECAY * params)
    return (block_out, input_grad, grad_norm, new_params, new_first, new_second, new_params.astype(jnp.bfloat16))
```

```python
import math

import jax
import jax.numpy as jnp
from jax import lax
from jax.sharding import PartitionSpec as P

C = 96
HEADS = 6
HEAD = 16
HID = 384
WS = 7
SHIFT = 3
TABLE = 2197
SY = 14
SZ = 14
BPAD = 124928
STEP = 5


EPS_NORM = 1e-05
CLIP_LIMIT = 1.0
LEARN_RATE = 0.4
BETA_FIRST = 0.9
BETA_SECOND = 0.999
WEIGHT_DECAY = 0.05
EPS_ADAM = 1e-08
MASK_FILL = -1e30


def shifted_2(shard, axis, by):
    size = lax.axis_size(axis)
    return lax.ppermute(shard, axis, [(i, (i + by) % size) for i in range(size)])


def piece_sizes():
    return [C * 3 * C, C * C, C * HID, HID * C, TABLE * HEADS, C, C, C, C, C, C, C, HID, C]


def split_block(flat_row):
    shapes = [
        (C, 3 * C),
        (C, C),
        (C, HID),
        (HID, C),
        (TABLE, HEADS),
        (C,),
        (C,),
        (C,),
        (C,),
        (C,),
        (C,),
        (C,),
        (HID,),
        (C,),
    ]
    pieces = []
    offset = 0
    for extent, shape_one in zip(piece_sizes(), shapes):
        pieces.append(flat_row[offset : offset + extent].reshape(shape_one))
        offset = offset + extent
    return pieces


def pack_block(grads_list):
    flat_row = jnp.concatenate([member.reshape(-1) for member in grads_list])
    return jnp.pad(flat_row, (0, BPAD - flat_row.shape[0]))


def relative_index():
    spots_all = jnp.arange(WS**3)
    coord_a = spots_all // (WS * WS)
    coord_b = spots_all // WS % WS
    coord_c = spots_all % WS
    table_span = 2 * WS - 1

    def differ(coord_one):
        return coord_one[:, None] - coord_one[None, :] + WS - 1

    return (differ(coord_a) * table_span + differ(coord_b)) * table_span + differ(coord_c)


def expand_table(bias_table):
    span = 2 * WS - 1
    cube = bias_table.T.reshape(HEADS, span, span, span)
    cube = jnp.stack([cube[:, :, :, WS - 1 - k : 2 * WS - 1 - k] for k in range(WS)], axis=1)
    cube = jnp.stack([cube[:, :, :, WS - 1 - k : 2 * WS - 1 - k] for k in range(WS)], axis=1)
    cube = jnp.stack([cube[:, :, :, WS - 1 - k : 2 * WS - 1 - k] for k in range(WS)], axis=1)
    return cube.reshape(HEADS, WS**3, WS**3).transpose(0, 2, 1)


def collapse_table(d_full):
    pull = jax.linear_transpose(
        expand_table, jax.ShapeDtypeStruct((TABLE, HEADS), jnp.float32)
    )
    return pull(d_full)[0]


def region_labels(extent):
    spots_all = jnp.arange(extent)
    return (spots_all >= extent - WS).astype(jnp.int32) + (spots_all >= extent - SHIFT).astype(
        jnp.int32
    )


def to_windows(values):
    extent_x, extent_y, extent_z = values.shape[:3]
    trailing = values.shape[3:]
    blocked = values.reshape(
        (extent_x // WS, WS, extent_y // WS, WS, extent_z // WS, WS) + trailing
    )
    axes_order = (0, 2, 4, 1, 3, 5) + tuple(range(6, 6 + len(trailing)))
    return blocked.transpose(axes_order).reshape((-1, WS**3) + trailing)


def from_windows(windows, extent_x, extent_y, extent_z):
    trailing = windows.shape[2:]
    blocked = windows.reshape(
        (extent_x // WS, extent_y // WS, extent_z // WS, WS, WS, WS) + trailing
    )
    axes_order = (0, 3, 1, 4, 2, 5) + tuple(range(6, 6 + len(trailing)))
    return blocked.transpose(axes_order).reshape((extent_x, extent_y, extent_z) + trailing)


def layer_norm(values, gain_row, bias_row):
    centered = values - jnp.mean(values, axis=-1, keepdims=True)
    variance = jnp.mean(centered * centered, axis=-1, keepdims=True)
    return centered * lax.rsqrt(variance + EPS_NORM) * gain_row + bias_row


def gelu_exact(values):
    return jax.nn.gelu(values, approximate=False)


def gather_block(shard_row):
    whole = lax.all_gather(shard_row.astype(jnp.bfloat16), "fsdp", axis=0, tiled=True)
    return split_block(whole)


def masked_scores(queries, key_rows, block_labels, table_bias):
    scores = (
        HEAD ** (-0.5)
        * jnp.einsum("wqhd,wkhd->whqk", queries, key_rows, preferred_element_type=jnp.float32)
        + table_bias[None]
    )
    allowed = (block_labels[:, :, None] == block_labels[:, None, :])[:, None]
    return jnp.where(allowed, scores, MASK_FILL)


def attention_forward(qkv_wins, label_wins, table_bias):
    window_count = qkv_wins.shape[0]
    group_size = math.gcd(window_count, 2)
    stacked = qkv_wins.reshape(window_count // group_size, group_size, WS**3, 3, HEADS, HEAD)
    label_stack = label_wins.reshape(window_count // group_size, group_size, WS**3)

    def one_group(inputs):
        block_qkv, block_labels = inputs
        queries = block_qkv[:, :, 0]
        key_rows = block_qkv[:, :, 1]
        value_rows = block_qkv[:, :, 2]
        masked = masked_scores(queries, key_rows, block_labels, table_bias)
        highest = jnp.max(masked, axis=-1, keepdims=True)
        log_total = highest + jnp.log(jnp.sum(jnp.exp(masked - highest), axis=-1, keepdims=True))
        soft_weights = jnp.exp(masked - log_total).astype(jnp.bfloat16)
        attended = jnp.einsum(
            "whqk,wkhd->wqhd", soft_weights, value_rows, preferred_element_type=jnp.float32
        )
        return (attended.astype(jnp.bfloat16), log_total[..., 0])

    attended, log_totals = lax.map(one_group, (stacked, label_stack))
    return (attended.reshape(window_count, WS**3, C), log_totals)


def attention_backward(qkv_wins, label_wins, table_bias, log_totals, d_attended):
    window_count = qkv_wins.shape[0]
    group_size = math.gcd(window_count, 2)
    stacked = qkv_wins.reshape(window_count // group_size, group_size, WS**3, 3, HEADS, HEAD)
    label_stack = label_wins.reshape(window_count // group_size, group_size, WS**3)
    grad_stack = d_attended.reshape(window_count // group_size, group_size, WS**3, HEADS, HEAD)

    def one_group(table_total, inputs):
        block_qkv, block_labels, block_log, block_grad = inputs
        queries = block_qkv[:, :, 0]
        key_rows = block_qkv[:, :, 1]
        value_rows = block_qkv[:, :, 2]
        masked = masked_scores(queries, key_rows, block_labels, table_bias)
        soft_exact = jnp.exp(masked - block_log[..., None])
        d_soft = jnp.einsum(
            "wqhd,wkhd->whqk", block_grad, value_rows, preferred_element_type=jnp.float32
        )
        inner_sum = jnp.sum(d_soft * soft_exact, axis=-1, keepdims=True)
        d_scores = (soft_exact * (d_soft - inner_sum)).astype(jnp.bfloat16)
        d_values = jnp.einsum(
            "whqk,wqhd->wkhd",
            soft_exact.astype(jnp.bfloat16),
            block_grad,
            preferred_element_type=jnp.float32,
        )
        d_queries = HEAD ** (-0.5) * jnp.einsum(
            "whqk,wkhd->wqhd", d_scores, key_rows, preferred_element_type=jnp.float32
        )
        d_keys = HEAD ** (-0.5) * jnp.einsum(
            "whqk,wqhd->wkhd", d_scores, queries, preferred_element_type=jnp.float32
        )
        d_triple = jnp.stack([d_queries, d_keys, d_values], axis=2).astype(jnp.bfloat16)
        return (table_total + jnp.sum(d_scores.astype(jnp.float32), axis=0), d_triple)

    start_table = jnp.zeros((HEADS, WS**3, WS**3), jnp.float32)
    d_table_full, d_qkv = lax.scan(
        one_group, start_table, (stacked, label_stack, log_totals, grad_stack)
    )
    return (d_qkv.reshape(window_count, WS**3, 3 * C), d_table_full)


def block_forward(cell_values, labels, weights, rel_index, shifted):
    (
        w_qkv,
        w_proj,
        w_one,
        w_two,
        bias_table,
        gain_one,
        bias_one,
        bias_query,
        bias_value,
        bias_proj,
        gain_two,
        bias_two,
        bias_hidden,
        bias_out,
    ) = weights
    extent_x = cell_values.shape[0]
    normed, norm_one_pull = jax.vjp(
        layer_norm, cell_values, gain_one.astype(jnp.float32), bias_one.astype(jnp.float32)
    )
    normed = normed.astype(jnp.bfloat16)
    if shifted:
        halo_slab = shifted_2(normed[:SHIFT], "win", -1)
        region = jnp.concatenate([normed[SHIFT:], halo_slab], axis=0)
        region = jnp.roll(region, (-SHIFT, -SHIFT), axis=(1, 2))
    else:
        region = normed
    windows = to_windows(region)
    label_wins = to_windows(labels)
    bias_all = jnp.concatenate([bias_query, jnp.zeros_like(bias_query), bias_value]).astype(
        jnp.float32
    )
    qkv_flat = jnp.dot(windows.reshape(-1, C), w_qkv, preferred_element_type=jnp.float32) + bias_all
    qkv_wins = qkv_flat.astype(jnp.bfloat16).reshape(-1, WS**3, 3 * C)
    table_bias = expand_table(bias_table.astype(jnp.float32))
    attended_wins, log_totals = attention_forward(qkv_wins, label_wins, table_bias)
    attended = from_windows(attended_wins, extent_x, SY, SZ)
    if shifted:
        attended = jnp.roll(attended, (SHIFT, SHIFT), axis=(1, 2))
    branch = jnp.dot(
        attended.reshape(-1, C), w_proj, preferred_element_type=jnp.float32
    ) + bias_proj.astype(jnp.float32)
    branch = branch.astype(jnp.bfloat16).reshape(extent_x, SY, SZ, C)
    if shifted:
        incoming = shifted_2(branch[extent_x - SHIFT :], "win", 1)
        branch = jnp.concatenate([incoming, branch[: extent_x - SHIFT]], axis=0)
    middle = cell_values + branch.astype(jnp.float32)
    normed_two, norm_two_pull = jax.vjp(
        layer_norm, middle, gain_two.astype(jnp.float32), bias_two.astype(jnp.float32)
    )
    normed_two = normed_two.astype(jnp.bfloat16).reshape(-1, C)
    hidden = jnp.dot(normed_two, w_one, preferred_element_type=jnp.float32) + bias_hidden.astype(
        jnp.float32
    )
    active, gelu_pull = jax.vjp(gelu_exact, hidden)
    active = active.astype(jnp.bfloat16)
    result = jnp.dot(active, w_two, preferred_element_type=jnp.float32) + bias_out.astype(
        jnp.float32
    )
    output = middle + result.reshape(extent_x, SY, SZ, C)
    kept = (
        norm_one_pull,
        windows,
        label_wins,
        qkv_wins,
        table_bias,
        log_totals,
        attended,
        norm_two_pull,
        normed_two,
        gelu_pull,
        active,
    )
    return (output, kept)


def block_backward(d_output, kept, weights, rel_index, shifted):
    (
        w_qkv,
        w_proj,
        w_one,
        w_two,
        bias_table,
        gain_one,
        bias_one,
        bias_query,
        bias_value,
        bias_proj,
        gain_two,
        bias_two,
        bias_hidden,
        bias_out,
    ) = weights
    (
        norm_one_pull,
        windows,
        label_wins,
        qkv_wins,
        table_bias,
        log_totals,
        attended,
        norm_two_pull,
        normed_two,
        gelu_pull,
        active,
    ) = kept
    extent_x = d_output.shape[0]
    d_result = d_output.reshape(-1, C).astype(jnp.bfloat16)
    grad_bias_out = jnp.sum(d_result.astype(jnp.float32), axis=0)
    grad_w_two = jnp.dot(active.T, d_result, preferred_element_type=jnp.float32)
    d_active = jnp.dot(d_result, w_two.T, preferred_element_type=jnp.float32)
    d_hidden = gelu_pull(d_active)[0].astype(jnp.bfloat16)
    grad_bias_hidden = jnp.sum(d_hidden.astype(jnp.float32), axis=0)
    grad_w_one = jnp.dot(normed_two.T, d_hidden, preferred_element_type=jnp.float32)
    d_normed_two = jnp.dot(d_hidden, w_one.T, preferred_element_type=jnp.float32)
    d_middle_norm, grad_gain_two, grad_bias_two = norm_two_pull(
        d_normed_two.reshape(extent_x, SY, SZ, C)
    )
    d_middle = d_output + d_middle_norm
    d_branch = d_middle.astype(jnp.bfloat16)
    if shifted:
        returned = shifted_2(d_branch[:SHIFT], "win", -1)
        d_branch = jnp.concatenate([d_branch[SHIFT:], returned], axis=0)
    d_branch_flat = d_branch.reshape(-1, C)
    grad_bias_proj = jnp.sum(d_branch_flat.astype(jnp.float32), axis=0)
    grad_w_proj = jnp.dot(
        attended.reshape(-1, C).T, d_branch_flat, preferred_element_type=jnp.float32
    )
    d_attended = jnp.dot(d_branch_flat, w_proj.T, preferred_element_type=jnp.float32)
    d_attended = d_attended.astype(jnp.bfloat16).reshape(extent_x, SY, SZ, C)
    if shifted:
        d_attended = jnp.roll(d_attended, (-SHIFT, -SHIFT), axis=(1, 2))
    d_qkv, d_table_full = attention_backward(
        qkv_wins, label_wins, table_bias, log_totals, to_windows(d_attended)
    )
    d_qkv_flat = d_qkv.reshape(-1, 3 * C)
    grad_w_qkv = jnp.dot(windows.reshape(-1, C).T, d_qkv_flat, preferred_element_type=jnp.float32)
    column_sums = jnp.sum(d_qkv_flat.astype(jnp.float32), axis=0)
    grad_bias_query = column_sums[:C]
    grad_bias_value = column_sums[2 * C :]
    grad_table = collapse_table(d_table_full)
    d_region = jnp.dot(d_qkv_flat, w_qkv.T, preferred_element_type=jnp.float32)
    d_region = from_windows(d_region.reshape(-1, WS**3, C), extent_x, SY, SZ)
    if shifted:
        d_region = jnp.roll(d_region, (SHIFT, SHIFT), axis=(1, 2)).astype(jnp.bfloat16)
        sent_back = shifted_2(d_region[extent_x - SHIFT :], "win", 1)
        d_normed = jnp.concatenate([sent_back, d_region[: extent_x - SHIFT]], axis=0).astype(
            jnp.float32
        )
    else:
        d_normed = d_region
    d_cells_norm, grad_gain_one, grad_bias_one = norm_one_pull(d_normed)
    d_cells = d_middle + d_cells_norm
    grads_list = [
        grad_w_qkv,
        grad_w_proj,
        grad_w_one,
        grad_w_two,
        grad_table,
        grad_gain_one,
        grad_bias_one,
        grad_bias_query,
        grad_bias_value,
        grad_bias_proj,
        grad_gain_two,
        grad_bias_two,
        grad_bias_hidden,
        grad_bias_out,
    ]
    return (d_cells, grads_list)


def reduce_block(flat_grad):
    summed = lax.psum(flat_grad.astype(jnp.bfloat16), "win")
    return lax.psum_scatter(summed, "fsdp", scatter_dimension=0, tiled=True).astype(jnp.float32)


def per_device(tokens, cotangent, crop_ids, params, first_moment, second_moment):
    extent_x = tokens.shape[1]
    position = lax.axis_index("win")
    total_x = extent_x * lax.axis_size("win")
    cell_values = tokens[0].astype(jnp.float32).reshape(extent_x, SY, SZ, C)
    crop_row = crop_ids[0]
    spots_x = jnp.arange(extent_x)
    crops_plain = jnp.take(crop_row, position * extent_x + spots_x)
    crops_shift = jnp.take(crop_row, (position * extent_x + SHIFT + spots_x) % total_x)
    labels_plain = jnp.broadcast_to(9 * crops_plain[:, None, None], (extent_x, SY, SZ))
    labels_shift = (
        9 * crops_shift[:, None, None]
        + 3 * region_labels(SY)[None, :, None]
        + region_labels(SZ)[None, None, :]
    )
    rel_index = relative_index().reshape(-1)
    first_weights = gather_block(params[0])
    first_out, first_kept = block_forward(
        cell_values, labels_plain, first_weights, rel_index, False
    )
    second_weights = gather_block(params[1])
    second_out, second_kept = block_forward(
        first_out, labels_shift, second_weights, rel_index, True
    )
    d_final = cotangent[0].astype(jnp.float32).reshape(extent_x, SY, SZ, C)
    d_first, second_grads = block_backward(d_final, second_kept, second_weights, rel_index, True)
    d_input, first_grads = block_backward(d_first, first_kept, first_weights, rel_index, False)
    shard_first = reduce_block(pack_block(first_grads))
    shard_second = reduce_block(pack_block(second_grads))
    shards = jnp.stack([shard_first, shard_second])
    grad_norm = jnp.sqrt(lax.psum(jnp.sum(shards * shards), "fsdp"))
    clipped = shards * jnp.minimum(1.0, CLIP_LIMIT / (grad_norm + 1e-06))
    new_first = BETA_FIRST * first_moment + (1.0 - BETA_FIRST) * clipped
    new_second = BETA_SECOND * second_moment + (1.0 - BETA_SECOND) * clipped * clipped
    first_hat = new_first / (1.0 - BETA_FIRST**STEP)
    second_hat = new_second / (1.0 - BETA_SECOND**STEP)
    new_params = params - LEARN_RATE * (
        first_hat / (jnp.sqrt(second_hat) + EPS_ADAM) + WEIGHT_DECAY * params
    )
    block_out = second_out.reshape(1, extent_x, SY, SZ * C).astype(jnp.bfloat16)
    input_grad = d_input.reshape(1, extent_x, SY, SZ * C).astype(jnp.bfloat16)
    return (
        block_out,
        input_grad,
        grad_norm,
        new_params,
        new_first,
        new_second,
        new_params.astype(jnp.bfloat16),
    )


def solution(mesh):
    return jax.shard_map(
        per_device,
        mesh=mesh,
        in_specs=(
            P("fsdp", "win", None, None),
            P("fsdp", "win", None, None),
            P("fsdp", None),
            P(None, "fsdp"),
            P(None, "fsdp"),
            P(None, "fsdp"),
        ),
        out_specs=(
            P("fsdp", "win", None, None),
            P("fsdp", "win", None, None),
            P(),
            P(None, "fsdp"),
            P(None, "fsdp"),
            P(None, "fsdp"),
            P(None, "fsdp"),
        ),
        check_vma=False,
    )
```

```python
import functools

import jax
import jax.numpy as jnp
import numpy as np
from jax import lax
from jax.experimental import pallas as pl
from jax.experimental.pallas import tpu as pltpu
from jax.sharding import PartitionSpec as P

C = 96
HEADS = 6
HEAD = 16
HID = 384
WS = 7
SHIFT = 3
SY = 14
SZ = 14
BPAD = 124928
STEP = 5
EPS_NORM = 1e-05
CLIP_LIMIT = 1.0
LEARN_RATE = 0.4
BETA_FIRST = 0.9
BETA_SECOND = 0.999
WEIGHT_DECAY = 0.05
EPS_ADAM = 1e-08
BIG = 1e30
LOG2E = 1.4426950408889634
LN2 = 0.6931471805599453

CELLS = WS**3
KROW = 352
QLANE = 384
FLAT = BPAD // 128
ROW_PROJ = 216
ROW_ONE = 288
ROW_TWO = 576
ROW_TABLE = 864
ROW_TAIL = 966
V_GAIN1, V_BIAS1, V_BQ, V_BV, V_BPROJ, V_GAIN2, V_BIAS2, V_BHID, V_BOUT = (
    0, 96, 192, 288, 384, 480, 576, 672, 1056,
)

F32 = jnp.float32
BF16 = jnp.bfloat16


def nn(a, b):
    return lax.dot_general(a, b, (((1,), (0,)), ((), ())), preferred_element_type=F32)


def nt(a, b):
    return lax.dot_general(a, b, (((1,), (1,)), ((), ())), preferred_element_type=F32)


def iota(shape, dim):
    return lax.broadcasted_iota(jnp.int32, shape, dim)


def roll(x, by):
    by = by % 128
    return x if by == 0 else pltpu.roll(x, by, 1)


def skew(x, by):
    while by > 0:
        some = min(1 << (by.bit_length() - 1), 16)
        x = pltpu.roll(x, 0, 1, stride=some, stride_axis=0)
        by -= some
    return x


def constant_tables():
    t = np.arange(QLANE)
    live = t < CELLS
    z, x, y = t // 49, t % 49 // 7, t % 7
    ints = np.full((8, QLANE), -1, np.int32)
    for s in range(2):
        for wy in range(2):
            cell_y = (y + 7 * wy + SHIFT * s) % SY
            ints[2 * s + wy] = np.where(live, z * 128 + x * 16 + cell_y, -1)
    ints[4] = np.where(live, z * 128 + t % 49, -1)
    ints[5] = np.where(live, x, -1)
    lane = np.arange(128)
    ints[6, :128] = np.where(lane < 49, 13 * (lane // 7) + lane % 7, -1000)
    marks = np.zeros((64, QLANE), np.float32)
    for i in range(7):
        marks[i] = live & (x == i)
        marks[7 + i] = live & (y == i)
        marks[14 + i] = live & (z == i)
        marks[32 + 7 + i] = live & ((i >= 4) != (y >= 4))
        marks[32 + 14 + i] = live & ((i >= 4) != (z >= 4))
    return jnp.asarray(ints), jnp.asarray(marks, BF16)


def unit_copy(pieces, units):
    out = None
    for at, unit in enumerate(units):
        if unit is None:
            continue
        i, g = unit
        moved = roll(pieces[i], 32 * (at - g))
        group = iota(moved.shape, 1) // 32
        base = jnp.zeros_like(moved) if out is None else out
        out = jnp.where(group == at, moved, base)
    return out


def read_matrix(flat, base, rows, width, store):
    units = width // 32
    if units % 4 == 0:
        step = units // 4
        for o in range(step):
            store(0, 1, o, flat[pl.ds(base + o, rows, stride=step), :])
        return
    groups = rows // 4
    loaded = [flat[pl.ds(base + o, groups, stride=units), :] for o in range(units)]
    for j in range(4):
        for p in range(units // 3):
            first = units * j + 3 * p
            store(j, 4, p, unit_copy(loaded, [divmod(first + s, 4) for s in range(3)] + [None]))


def write_matrix(flat, base, rows, width, load):
    units = width // 32
    if units % 4 == 0:
        step = units // 4
        for o in range(step):
            flat[pl.ds(base + o, rows, stride=step), :] = load(0, 1, o)
        return
    groups = rows // 4
    parts = units // 3
    loaded = [load(j, 4, p) for j in range(4) for p in range(parts)]
    for o in range(units):
        flat[pl.ds(base + o, groups, stride=units), :] = unit_copy(
            loaded, [divmod(4 * o + g, 3) for g in range(4)]
        )


def build_selectors(ints, select, place, spread):
    for s in range(2):
        for wy in range(2):
            need = ints[2 * s + wy : 2 * s + wy + 1, :]
            for r in range(7):
                row = iota((128, QLANE), 0) + 128 * r
                select[s, 128 * r : 128 * r + 128, QLANE * wy : QLANE * wy + QLANE] = jnp.where(
                    row == need, 1.0, 0.0
                ).astype(BF16)
    need = ints[4:5, :]
    for r in range(7):
        row = iota((128, QLANE), 0) + 128 * r
        place[128 * r : 128 * r + 128, :] = jnp.where(row == need, 1.0, 0.0).astype(BF16)
    gap = iota((176, 128), 0) - ints[6:7, :128]
    for k in range(49):
        hit = gap == 84 - 13 * (k // 7) - k % 7
        spread[:, 128 * k : 128 * k + 128] = jnp.where(hit, 1.0, 0.0).astype(BF16)


def table_pick(second):
    row = iota((176, 104), 0)
    col = iota((176, 104), 1) - second
    at = 128 * col
    start = 78 * row
    hit = (start >= at) & (start < at + 128) & (row < 169)
    return jnp.where(hit, 1.0, 0.0).astype(BF16)


def table_start():
    row = iota((176, 128), 0)
    return jnp.bitwise_and(78 * row, 127)


def build_table(flat, spread, place, tiles, table):
    rows = flat[ROW_TABLE : ROW_TABLE + 104, :].astype(BF16)
    first = skew(nn(table_pick(0), rows), 50)
    second = skew(nn(table_pick(1), rows), 50)
    lane = iota((176, 128), 1)
    mixed = jnp.where(lane + table_start() < 128, first, second)
    mixed = jnp.where((lane < 78) & (iota((176, 128), 0) < 169), mixed, 0.0)
    turned = jnp.concatenate([mixed, jnp.zeros((80, 128), F32)], axis=0).T
    cube = turned[:80, :176].astype(BF16)
    for k in range(49):
        tiles[pl.ds(k, 80, stride=56), :] = nn(cube, spread[:, 128 * k : 128 * k + 128])
    for ck in range(7):
        lhs = jnp.concatenate(
            [tiles[336 * (cq - ck + 6) : 336 * (cq - ck + 7), :].astype(BF16) for cq in range(7)],
            axis=1,
        )
        block = nn(lhs, place[...]) * LOG2E
        for h in range(HEADS):
            table[h, 49 * ck : 49 * ck + 49, :] = block[56 * h : 56 * h + 49, :]
    for h in range(HEADS):
        table[h, CELLS:KROW, :] = jnp.full((KROW - CELLS, QLANE), -BIG, F32)


def collapse_table(total, spread, place, tiles, flat):
    tiles[...] = jnp.zeros(tiles.shape, F32)
    for ck in range(7):
        lhs = jnp.concatenate(
            [total[h, 49 * ck : 49 * ck + 56, :] for h in range(HEADS)], axis=0
        ).astype(BF16)
        for cq in range(7):
            dc = cq - ck + 6
            tiles[336 * dc : 336 * dc + 336, :] += nt(lhs, place[128 * cq : 128 * cq + 128, :])
    cube = jnp.zeros((80, 176), F32)
    for k in range(49):
        cube += nt(
            tiles[pl.ds(k, 80, stride=56), :].astype(BF16), spread[:, 128 * k : 128 * k + 128]
        )
    wide = jnp.concatenate([cube, jnp.zeros((80, 80), F32)], axis=1)
    wide = jnp.concatenate([wide, jnp.zeros((48, 256), F32)], axis=0)
    mixed = wide.T[:176, :]
    mixed = skew(mixed, 78)
    fits = iota((176, 128), 1) >= table_start()
    lane = iota((176, 128), 1)
    length = jnp.bitwise_and(lane - table_start(), 127)
    live = (length < 78) & (iota((176, 128), 0) < 169)
    head = jnp.where(fits & live, mixed, 0.0).astype(BF16)
    rest = jnp.where(jnp.logical_not(fits) & live, mixed, 0.0).astype(BF16)

    def tn(a, b):
        return lax.dot_general(a, b, (((0,), (0,)), ((), ())), preferred_element_type=F32)

    return tn(table_pick(0), head) + tn(table_pick(1), rest)


def tail_vector(tail, start, width):
    o, at = divmod(start, 128)
    lane = iota((1, 128), 1)
    out = roll(tail[o : o + 1, :], -at)
    if at + width > 128:
        out = jnp.where(lane < 128 - at, out, roll(tail[o + 1 : o + 2, :], -at))
    return jnp.where(lane < width, out, 0.0)


def prepare(flat, W, wide, spread, place, tiles):
    rows = flat[ROW_TAIL : ROW_TAIL + 16, :]
    lane = iota((9, 128), 1)
    tail = jnp.where(lane < 2, roll(rows[:9], 2), roll(rows[1:10], 2))
    turned = jnp.concatenate([tail, jnp.zeros((119, 128), F32)], axis=0).T
    for o in range(9):
        W["cols"][128 * o : 128 * o + 128, :] = jnp.broadcast_to(turned[:, o : o + 1], (128, 128))

    def into(j, step, p, value):
        wide[p, pl.ds(j, value.shape[0], stride=step), :] = value

    def finish(p, bias):
        wide[p, 96:97, :] = bias
        wide[p, 97:128, :] = jnp.zeros((31, 128), F32)

    read_matrix(flat, 0, C, 3 * C, into)
    finish(0, tail_vector(tail, V_BQ, C))
    finish(1, jnp.zeros((1, 128), F32))
    finish(2, tail_vector(tail, V_BV, C))
    W["q_n"][...] = wide[0, 0:96, :].astype(BF16)
    for p in range(1, 3):
        W["kv_n"][:, 128 * p - 128 : 128 * p] = wide[p, 0:96, :].astype(BF16)
    for p in range(3):
        W["qkv_t"][96 * p : 96 * p + 96, :] = wide[p, 0:128, :].T[:96].astype(BF16)

    read_matrix(flat, ROW_PROJ, C, C, into)
    finish(0, tail_vector(tail, V_BPROJ, C))
    W["proj_n"][...] = wide[0, 0:96, :].astype(BF16)
    W["proj_t"][...] = wide[0, 0:128, :].T[:96].astype(BF16)

    read_matrix(flat, ROW_ONE, C, HID, into)
    for p in range(3):
        finish(p, tail_vector(tail, V_BHID + 128 * p, 128))
        W["one_n"][:, 128 * p : 128 * p + 128] = wide[p, 0:96, :].astype(BF16)
        W["one_t"][128 * p : 128 * p + 128, :] = wide[p, 0:128, :].T.astype(BF16)

    read_matrix(flat, ROW_TWO, HID, C, into)
    W["two_n"][...] = wide[0].astype(BF16)
    for p in range(3):
        W["two_t"][:, 128 * p : 128 * p + 128] = wide[0, 128 * p : 128 * p + 128, :].T[:96].astype(
            BF16
        )
    build_table(flat, spread, place, tiles, W["table"])


WEIGHT_SHAPES = dict(
    cols=((1152, 128), F32),
    q_n=((96, 128), BF16),
    kv_n=((96, 256), BF16),
    qkv_t=((288, 128), BF16),
    proj_n=((96, 128), BF16),
    proj_t=((96, 128), BF16),
    one_n=((96, 384), BF16),
    one_t=((384, 128), BF16),
    two_n=((384, 128), BF16),
    two_t=((96, 384), BF16),
    table=((HEADS, KROW, QLANE), F32),
)


SAVED_SHAPES = dict(
    normed=((128, QLANE), BF16),
    hat=((96, QLANE), F32),
    scale=((8, QLANE), F32),
    qkv=((288, QLANE), BF16),
    probs=((HEADS, KROW, QLANE), BF16),
    inverse=((8, QLANE), F32),
    attended=((128, QLANE), BF16),
    hat_two=((96, QLANE), F32),
    scale_two=((8, QLANE), F32),
    normed_two=((128, QLANE), BF16),
    slope=((HID, QLANE), BF16),
    active=((HID, QLANE), BF16),
)

GRAD_SHAPES = dict(
    q=((112, 128), F32),
    kv=((2, 112, 128), F32),
    proj=((112, 128), F32),
    one=((112, 384), F32),
    two=((400, 128), F32),
    gain1=((96, 128), F32),
    bias1=((96, 128), F32),
    gain2=((96, 128), F32),
    bias2=((96, 128), F32),
    total=((HEADS, KROW, QLANE), F32),
)


def column(W, start, rows=96):
    part = W["cols"][start : start + rows, :]
    return jnp.concatenate([part, part, part], axis=1)


def extended(rows):
    width = rows.shape[1]
    return jnp.concatenate([rows, jnp.ones((16, width), BF16), jnp.zeros((16, width), BF16)], axis=0)


def standardize(x):
    centered = x - jnp.mean(x, axis=0, keepdims=True)
    variance = jnp.mean(centered * centered, axis=0, keepdims=True)
    scale = lax.rsqrt(variance + EPS_NORM)
    return centered * scale, scale


def at_head(h, rows, tail):
    width = rows.shape[1]
    parts = []
    if h > 0:
        parts.append(jnp.zeros((16 * h, width), BF16))
    parts.append(rows)
    if h < HEADS - 1:
        parts.append(jnp.zeros((16 * (HEADS - 1 - h), width), BF16))
    return jnp.concatenate(parts + [tail], axis=0)


def scaled_queries(qkv):
    return (qkv[0:96].astype(F32) * (HEAD**-0.5 * LOG2E)).astype(BF16)


def window_forward(x, W, S, s, marks, barred):
    hat, scale = standardize(x)
    S["hat"][s] = hat
    S["scale"][s, 0:1] = scale
    normed = extended((hat * column(W, V_GAIN1) + column(W, V_BIAS1)).astype(BF16))
    S["normed"][s] = normed
    qkv = nn(W["qkv_t"][...], normed).astype(BF16)
    S["qkv"][s] = qkv
    queries = scaled_queries(qkv)
    keys = jnp.concatenate([qkv[96:192], marks[0:32, :]], axis=0).T[:KROW]
    ones = jnp.ones((16, KROW), BF16)
    parts = []
    for h in range(HEADS):
        scores = nn(keys, at_head(h, queries[16 * h : 16 * h + 16], barred)) + W["table"][h]
        highest = jnp.max(scores, axis=0, keepdims=True)
        probs = jnp.exp2(scores - highest).astype(BF16)
        S["probs"][s, h] = probs
        values = jnp.concatenate([qkv[192 + 16 * h : 208 + 16 * h, :KROW], ones], axis=0)
        mixed = nn(values, probs)
        inverse = 1.0 / mixed[16:17]
        S["inverse"][s, h : h + 1] = inverse
        parts.append((mixed[:16] * inverse).astype(BF16))
    attended = extended(jnp.concatenate(parts, axis=0))
    S["attended"][s] = attended
    branch = nn(W["proj_t"][...], attended).astype(BF16)
    middle = x + branch.astype(F32)
    hat, scale = standardize(middle)
    S["hat_two"][s] = hat
    S["scale_two"][s, 0:1] = scale
    normed_two = extended((hat * column(W, V_GAIN2) + column(W, V_BIAS2)).astype(BF16))
    S["normed_two"][s] = normed_two
    hidden = nn(W["one_t"][...], normed_two)
    share = 0.5 + 0.5 * lax.erf(hidden * (0.5**0.5))
    active = (hidden * share).astype(BF16)
    S["active"][s] = active
    slope = share + hidden * jnp.exp2(hidden * hidden * (-0.5 * LOG2E)) * 0.3989422804014327
    S["slope"][s] = slope.astype(BF16)
    return middle + nn(W["two_t"][...], active) + column(W, V_BOUT)


def fold(x):
    return x[:, 0:128] + x[:, 128:256] + x[:, 256:384]


def norm_backward(grad, hat, scale, gain):
    scaled = grad * gain
    mean_one = jnp.mean(scaled, axis=0, keepdims=True)
    mean_two = jnp.mean(scaled * hat, axis=0, keepdims=True)
    return scale * (scaled - mean_one - hat * mean_two)


def window_backward(grad, W, S, s, G, marks, barred):
    result = extended(grad.astype(BF16))
    active = S["active"][s]
    G["two"][...] += nt(jnp.concatenate([active, jnp.ones((16, QLANE), BF16)], axis=0), result)
    hidden = (nn(W["two_n"][...], result) * S["slope"][s].astype(F32)).astype(BF16)
    G["one"][...] += nt(S["normed_two"][s, 0:112], hidden)
    d_normed = nn(W["one_n"][...], hidden)
    hat = S["hat_two"][s]
    G["gain2"][...] += fold(d_normed * hat)
    G["bias2"][...] += fold(d_normed)
    d_middle = grad + norm_backward(d_normed, hat, S["scale_two"][s, 0:1], column(W, V_GAIN2))
    d_branch = extended(d_middle.astype(BF16))
    attended = S["attended"][s]
    G["proj"][...] += nt(attended[0:112], d_branch)
    d_attended = nn(W["proj_n"][...], d_branch).astype(BF16).astype(F32)
    product = d_attended * attended[0:96].astype(F32)
    qkv = S["qkv"][s]
    queries = scaled_queries(qkv)
    values = extended(qkv[192:288]).T[:KROW]
    d_keys = jnp.zeros((KROW, 128), F32)
    d_values = jnp.zeros((KROW, 128), F32)
    parts = []
    for h in range(HEADS):
        inverse = S["inverse"][s, h : h + 1]
        inner = jnp.sum(product[16 * h : 16 * h + 16], axis=0, keepdims=True) * inverse
        high = inner.astype(BF16)
        low = (inner - high.astype(F32)).astype(BF16)
        row = iota((32, QLANE), 0)
        less = jnp.where(row == 0, -high.astype(F32), jnp.where(row == 1, -low.astype(F32), 0.0))
        d_out = at_head(
            h, (d_attended[16 * h : 16 * h + 16] * inverse).astype(BF16), less.astype(BF16)
        )
        probs = S["probs"][s, h]
        d_scores = probs * nn(values, d_out).astype(BF16)
        G["total"][h] += d_scores.astype(F32)
        d_values += nt(probs, d_out)
        d_keys += nt(d_scores, at_head(h, queries[16 * h : 16 * h + 16], jnp.zeros_like(barred)))
        parts.append(nn(qkv[96 + 16 * h : 112 + 16 * h, :KROW], d_scores))
    d_queries = (jnp.concatenate(parts, axis=0) * HEAD**-0.5).astype(BF16)
    live = iota((KROW, 128), 1) < 96
    d_pair = jnp.concatenate(
        [jnp.where(live, d_keys * LN2, 0.0), jnp.where(live, d_values, 0.0)], axis=1
    ).astype(BF16)
    normed = S["normed"][s, 0:112]
    G["q"][:, 0:96] += nt(normed, d_queries)
    both = nn(normed[:, :KROW], d_pair)
    for p in range(2):
        G["kv"][p] += both[:, 128 * p : 128 * p + 128]
    d_pair = jnp.concatenate([d_pair, jnp.zeros((QLANE - KROW, 256), BF16)], axis=0)
    d_normed = nn(W["q_n"][:, 0:96], d_queries) + nt(W["kv_n"][...], d_pair)
    hat = S["hat"][s]
    G["gain1"][...] += fold(d_normed * hat)
    G["bias1"][...] += fold(d_normed)
    return d_middle + norm_backward(d_normed, hat, S["scale"][s, 0:1], column(W, V_GAIN1))


def finish_gradients(G, flat, wide, spread, place, tiles):
    def qkv_rows(j, step, p):
        if p == 0:
            return G["q"][pl.ds(j, 24, stride=4), :]
        return G["kv"][p - 1, pl.ds(j, 24, stride=4), :]

    write_matrix(flat, 0, C, 3 * C, qkv_rows)
    write_matrix(flat, ROW_PROJ, C, C, lambda j, step, p: G["proj"][pl.ds(j, 24, stride=4), :])
    write_matrix(
        flat, ROW_ONE, C, HID, lambda j, step, p: G["one"][0:96, 128 * p : 128 * p + 128]
    )
    write_matrix(flat, ROW_TWO, HID, C, lambda j, step, p: G["two"][pl.ds(j, 96, stride=4), :])
    lane = iota((96, 128), 1)
    columns = jnp.zeros((96, 128), F32)
    for at, name in enumerate(["gain1", "bias1", "gain2", "bias2"]):
        columns = jnp.where(lane == at, jnp.sum(G[name][...], axis=1, keepdims=True), columns)
    turned = jnp.concatenate([columns, jnp.zeros((32, 128), F32)], axis=0).T
    sources = [
        (turned[0:1], 3),
        (turned[1:2], 3),
        (G["q"][96:97, :], 3),
        (G["kv"][1, 96:97, :], 3),
        (G["proj"][96:97, :], 3),
        (turned[2:3], 3),
        (turned[3:4], 3),
        (G["one"][96:97, 0:128], 4),
        (G["one"][96:97, 128:256], 4),
        (G["one"][96:97, 256:384], 4),
        (G["two"][384:385, :], 3),
    ]
    pieces = [source for source, _ in sources]
    units = [(i, g) for i, (_, count) in enumerate(sources) for g in range(count)]
    tail = jnp.concatenate(
        [unit_copy(pieces, units[4 * o : 4 * o + 4]) for o in range(9)], axis=0
    )
    table = collapse_table(G["total"], spread, place, tiles, flat)
    flat[ROW_TABLE:ROW_TAIL, :] = table[0:102]
    none = jnp.zeros((1, 128), F32)
    moved = roll(jnp.concatenate([none, tail, none], axis=0), 126)
    lane = iota((10, 128), 1)
    mixed = jnp.where(lane >= 126, moved[1:11], moved[0:10])
    first = jnp.where(iota((1, 128), 1) >= 126, mixed[0:1], table[102:103])
    flat[ROW_TAIL:FLAT, :] = jnp.concatenate([first, mixed[1:10]], axis=0)


def round_up(value, to):
    return -(-value // to) * to


def take_grid(row_of, square, tall, grid, wrapped):
    for x in range(7):
        square[16 * x : 16 * x + 14, 0 : SZ * C] = row_of(x)
    for i in range(11):
        tall[128 * i : 128 * i + 128, :] = square[:, 128 * i : 128 * i + 128].T
    for z in range(SZ + 3 if wrapped else SZ):
        grid[:, 128 * z : 128 * z + 128] = tall[C * (z % SZ) : C * (z % SZ) + C, :].astype(BF16)


def take_window(grid, select, s, wy, wz):
    rows = grid[:, pl.ds(pl.multiple_of(896 * wz + 384 * s, 128), 896)]
    return nn(rows, select[s, :, pl.ds(pl.multiple_of(QLANE * wy, 128), QLANE)])


def give_grid(windows, select, s, put):
    for wz in range(2):
        both = jnp.concatenate([windows[wz], windows[2 + wz]], axis=1).astype(BF16)
        cells = nt(both, select[s])
        for r in range(7):
            put((r + 7 * wz + SHIFT * s) % SZ, cells[:, 128 * r : 128 * r + 128])


def give_rows(tall, square):
    for i in range(11):
        square[:, 128 * i : 128 * i + 128] = tall[128 * i : 128 * i + 128, :].T


def crop_bars(crop, ints, first, total):
    ids = [crop[0, lax.rem(first + a, total)] for a in range(7)]
    at = ints[5:6, :]
    own = jnp.zeros((1, QLANE), jnp.int32)
    for a in range(7):
        own = jnp.where(at == a, ids[a], own)
    row = iota((32, QLANE), 0)
    key = jnp.full((32, QLANE), -1, jnp.int32)
    for a in range(7):
        key = jnp.where(row == a, ids[a], key)
    return jnp.where((row < 7) & (key != own), -BIG, 0.0)


def shift_bars(marks, wy, wz):
    row = iota((32, QLANE), 0)
    factor = jnp.where(row < 14, wy, wz).astype(F32) * -BIG
    return marks[32:64, :].astype(F32) * factor


def step_kernel(n_win, n_fsdp, names, *refs):
    R = dict(zip(names, refs))
    W = {k: R["w_" + k] for k in WEIGHT_SHAPES}
    S = {k: R["s_" + k] for k in SAVED_SHAPES}
    G = {k: R["g_" + k] for k in GRAD_SHAPES}
    tokens, cotangent, crop = R["tokens"], R["cotangent"], R["crop"]
    ints, marks = R["ints"], R["marks"]
    select, place, spread = R["select"], R["place"], R["spread"]
    flat, wide, tiles = R["flat"], R["wide"], R["tiles"]
    square, tall = R["square"], R["tall"]
    send, recv = R["send"], R["recv"]
    shard = FLAT // n_fsdp
    extent = tokens.shape[0]
    total = n_win * extent
    me_win, me_fsdp = lax.axis_index("win"), lax.axis_index("fsdp")
    left, right = lax.rem(me_win + n_win - 1, n_win), lax.rem(me_win + 1, n_win)
    used = [0]

    def remote(src, dst, axis, to):
        slot = used[0]
        used[0] += 1
        copy = pltpu.make_async_remote_copy(
            src_ref=src,
            dst_ref=dst,
            send_sem=send.at[slot],
            recv_sem=recv.at[slot],
            device_id={axis: to},
            device_id_type=pl.DeviceIdType.MESH,
        )
        copy.start()
        return copy

    def to_all(axis, me, count, src_of, dst):
        copies = []
        for k in range(1, count):
            to = lax.rem(me + k, count)
            copies.append(remote(src_of(to), dst, axis, to))
        return copies

    def neighbour(src, dst, to):
        if n_win > 1:
            return [remote(src, dst, "win", to)]
        dst[...] = src[...]
        return []

    def wait(copies):
        for copy in copies:
            copy.wait()

    if n_win * n_fsdp > 1:
        barrier = pltpu.get_barrier_semaphore()
        for axis, me, count in (("fsdp", me_fsdp, n_fsdp), ("win", me_win, n_win)):
            for k in range(1, count):
                pl.semaphore_signal(
                    barrier,
                    inc=1,
                    device_id={axis: lax.rem(me + k, count)},
                    device_id_type=pl.DeviceIdType.MESH,
                )
        pl.semaphore_wait(barrier, n_win + n_fsdp - 2)

    gathered = R["gathered"]
    weights_in = []
    for b in range(2):
        gathered[me_fsdp, b, 0:shard, :] = R["params"][pl.ds(b, shard, stride=2), :].astype(BF16)
        mine = gathered.at[me_fsdp, b]
        weights_in.append(to_all("fsdp", me_fsdp, n_fsdp, lambda to: mine, mine))
    R["edge"][...] = cotangent[0:SHIFT]
    halo_in = neighbour(R["edge"], R["edge_in"], left)

    build_selectors(ints, select, place, spread)
    square[...] = jnp.zeros(square.shape, F32)
    take_grid(lambda x: tokens[x].astype(F32), square, tall, R["grid"], False)

    def spread_weights(b):
        wait(weights_in[b])
        for f in range(n_fsdp):
            flat[shard * f : shard * f + shard, :] = gathered[f, b, 0:shard, :].astype(F32)
        prepare(flat, W, wide, spread, place, tiles)

    spread_weights(0)
    windows, deltas = R["windows"], R["deltas"]
    R["bars"][...] = crop_bars(crop, ints, me_win * extent, total)

    def first_forward(w, carry):
        x = take_window(R["grid"], select, 0, w // 2, lax.rem(w, 2))
        windows[w] = window_forward(x, W, S, w, marks, R["bars"][...].astype(BF16))
        return carry

    lax.fori_loop(0, 4, first_forward, 0)

    halo, halo_back = R["halo"], R["halo_back"]
    kept = R["kept"]
    lane = iota((C, 128), 1)

    def first_slices(z, value):
        kept[z] = value

    give_grid(windows, select, 0, first_slices)
    for i in range(7):
        pair = jnp.where(lane < 64, kept[2 * i], roll(kept[2 * i + 1], 64))
        halo[:, 128 * i : 128 * i + 128] = pair.astype(BF16)
    slab_in = neighbour(halo, R["halo_in"], left)
    first_weights = {}
    for k in ("cols", "q_n", "kv_n", "proj_n", "one_n", "two_n"):
        R["k_" + k][...] = W[k][...]
        first_weights[k] = R["k_" + k]
    spread_weights(1)
    wait(halo_in)

    def shifted_cotangent(x):
        return (cotangent[x + SHIFT] if x < 7 - SHIFT else R["edge_in"][x - 7 + SHIFT]).astype(F32)

    take_grid(shifted_cotangent, square, tall, R["grid_two"], True)
    wait(slab_in)
    for z in range(SZ + 3):
        pair = R["halo_in"][:, 128 * (z % SZ // 2) : 128 * (z % SZ // 2) + 128].astype(F32)
        if z % SZ % 2 == 0:
            pair = roll(pair, 64)
        joined = jnp.where(lane < 64, roll(kept[z % SZ], -48), pair)
        R["grid"][:, 128 * z : 128 * z + 128] = joined.astype(BF16)

    def clear(ref):
        ref[...] = jnp.zeros(ref.shape, ref.dtype)

    for ref in G.values():
        clear(ref)
    R["bars"][...] = crop_bars(crop, ints, me_win * extent + SHIFT, total)

    def second(w, carry):
        wy, wz = w // 2, lax.rem(w, 2)
        bars = (R["bars"][...] + shift_bars(marks, wy, wz)).astype(BF16)
        x = take_window(R["grid"], select, 1, wy, wz)
        windows[w] = window_forward(x, W, S, 4, marks, bars)
        grad = take_window(R["grid_two"], select, 1, wy, wz)
        deltas[w] = window_backward(grad, W, S, 4, G, marks, bars)
        return carry

    lax.fori_loop(0, 4, second, 0)

    def put_kept(z, value):
        kept[z] = value

    give_grid(deltas, select, 1, put_kept)
    for i in range(7):
        pair = jnp.where(lane < 64, roll(kept[2 * i], 64), kept[2 * i + 1])
        halo_back[:, 128 * i : 128 * i + 128] = pair.astype(BF16)
    slab_back = neighbour(halo_back, R["halo_back_in"], right)

    def put_tall(z, value):
        tall[C * z : C * z + C, :] = value

    give_grid(windows, select, 1, put_tall)
    give_rows(tall, square)
    for x in range(7 - SHIFT):
        R["block_out"][x + SHIFT] = square[16 * x : 16 * x + 14, 0 : SZ * C].astype(BF16)
    for x in range(SHIFT):
        at = 16 * (x + 7 - SHIFT)
        R["edge"][x] = square[at : at + 14, 0 : SZ * C].astype(BF16)
    out_back = neighbour(R["edge"], R["edge_back"], right)

    piece = R["sums"].shape[1] // n_win
    padded = R["sums"].shape[1]

    def scatter(b):
        finish_gradients(G, flat, wide, spread, place, tiles)
        for f in range(n_fsdp):
            R["outgoing"][b, f, 0:shard, :] = flat[shard * f : shard * f + shard, :].astype(BF16)
            if padded > shard:
                R["outgoing"][b, f, shard:padded, :] = jnp.zeros((padded - shard, 128), BF16)
        return to_all(
            "fsdp",
            me_fsdp,
            n_fsdp,
            lambda to: R["outgoing"].at[b, to],
            R["incoming"].at[b, me_fsdp],
        )

    def add_fsdp(b, copies):
        wait(copies)
        R["incoming"][b, me_fsdp] = R["outgoing"][b, me_fsdp]
        total_rows = R["incoming"][b, 0].astype(F32)
        for f in range(1, n_fsdp):
            total_rows += R["incoming"][b, f].astype(F32)
        R["sums"][b] = total_rows.astype(BF16)
        return to_all(
            "win",
            me_win,
            n_win,
            lambda to: R["sums"].at[b, pl.ds(pl.multiple_of(piece * to, 16), piece)],
            R["parts"].at[b, me_win],
        )

    def add_win(b, copies):
        wait(copies)
        own = pl.ds(pl.multiple_of(piece * me_win, 16), piece)
        R["parts"][b, me_win] = R["sums"][b, own, :]
        total_rows = R["parts"][b, 0].astype(F32)
        for w in range(1, n_win):
            total_rows += R["parts"][b, w].astype(F32)
        R["whole"][b, own, :] = total_rows.astype(BF16)
        mine = R["whole"].at[b, own]
        return to_all("win", me_win, n_win, lambda to: mine, mine)

    first_scatter = scatter(1)
    wait(slab_back)
    wait(out_back)
    R["block_out"][0:SHIFT] = R["edge_back"][...]
    for z in range(SZ):
        pair = R["halo_back_in"][:, 128 * (z // 2) : 128 * (z // 2) + 128].astype(F32)
        if z % 2 == 1:
            pair = roll(pair, 64)
        joined = jnp.where(lane < 48, pair, roll(kept[z], 48))
        R["grid"][:, 128 * z : 128 * z + 128] = joined.astype(BF16)
    for ref in G.values():
        clear(ref)
    W0 = {**W, **first_weights}

    def first_backward(w, carry):
        grad = take_window(R["grid"], select, 0, w // 2, lax.rem(w, 2))
        deltas[w] = window_backward(grad, W0, S, w, G, marks, R["bars"][...].astype(BF16))
        return carry

    lax.fori_loop(0, 4, first_backward, 0)
    second_scatter = scatter(0)
    give_grid(deltas, select, 0, put_tall)
    give_rows(tall, square)
    for x in range(7):
        R["input_grad"][x] = square[16 * x : 16 * x + 14, 0 : SZ * C].astype(BF16)
    first_sum = add_fsdp(1, first_scatter)
    second_sum = add_fsdp(0, second_scatter)
    first_whole = add_win(1, first_sum)
    second_whole = add_win(0, second_sum)
    wait(first_whole)
    wait(second_whole)

    squares = jnp.zeros((1, 1), F32)
    for b in range(2):
        rows = R["whole"][b, 0:shard, :].astype(F32)
        squares += jnp.sum(jnp.sum(rows * rows, axis=0, keepdims=True), axis=1, keepdims=True)
    R["norms"][me_fsdp] = jnp.broadcast_to(squares, (8, 128))
    mine = R["norms"].at[me_fsdp]
    wait(to_all("fsdp", me_fsdp, n_fsdp, lambda to: mine, mine))
    norm = R["norms"][0]
    for f in range(1, n_fsdp):
        norm += R["norms"][f]
    norm = jnp.sqrt(norm)
    R["grad_norm"][...] = norm
    factor = jnp.minimum(1.0, CLIP_LIMIT / (norm + 1e-06))[0:1]
    for b in range(2):
        at = pl.ds(b, shard, stride=2)
        clipped = R["whole"][b, 0:shard, :].astype(F32) * factor
        new_first = BETA_FIRST * R["first"][at, :] + (1.0 - BETA_FIRST) * clipped
        new_second = BETA_SECOND * R["second"][at, :] + (1.0 - BETA_SECOND) * clipped * clipped
        first_hat = new_first / (1.0 - BETA_FIRST**STEP)
        second_hat = new_second / (1.0 - BETA_SECOND**STEP)
        params = R["params"][at, :]
        R["new_params"][at, :] = params - LEARN_RATE * (
            first_hat / (jnp.sqrt(second_hat) + EPS_ADAM) + WEIGHT_DECAY * params
        )
        R["new_first"][at, :] = new_first
        R["new_second"][at, :] = new_second


def interleave(rows):
    return rows.reshape(2, -1, 128).transpose(1, 0, 2).reshape(-1, 128)


def separate(rows):
    return rows.reshape(-1, 2, 128).transpose(1, 0, 2).reshape(2, -1)


def per_device(n_win, n_fsdp, tokens, cotangent, crop_ids, params, first_moment, second_moment):
    ints, marks = constant_tables()
    extent = tokens.shape[1]
    shard = FLAT // n_fsdp
    held = round_up(shard, 16)
    padded = round_up(-(-shard // n_win), 16) * n_win
    rows = jax.ShapeDtypeStruct((2 * shard, 128), F32)
    cells = jax.ShapeDtypeStruct((extent, SY, SZ * C), BF16)
    inputs = dict(
        tokens=tokens[0],
        cotangent=cotangent[0],
        crop=crop_ids,
        ints=ints,
        marks=marks,
        params=interleave(params),
        first=interleave(first_moment),
        second=interleave(second_moment),
    )
    outputs = dict(
        block_out=cells,
        input_grad=cells,
        grad_norm=jax.ShapeDtypeStruct((8, 128), F32),
        new_params=rows,
        new_first=rows,
        new_second=rows,
    )
    V = pltpu.VMEM
    edge = V((SHIFT, SY, SZ * C), BF16)
    scratch = dict(
        gathered=V((n_fsdp, 2, held, 128), BF16),
        edge=edge,
        edge_in=edge,
        edge_back=edge,
        halo=V((C, 896), BF16),
        halo_in=V((C, 896), BF16),
        halo_back=V((C, 896), BF16),
        halo_back_in=V((C, 896), BF16),
        outgoing=V((2, n_fsdp, padded, 128), BF16),
        incoming=V((2, n_fsdp, padded, 128), BF16),
        sums=V((2, padded, 128), BF16),
        parts=V((2, n_win, padded // n_win, 128), BF16),
        whole=V((2, padded, 128), BF16),
        norms=V((n_fsdp, 8, 128), F32),
        select=V((2, 896, 2 * QLANE), BF16),
        place=V((896, QLANE), BF16),
        spread=V((176, 49 * 128), BF16),
        flat=V((FLAT + 8, 128), F32),
        wide=V((3, 384, 128), F32),
        tiles=V((80 * 56, 128), F32),
        square=V((128, 1408), F32),
        tall=V((1408, 128), F32),
        grid=V((C, 17 * 128), BF16),
        grid_two=V((C, 17 * 128), BF16),
        kept=V((SZ, C, 128), F32),
        windows=V((4, C, QLANE), F32),
        deltas=V((4, C, QLANE), F32),
        bars=V((32, QLANE), F32),
    )
    for k, (shape, kind) in WEIGHT_SHAPES.items():
        scratch["w_" + k] = V(shape, kind)
    for k in ("cols", "q_n", "kv_n", "proj_n", "one_n", "two_n"):
        scratch["k_" + k] = V(*WEIGHT_SHAPES[k])
    for k, (shape, kind) in SAVED_SHAPES.items():
        scratch["s_" + k] = V((5, *shape), kind)
    for k, (shape, kind) in GRAD_SHAPES.items():
        scratch["g_" + k] = V(shape, kind)
    copies = 5 * (n_fsdp - 1) + 4 * (n_win - 1) + 4
    scratch["send"] = pltpu.SemaphoreType.DMA((copies,))
    scratch["recv"] = pltpu.SemaphoreType.DMA((copies,))
    names = [*inputs, *outputs, *scratch]
    vmem = pl.BlockSpec(memory_space=pltpu.VMEM)
    results = pl.pallas_call(
        functools.partial(step_kernel, n_win, n_fsdp, names),
        out_shape=tuple(outputs.values()),
        in_specs=[
            pl.BlockSpec(memory_space=pltpu.SMEM) if k == "crop" else vmem for k in inputs
        ],
        out_specs=tuple(vmem for _ in outputs),
        scratch_shapes=list(scratch.values()),
        compiler_params=pltpu.CompilerParams(
            collective_id=0 if n_win * n_fsdp > 1 else None,
            has_side_effects=True,
            vmem_limit_bytes=66 * 1024 * 1024 - 2 * 1024 * 1024,
        ),
        name="layer_step",
    )(*inputs.values())
    block_out, input_grad, grad_norm, new_params, new_first, new_second = results
    new_params = separate(new_params)
    return (
        block_out[None],
        input_grad[None],
        grad_norm[0, 0],
        new_params,
        separate(new_first),
        separate(new_second),
        new_params.astype(BF16),
    )


def solution(mesh):
    data = P("fsdp", "win", None, None)
    state = P(None, "fsdp")
    return jax.shard_map(
        functools.partial(per_device, mesh.shape["win"], mesh.shape["fsdp"]),
        mesh=mesh,
        in_specs=(data, data, P("fsdp", None), state, state, state),
        out_specs=(data, data, P(), state, state, state, state),
        check_vma=False,
    )
```

```python
import functools
from types import SimpleNamespace as Names

import jax
import jax.numpy as jnp
import numpy as np
from jax import lax
from jax.experimental import pallas as pl
from jax.experimental.pallas import tpu as pltpu
from jax.sharding import PartitionSpec as P

C = 96
HEADS = 6
HEAD = 16
HID = 384
WS = 7
SHIFT = 3
SY = 14
SZ = 14
BPAD = 124928
STEP = 5
EPS_NORM = 1e-05
CLIP_LIMIT = 1.0
LEARN_RATE = 0.4
BETA_FIRST = 0.9
BETA_SECOND = 0.999
WEIGHT_DECAY = 0.05
EPS_ADAM = 1e-08
BIG = 1e30
LOG2E = 1.4426950408889634
LN2 = 0.6931471805599453

CELLS = WS**3
KROW = 352
QLANE = 384
FLAT = BPAD // 128
ROW_PROJ = 216
ROW_ONE = 288
ROW_TWO = 576
ROW_TABLE = 864
ROW_TAIL = 966
V_GAIN1, V_BIAS1, V_BQ, V_BV, V_BPROJ, V_GAIN2, V_BIAS2, V_BHID, V_BOUT = (
    0, 96, 192, 288, 384, 480, 576, 672, 1056,
)

F32 = jnp.float32
BF16 = jnp.bfloat16


def nn(a, b):
    return lax.dot_general(a, b, (((1,), (0,)), ((), ())), preferred_element_type=F32)


def nt(a, b):
    return lax.dot_general(a, b, (((1,), (1,)), ((), ())), preferred_element_type=F32)


def iota(shape, dim):
    return lax.broadcasted_iota(jnp.int32, shape, dim)


def roll(x, by):
    by = by % 128
    return x if by == 0 else pltpu.roll(x, by, 1)


def skew(x, by):
    while by > 0:
        some = min(1 << (by.bit_length() - 1), 16)
        x = pltpu.roll(x, 0, 1, stride=some, stride_axis=0)
        by -= some
    return x


def constant_tables():
    t = np.arange(QLANE)
    live = t < CELLS
    z, x, y = t // 49, t % 49 // 7, t % 7
    ints = np.full((8, QLANE), -1, np.int32)
    for s in range(2):
        for wy in range(2):
            cell_y = (y + 7 * wy + SHIFT * s) % SY
            ints[2 * s + wy] = np.where(live, z * 128 + x * 16 + cell_y, -1)
    ints[4] = np.where(live, z * 128 + t % 49, -1)
    ints[5] = np.where(live, x, -1)
    lane = np.arange(128)
    ints[6, :128] = np.where(lane < 49, 13 * (lane // 7) + lane % 7, -1000)
    marks = np.zeros((64, QLANE), np.float32)
    for i in range(7):
        marks[i] = live & (x == i)
        marks[7 + i] = live & (y == i)
        marks[14 + i] = live & (z == i)
        marks[32 + 7 + i] = live & ((i >= 4) != (y >= 4))
        marks[32 + 14 + i] = live & ((i >= 4) != (z >= 4))
    return jnp.asarray(ints), jnp.asarray(marks, BF16)


def unit_copy(pieces, units):
    out = None
    for at, unit in enumerate(units):
        if unit is None:
            continue
        i, g = unit
        moved = roll(pieces[i], 32 * (at - g))
        group = iota(moved.shape, 1) // 32
        base = jnp.zeros_like(moved) if out is None else out
        out = jnp.where(group == at, moved, base)
    return out


def read_matrix(flat, base, rows, width, store):
    units = width // 32
    if units % 4 == 0:
        step = units // 4
        for o in range(step):
            store(0, 1, o, flat[pl.ds(base + o, rows, stride=step), :])
        return
    groups = rows // 4
    loaded = [flat[pl.ds(base + o, groups, stride=units), :] for o in range(units)]
    for j in range(4):
        for p in range(units // 3):
            first = units * j + 3 * p
            store(j, 4, p, unit_copy(loaded, [divmod(first + s, 4) for s in range(3)] + [None]))


def write_matrix(flat, base, rows, width, load):
    units = width // 32
    if units % 4 == 0:
        step = units // 4
        for o in range(step):
            flat[pl.ds(base + o, rows, stride=step), :] = load(0, 1, o)
        return
    groups = rows // 4
    parts = units // 3
    loaded = [load(j, 4, p) for j in range(4) for p in range(parts)]
    for o in range(units):
        flat[pl.ds(base + o, groups, stride=units), :] = unit_copy(
            loaded, [divmod(4 * o + g, 3) for g in range(4)]
        )


def build_selectors(ints, select, place, spread):
    for s in range(2):
        for wy in range(2):
            need = ints[2 * s + wy : 2 * s + wy + 1, :]
            for r in range(7):
                row = iota((128, QLANE), 0) + 128 * r
                select[s, 128 * r : 128 * r + 128, QLANE * wy : QLANE * wy + QLANE] = jnp.where(
                    row == need, 1.0, 0.0
                ).astype(BF16)
    need = ints[4:5, :]
    for r in range(7):
        row = iota((128, QLANE), 0) + 128 * r
        place[128 * r : 128 * r + 128, :] = jnp.where(row == need, 1.0, 0.0).astype(BF16)
    gap = iota((176, 128), 0) - ints[6:7, :128]
    for k in range(49):
        hit = gap == 84 - 13 * (k // 7) - k % 7
        spread[:, 128 * k : 128 * k + 128] = jnp.where(hit, 1.0, 0.0).astype(BF16)


def table_pick(second):
    row = iota((176, 104), 0)
    col = iota((176, 104), 1) - second
    at = 128 * col
    start = 78 * row
    hit = (start >= at) & (start < at + 128) & (row < 169)
    return jnp.where(hit, 1.0, 0.0).astype(BF16)


def table_start():
    row = iota((176, 128), 0)
    return jnp.bitwise_and(78 * row, 127)


def build_table(flat, spread, place, tiles, table):
    rows = flat[ROW_TABLE : ROW_TABLE + 104, :].astype(BF16)
    first = skew(nn(table_pick(0), rows), 50)
    second = skew(nn(table_pick(1), rows), 50)
    lane = iota((176, 128), 1)
    mixed = jnp.where(lane + table_start() < 128, first, second)
    mixed = jnp.where((lane < 78) & (iota((176, 128), 0) < 169), mixed, 0.0)
    turned = jnp.concatenate([mixed, jnp.zeros((80, 128), F32)], axis=0).T
    cube = turned[:80, :176].astype(BF16)
    for k in range(0, 49, 2):
        some = min(2, 49 - k)
        block = nn(cube, spread[:, 128 * k : 128 * k + 128 * some])
        for i in range(some):
            tiles[pl.ds(k + i, 80, stride=56), :] = block[:, 128 * i : 128 * i + 128]

    def gathered(ck, first, last):
        return jnp.concatenate(
            [
                tiles[336 * (cq - ck + 6) : 336 * (cq - ck + 7), :].astype(BF16)
                for cq in range(first, last)
            ],
            axis=1,
        )

    for ck in range(7):
        block = jnp.concatenate(
            [
                nn(gathered(ck, 0, 6), place[0:768, 0:256]),
                nn(gathered(ck, 5, 7), place[640:896, 256:QLANE]),
            ],
            axis=1,
        )
        block = block * LOG2E
        for h in range(HEADS):
            table[h, 49 * ck : 49 * ck + 49, :] = block[56 * h : 56 * h + 49, :]
    for h in range(HEADS):
        table[h, CELLS:KROW, :] = jnp.full((KROW - CELLS, QLANE), -BIG, F32)


def collapse_table(total, spread, place, tiles, flat):
    tiles[...] = jnp.zeros(tiles.shape, F32)
    for ck in range(7):
        lhs = jnp.concatenate(
            [total[h, 49 * ck : 49 * ck + 56, :] for h in range(HEADS)], axis=0
        ).astype(BF16)
        for cq, start, end in ((0, 0, 128), (2, 0, 256), (4, 128, 384), (6, 256, 384)):
            some = min(2, 7 - cq)
            block = nt(lhs[:, start:end], place[128 * cq : 128 * cq + 128 * some, start:end])
            for i in range(some):
                dc = cq + i - ck + 6
                tiles[336 * dc : 336 * dc + 336, :] += block[:, 128 * i : 128 * i + 128]
    lhs = jnp.concatenate(
        [tiles[pl.ds(k, 80, stride=56), :].astype(BF16) for k in range(49)], axis=1
    )
    cube = nt(lhs, spread[...])
    wide = jnp.concatenate([cube, jnp.zeros((80, 80), F32)], axis=1)
    wide = jnp.concatenate([wide, jnp.zeros((48, 256), F32)], axis=0)
    mixed = wide.T[:176, :]
    mixed = skew(mixed, 78)
    fits = iota((176, 128), 1) >= table_start()
    lane = iota((176, 128), 1)
    length = jnp.bitwise_and(lane - table_start(), 127)
    live = (length < 78) & (iota((176, 128), 0) < 169)
    head = jnp.where(fits & live, mixed, 0.0).astype(BF16)
    rest = jnp.where(jnp.logical_not(fits) & live, mixed, 0.0).astype(BF16)

    def tn(a, b):
        return lax.dot_general(a, b, (((0,), (0,)), ((), ())), preferred_element_type=F32)

    return tn(table_pick(0), head) + tn(table_pick(1), rest)


def tail_vector(tail, start, width):
    o, at = divmod(start, 128)
    lane = iota((1, 128), 1)
    out = roll(tail[o : o + 1, :], -at)
    if at + width > 128:
        out = jnp.where(lane < 128 - at, out, roll(tail[o + 1 : o + 2, :], -at))
    return jnp.where(lane < width, out, 0.0)


def prepare(flat, W, wide, spread, place, tiles):
    rows = flat[ROW_TAIL : ROW_TAIL + 16, :]
    lane = iota((9, 128), 1)
    tail = jnp.where(lane < 2, roll(rows[:9], 2), roll(rows[1:10], 2))
    turned = jnp.concatenate([tail, jnp.zeros((119, 128), F32)], axis=0).T
    for o in range(9):
        W.cols[128 * o : 128 * o + 128, :] = jnp.broadcast_to(turned[:, o : o + 1], (128, 128))

    def into(j, step, p, value):
        wide[p, pl.ds(j, value.shape[0], stride=step), :] = value

    def finish(p, bias):
        wide[p, 96:97, :] = bias
        wide[p, 97:128, :] = jnp.zeros((31, 128), F32)

    read_matrix(flat, 0, C, 3 * C, into)
    finish(0, tail_vector(tail, V_BQ, C))
    finish(1, jnp.zeros((1, 128), F32))
    finish(2, tail_vector(tail, V_BV, C))
    W.q_n[...] = wide[0, 0:96, :].astype(BF16)
    for p in range(1, 3):
        W.kv_n[:, 128 * p - 128 : 128 * p] = wide[p, 0:96, :].astype(BF16)
    for p in range(3):
        W.qkv_t[96 * p : 96 * p + 96, :] = wide[p, 0:128, :].T[:96].astype(BF16)

    read_matrix(flat, ROW_PROJ, C, C, into)
    finish(0, tail_vector(tail, V_BPROJ, C))
    W.proj_n[...] = wide[0, 0:96, :].astype(BF16)
    W.proj_t[...] = wide[0, 0:128, :].T[:96].astype(BF16)

    read_matrix(flat, ROW_ONE, C, HID, into)
    for p in range(3):
        finish(p, tail_vector(tail, V_BHID + 128 * p, 128))
        W.one_n[:, 128 * p : 128 * p + 128] = wide[p, 0:96, :].astype(BF16)
        W.one_t[128 * p : 128 * p + 128, :] = wide[p, 0:128, :].T.astype(BF16)

    read_matrix(flat, ROW_TWO, HID, C, into)
    W.two_n[...] = wide[0].astype(BF16)
    for p in range(3):
        W.two_t[:, 128 * p : 128 * p + 128] = wide[0, 128 * p : 128 * p + 128, :].T[:96].astype(
            BF16
        )
    build_table(flat, spread, place, tiles, W.table)


WEIGHT_SHAPES = dict(
    cols=((1152, 128), F32),
    q_n=((96, 128), BF16),
    kv_n=((96, 256), BF16),
    qkv_t=((288, 128), BF16),
    proj_n=((96, 128), BF16),
    proj_t=((96, 128), BF16),
    one_n=((96, 384), BF16),
    one_t=((384, 128), BF16),
    two_n=((384, 128), BF16),
    two_t=((96, 384), BF16),
    table=((HEADS, KROW, QLANE), F32),
)


SAVED_SHAPES = dict(
    normed=((128, QLANE), BF16),
    hat=((96, QLANE), F32),
    scale=((8, QLANE), F32),
    qkv=((288, QLANE), BF16),
    probs=((HEADS, KROW, QLANE), BF16),
    inverse=((8, QLANE), F32),
    attended=((128, QLANE), BF16),
    hat_two=((96, QLANE), F32),
    scale_two=((8, QLANE), F32),
    normed_two=((128, QLANE), BF16),
    slope=((HID, QLANE), BF16),
    active=((HID, QLANE), BF16),
)

GRAD_SHAPES = dict(
    q=((112, 128), F32),
    kv=((2, 112, 128), F32),
    proj=((112, 128), F32),
    one=((112, 384), F32),
    two=((400, 128), F32),
    gain1=((96, 128), F32),
    bias1=((96, 128), F32),
    gain2=((96, 128), F32),
    bias2=((96, 128), F32),
    total=((HEADS, KROW, QLANE), F32),
)


def column(W, start, rows=96):
    part = W.cols[start : start + rows, :]
    return jnp.concatenate([part, part, part], axis=1)


def extended(rows):
    width = rows.shape[1]
    return jnp.concatenate([rows, jnp.ones((16, width), BF16), jnp.zeros((16, width), BF16)], axis=0)


def standardize(x):
    centered = x - jnp.mean(x, axis=0, keepdims=True)
    variance = jnp.mean(centered * centered, axis=0, keepdims=True)
    scale = lax.rsqrt(variance + EPS_NORM)
    return centered * scale, scale


def at_head(h, rows, tail):
    width = rows.shape[1]
    parts = []
    if h > 0:
        parts.append(jnp.zeros((16 * h, width), BF16))
    parts.append(rows)
    if h < HEADS - 1:
        parts.append(jnp.zeros((16 * (HEADS - 1 - h), width), BF16))
    return jnp.concatenate(parts + [tail], axis=0)


def scaled_queries(qkv):
    return (qkv[0:96].astype(F32) * (HEAD**-0.5 * LOG2E)).astype(BF16)


def window_forward(x, W, S, s, marks, barred):
    hat, scale = standardize(x)
    S.hat[s] = hat
    S.scale[s, 0:1] = scale
    normed = extended((hat * column(W, V_GAIN1) + column(W, V_BIAS1)).astype(BF16))
    S.normed[s] = normed
    qkv = nn(W.qkv_t[...], normed).astype(BF16)
    S.qkv[s] = qkv
    queries = scaled_queries(qkv)
    keys = jnp.concatenate([qkv[96:192], marks[0:32, :]], axis=0).T[:KROW]
    ones = jnp.ones((16, KROW), BF16)

    def pair_scores(p):
        sides = [at_head(h, queries[16 * h : 16 * h + 16], barred) for h in (2 * p, 2 * p + 1)]
        return nn(keys, jnp.concatenate(sides, axis=1))

    parts = []
    coming = pair_scores(0)
    for h in range(HEADS):
        if h % 2 == 0:
            pair = coming
            if h + 2 < HEADS:
                coming = pair_scores(h // 2 + 1)
        scores = pair[:, QLANE * (h % 2) : QLANE * (h % 2) + QLANE] + W.table[h]
        highest = jnp.max(scores, axis=0, keepdims=True)
        probs = jnp.exp2(scores - highest).astype(BF16)
        S.probs[s, h] = probs
        values = jnp.concatenate([qkv[192 + 16 * h : 208 + 16 * h, :KROW], ones], axis=0)
        mixed = nn(values, probs)
        inverse = 1.0 / mixed[16:17]
        S.inverse[s, h : h + 1] = inverse
        parts.append((mixed[:16] * inverse).astype(BF16))
    attended = extended(jnp.concatenate(parts, axis=0))
    S.attended[s] = attended
    branch = nn(W.proj_t[...], attended).astype(BF16)
    middle = x + branch.astype(F32)
    hat, scale = standardize(middle)
    S.hat_two[s] = hat
    S.scale_two[s, 0:1] = scale
    normed_two = extended((hat * column(W, V_GAIN2) + column(W, V_BIAS2)).astype(BF16))
    S.normed_two[s] = normed_two
    hidden = nn(W.one_t[...], normed_two)
    share = 0.5 + 0.5 * lax.erf(hidden * (0.5**0.5))
    active = (hidden * share).astype(BF16)
    S.active[s] = active
    slope = share + hidden * jnp.exp2(hidden * hidden * (-0.5 * LOG2E)) * 0.3989422804014327
    S.slope[s] = slope.astype(BF16)
    return middle + nn(W.two_t[...], active) + column(W, V_BOUT)


def fold(x):
    return x[:, 0:128] + x[:, 128:256] + x[:, 256:384]


def norm_backward(grad, hat, scale, gain):
    scaled = grad * gain
    mean_one = jnp.mean(scaled, axis=0, keepdims=True)
    mean_two = jnp.mean(scaled * hat, axis=0, keepdims=True)
    return scale * (scaled - mean_one - hat * mean_two)


def window_backward(grad, W, S, s, G, marks, barred):
    result = extended(grad.astype(BF16))
    active = S.active[s]
    G.two[...] += nt(jnp.concatenate([active, jnp.ones((16, QLANE), BF16)], axis=0), result)
    hidden = (nn(W.two_n[...], result) * S.slope[s].astype(F32)).astype(BF16)
    G.one[...] += nt(S.normed_two[s, 0:112], hidden)
    d_normed = nn(W.one_n[...], hidden)
    hat = S.hat_two[s]
    G.gain2[...] += fold(d_normed * hat)
    G.bias2[...] += fold(d_normed)
    d_middle = grad + norm_backward(d_normed, hat, S.scale_two[s, 0:1], column(W, V_GAIN2))
    d_branch = extended(d_middle.astype(BF16))
    attended = S.attended[s]
    G.proj[...] += nt(attended[0:112], d_branch)
    d_attended = nn(W.proj_n[...], d_branch).astype(BF16).astype(F32)
    product = d_attended * attended[0:96].astype(F32)
    qkv = S.qkv[s]
    queries = scaled_queries(qkv)
    values = extended(qkv[192:288]).T[:KROW]
    d_both = jnp.zeros((KROW, 256), F32)
    none = jnp.zeros((32, QLANE), BF16)
    blank = jnp.zeros((128, QLANE), BF16)
    row = iota((32, QLANE), 0)
    parts = []

    def head_gradient(h):
        inverse = S.inverse[s, h : h + 1]
        inner = jnp.sum(product[16 * h : 16 * h + 16], axis=0, keepdims=True) * inverse
        high = inner.astype(BF16)
        low = (inner - high.astype(F32)).astype(BF16)
        less = jnp.where(row == 0, -high.astype(F32), jnp.where(row == 1, -low.astype(F32), 0.0))
        rows = (d_attended[16 * h : 16 * h + 16] * inverse).astype(BF16)
        return at_head(h, rows, less.astype(BF16))

    for p in range(HEADS // 2):
        d_outs = [head_gradient(h) for h in (2 * p, 2 * p + 1)]
        d_pair = nn(values, jnp.concatenate(d_outs, axis=1)).astype(BF16)
        for h in (2 * p, 2 * p + 1):
            probs = S.probs[s, h]
            d_scores = probs * d_pair[:, QLANE * (h % 2) : QLANE * (h % 2) + QLANE]
            G.total[h] += d_scores.astype(F32)
            sides = jnp.concatenate(
                [
                    jnp.concatenate(
                        [at_head(h, queries[16 * h : 16 * h + 16], none), blank], axis=0
                    ),
                    jnp.concatenate([blank, d_outs[h % 2]], axis=0),
                ],
                axis=1,
            )
            d_both += nt(jnp.concatenate([d_scores, probs], axis=1), sides)
            parts.append(nn(qkv[96 + 16 * h : 112 + 16 * h, :KROW], d_scores))
    d_queries = (jnp.concatenate(parts, axis=0) * HEAD**-0.5).astype(BF16)
    lane = iota((KROW, 256), 1)
    factor = jnp.where(lane < 96, LN2, jnp.where((lane >= 128) & (lane < 224), 1.0, 0.0))
    d_pair = jnp.where(factor > 0, d_both * factor, 0.0).astype(BF16)
    normed = S.normed[s, 0:112]
    G.q[:, 0:96] += nt(normed, d_queries)
    both = nn(normed[:, :KROW], d_pair)
    for p in range(2):
        G.kv[p] += both[:, 128 * p : 128 * p + 128]
    d_pair = jnp.concatenate([d_pair, jnp.zeros((QLANE - KROW, 256), BF16)], axis=0)
    d_normed = nn(W.q_n[:, 0:96], d_queries) + nt(W.kv_n[...], d_pair)
    hat = S.hat[s]
    G.gain1[...] += fold(d_normed * hat)
    G.bias1[...] += fold(d_normed)
    return d_middle + norm_backward(d_normed, hat, S.scale[s, 0:1], column(W, V_GAIN1))


def finish_gradients(G, flat, wide, spread, place, tiles):
    def qkv_rows(j, step, p):
        if p == 0:
            return G.q[pl.ds(j, 24, stride=4), :]
        return G.kv[p - 1, pl.ds(j, 24, stride=4), :]

    write_matrix(flat, 0, C, 3 * C, qkv_rows)
    write_matrix(flat, ROW_PROJ, C, C, lambda j, step, p: G.proj[pl.ds(j, 24, stride=4), :])
    write_matrix(
        flat, ROW_ONE, C, HID, lambda j, step, p: G.one[0:96, 128 * p : 128 * p + 128]
    )
    write_matrix(flat, ROW_TWO, HID, C, lambda j, step, p: G.two[pl.ds(j, 96, stride=4), :])
    lane = iota((96, 128), 1)
    columns = jnp.zeros((96, 128), F32)
    for at, ref in enumerate([G.gain1, G.bias1, G.gain2, G.bias2]):
        columns = jnp.where(lane == at, jnp.sum(ref[...], axis=1, keepdims=True), columns)
    turned = jnp.concatenate([columns, jnp.zeros((32, 128), F32)], axis=0).T
    sources = [
        (turned[0:1], 3),
        (turned[1:2], 3),
        (G.q[96:97, :], 3),
        (G.kv[1, 96:97, :], 3),
        (G.proj[96:97, :], 3),
        (turned[2:3], 3),
        (turned[3:4], 3),
        (G.one[96:97, 0:128], 4),
        (G.one[96:97, 128:256], 4),
        (G.one[96:97, 256:384], 4),
        (G.two[384:385, :], 3),
    ]
    pieces = [source for source, _ in sources]
    units = [(i, g) for i, (_, count) in enumerate(sources) for g in range(count)]
    tail = jnp.concatenate(
        [unit_copy(pieces, units[4 * o : 4 * o + 4]) for o in range(9)], axis=0
    )
    table = collapse_table(G.total, spread, place, tiles, flat)
    flat[ROW_TABLE:ROW_TAIL, :] = table[0:102]
    none = jnp.zeros((1, 128), F32)
    moved = roll(jnp.concatenate([none, tail, none], axis=0), 126)
    lane = iota((10, 128), 1)
    mixed = jnp.where(lane >= 126, moved[1:11], moved[0:10])
    first = jnp.where(iota((1, 128), 1) >= 126, mixed[0:1], table[102:103])
    flat[ROW_TAIL:FLAT, :] = jnp.concatenate([first, mixed[1:10]], axis=0)


def round_up(value, to):
    return -(-value // to) * to


def take_grid(row_of, square, tall, grid, wrapped):
    for x in range(7):
        square[16 * x : 16 * x + 14, 0 : SZ * C] = row_of(x)
    for i in range(11):
        tall[128 * i : 128 * i + 128, :] = square[:, 128 * i : 128 * i + 128].T
    for z in range(SZ + 3 if wrapped else SZ):
        grid[:, 128 * z : 128 * z + 128] = tall[C * (z % SZ) : C * (z % SZ) + C, :].astype(BF16)


def take_window(grid, select, s, wy, wz):
    rows = grid[:, pl.ds(pl.multiple_of(896 * wz + 384 * s, 128), 896)]
    return nn(rows, select[s, :, pl.ds(pl.multiple_of(QLANE * wy, 128), QLANE)])


def give_grid(windows, select, s, put):
    for wz in range(2):
        both = jnp.concatenate([windows[wz], windows[2 + wz]], axis=1).astype(BF16)
        cells = nt(both, select[s])
        for r in range(7):
            put((r + 7 * wz + SHIFT * s) % SZ, cells[:, 128 * r : 128 * r + 128])


def give_rows(tall, square):
    for i in range(11):
        square[:, 128 * i : 128 * i + 128] = tall[128 * i : 128 * i + 128, :].T


def crop_bars(crop, ints, first, total):
    ids = [crop[0, lax.rem(first + a, total)] for a in range(7)]
    at = ints[5:6, :]
    own = jnp.zeros((1, QLANE), jnp.int32)
    for a in range(7):
        own = jnp.where(at == a, ids[a], own)
    row = iota((32, QLANE), 0)
    key = jnp.full((32, QLANE), -1, jnp.int32)
    for a in range(7):
        key = jnp.where(row == a, ids[a], key)
    return jnp.where((row < 7) & (key != own), -BIG, 0.0)


def shift_bars(marks, wy, wz):
    row = iota((32, QLANE), 0)
    factor = jnp.where(row < 14, wy, wz).astype(F32) * -BIG
    return marks[32:64, :].astype(F32) * factor


def step_kernel(n_win, n_fsdp, names, *refs):
    held = dict(zip(names, refs))
    R = Names(**held)
    W = Names(**{k: held["w_" + k] for k in WEIGHT_SHAPES})
    S = Names(**{k: held["s_" + k] for k in SAVED_SHAPES})
    G = Names(**{k: held["g_" + k] for k in GRAD_SHAPES})
    tokens, cotangent, crop = R.tokens, R.cotangent, R.crop
    ints, marks = R.ints, R.marks
    select, place, spread = R.select, R.place, R.spread
    flat, wide, tiles = R.flat, R.wide, R.tiles
    square, tall = R.square, R.tall
    send, recv = R.send, R.recv
    shard = FLAT // n_fsdp
    extent = tokens.shape[0]
    total = n_win * extent
    me_win, me_fsdp = lax.axis_index("win"), lax.axis_index("fsdp")
    left, right = lax.rem(me_win + n_win - 1, n_win), lax.rem(me_win + 1, n_win)
    slots = {}

    def remote(name, src, dst, axis, to):
        slot = slots.setdefault(name, len(slots))
        return pltpu.make_async_remote_copy(
            src_ref=src,
            dst_ref=dst,
            send_sem=send.at[slot],
            recv_sem=recv.at[slot],
            device_id={axis: to},
            device_id_type=pl.DeviceIdType.MESH,
        )

    def to_all(name, axis, me, count, src_of, dst):
        copies = []
        for k in range(1, count):
            to = lax.rem(me + k, count)
            copies.append(remote((name, k), src_of(to), dst, axis, to))
        return copies

    def start(copies):
        for copy in copies:
            copy.start()
        return copies

    def neighbour(name, src, dst, to):
        if n_win > 1:
            return start([remote(name, src, dst, "win", to)])
        dst[...] = src[...]
        return []

    def wait(copies):
        for copy in copies:
            copy.wait()

    if n_win * n_fsdp > 1:
        barrier = pltpu.get_barrier_semaphore()
        for axis, me, count in (("fsdp", me_fsdp, n_fsdp), ("win", me_win, n_win)):
            for k in range(1, count):
                pl.semaphore_signal(
                    barrier,
                    inc=1,
                    device_id={axis: lax.rem(me + k, count)},
                    device_id_type=pl.DeviceIdType.MESH,
                )
    gathered = R.gathered
    for b in range(2):
        R.own[b] = R.params[b : b + 1, :].reshape(shard, 128)
        gathered[me_fsdp, b, 0:shard, :] = R.own[b].astype(BF16)
    R.edge[...] = cotangent[0:SHIFT]
    build_selectors(ints, select, place, spread)
    square[...] = jnp.zeros(square.shape, F32)
    take_grid(lambda x: tokens[x].astype(F32), square, tall, R.grid, False)
    if n_win * n_fsdp > 1:
        pl.semaphore_wait(barrier, n_win + n_fsdp - 2)

    weights_in = []
    for b in range(2):
        mine = gathered.at[me_fsdp, b]
        weights_in.append(
            start(to_all(("weights", b), "fsdp", me_fsdp, n_fsdp, lambda to: mine, mine))
        )
    halo_in = neighbour("halo", R.edge, R.edge_in, left)

    def spread_weights(b):
        wait(weights_in[b])
        for f in range(n_fsdp):
            flat[shard * f : shard * f + shard, :] = gathered[f, b, 0:shard, :].astype(F32)
        prepare(flat, W, wide, spread, place, tiles)

    spread_weights(0)
    windows, deltas = R.windows, R.deltas
    R.bars[...] = crop_bars(crop, ints, me_win * extent, total)

    def first_forward(w, carry):
        x = take_window(R.grid, select, 0, w // 2, lax.rem(w, 2))
        windows[w] = window_forward(x, W, S, w, marks, R.bars[...].astype(BF16))
        return carry

    lax.fori_loop(0, 4, first_forward, 0)

    halo, halo_back = R.halo, R.halo_back
    kept = R.kept
    lane = iota((C, 128), 1)

    def first_slices(z, value):
        kept[z] = value

    give_grid(windows, select, 0, first_slices)
    for i in range(7):
        pair = jnp.where(lane < 64, kept[2 * i], roll(kept[2 * i + 1], 64))
        halo[:, 128 * i : 128 * i + 128] = pair.astype(BF16)
    slab_in = neighbour("slab", halo, R.halo_in, left)
    first_weights = {}
    for k in ("cols", "q_n", "kv_n", "proj_n", "one_n", "two_n"):
        held["k_" + k][...] = held["w_" + k][...]
        first_weights[k] = held["k_" + k]
    spread_weights(1)
    wait(halo_in)

    def shifted_cotangent(x):
        return (cotangent[x + SHIFT] if x < 7 - SHIFT else R.edge_in[x - 7 + SHIFT]).astype(F32)

    take_grid(shifted_cotangent, square, tall, R.grid_two, True)
    wait(slab_in)
    for z in range(SZ + 3):
        pair = R.halo_in[:, 128 * (z % SZ // 2) : 128 * (z % SZ // 2) + 128].astype(F32)
        if z % SZ % 2 == 0:
            pair = roll(pair, 64)
        joined = jnp.where(lane < 64, roll(kept[z % SZ], -48), pair)
        R.grid[:, 128 * z : 128 * z + 128] = joined.astype(BF16)

    def clear(ref):
        ref[...] = jnp.zeros(ref.shape, ref.dtype)

    for ref in vars(G).values():
        clear(ref)
    R.bars[...] = crop_bars(crop, ints, me_win * extent + SHIFT, total)

    def second(w, carry):
        wy, wz = w // 2, lax.rem(w, 2)
        bars = (R.bars[...] + shift_bars(marks, wy, wz)).astype(BF16)
        x = take_window(R.grid, select, 1, wy, wz)
        windows[w] = window_forward(x, W, S, 4, marks, bars)
        grad = take_window(R.grid_two, select, 1, wy, wz)
        deltas[w] = window_backward(grad, W, S, 4, G, marks, bars)
        return carry

    lax.fori_loop(0, 4, second, 0)

    def put_kept(z, value):
        kept[z] = value

    give_grid(deltas, select, 1, put_kept)
    for i in range(7):
        pair = jnp.where(lane < 64, roll(kept[2 * i], 64), kept[2 * i + 1])
        halo_back[:, 128 * i : 128 * i + 128] = pair.astype(BF16)
    slab_back = neighbour("slab_back", halo_back, R.halo_back_in, right)

    def put_tall(z, value):
        tall[C * z : C * z + C, :] = value

    give_grid(windows, select, 1, put_tall)
    give_rows(tall, square)
    for x in range(7 - SHIFT):
        R.block_out[x + SHIFT] = square[16 * x : 16 * x + 14, 0 : SZ * C].astype(BF16)
    for x in range(SHIFT):
        at = 16 * (x + 7 - SHIFT)
        R.edge[x] = square[at : at + 14, 0 : SZ * C].astype(BF16)
    out_back = neighbour("out_back", R.edge, R.edge_back, right)

    piece = R.sums.shape[1] // n_win
    padded = R.sums.shape[1]

    def scatter(b):
        finish_gradients(G, flat, wide, spread, place, tiles)
        for f in range(n_fsdp):
            R.outgoing[b, f, 0:shard, :] = flat[shard * f : shard * f + shard, :].astype(BF16)
            if padded > shard:
                R.outgoing[b, f, shard:padded, :] = jnp.zeros((padded - shard, 128), BF16)
        start(fsdp_copies(b))

    def fsdp_copies(b):
        return to_all(
            ("scatter", b),
            "fsdp",
            me_fsdp,
            n_fsdp,
            lambda to: R.outgoing.at[b, to],
            R.incoming.at[b, me_fsdp],
        )

    def win_copies(b):
        return to_all(
            ("sum", b),
            "win",
            me_win,
            n_win,
            lambda to: R.sums.at[b, pl.ds(pl.multiple_of(piece * to, 16), piece)],
            R.parts.at[b, me_win],
        )

    own = pl.ds(pl.multiple_of(piece * me_win, 16), piece)

    def whole_copies(b):
        mine = R.whole.at[b, own]
        return to_all(("whole", b), "win", me_win, n_win, lambda to: mine, mine)

    def add_fsdp(b):
        wait(fsdp_copies(b))
        R.incoming[b, me_fsdp] = R.outgoing[b, me_fsdp]
        total_rows = R.incoming[b, 0].astype(F32)
        for f in range(1, n_fsdp):
            total_rows += R.incoming[b, f].astype(F32)
        R.sums[b] = total_rows.astype(BF16)
        start(win_copies(b))

    def add_win(b):
        wait(win_copies(b))
        R.parts[b, me_win] = R.sums[b, own, :]
        total_rows = R.parts[b, 0].astype(F32)
        for w in range(1, n_win):
            total_rows += R.parts[b, w].astype(F32)
        R.whole[b, own, :] = total_rows.astype(BF16)
        start(whole_copies(b))

    scatter(1)
    wait(slab_back)
    wait(out_back)
    R.block_out[0:SHIFT] = R.edge_back[...]
    for z in range(SZ):
        pair = R.halo_back_in[:, 128 * (z // 2) : 128 * (z // 2) + 128].astype(F32)
        if z % 2 == 1:
            pair = roll(pair, 64)
        joined = jnp.where(lane < 48, pair, roll(kept[z], 48))
        R.grid[:, 128 * z : 128 * z + 128] = joined.astype(BF16)
    for ref in vars(G).values():
        clear(ref)
    W0 = Names(**{**vars(W), **first_weights})

    def first_backward(w, carry):
        grad = take_window(R.grid, select, 0, w // 2, lax.rem(w, 2))
        deltas[w] = window_backward(grad, W0, S, w, G, marks, R.bars[...].astype(BF16))

        @pl.when(w == 1)
        def _():
            add_fsdp(1)

        @pl.when(w == 2)
        def _():
            add_win(1)

        return carry

    lax.fori_loop(0, 4, first_backward, 0)
    scatter(0)
    give_grid(deltas, select, 0, put_tall)
    give_rows(tall, square)
    for x in range(7):
        R.input_grad[x] = square[16 * x : 16 * x + 14, 0 : SZ * C].astype(BF16)
    for b in range(2):
        R.first_held[b] = BETA_FIRST * R.first[b : b + 1, :].reshape(shard, 128)
        R.second_held[b] = BETA_SECOND * R.second[b : b + 1, :].reshape(shard, 128)
    wait(whole_copies(1))
    add_fsdp(0)
    add_win(0)
    wait(whole_copies(0))

    squares = jnp.zeros((1, 1), F32)
    for b in range(2):
        rows = R.whole[b, 0:shard, :].astype(F32)
        squares += jnp.sum(jnp.sum(rows * rows, axis=0, keepdims=True), axis=1, keepdims=True)
    R.norms[me_fsdp] = jnp.broadcast_to(squares, (8, 128))
    mine = R.norms.at[me_fsdp]
    wait(start(to_all("norm", "fsdp", me_fsdp, n_fsdp, lambda to: mine, mine)))
    norm = R.norms[0]
    for f in range(1, n_fsdp):
        norm += R.norms[f]
    norm = jnp.sqrt(norm)
    R.grad_norm[0, 0] = norm[0, 0]
    factor = jnp.minimum(1.0, CLIP_LIMIT / (norm + 1e-06))[0:1]
    for b in range(2):

        def store(ref, rows):
            ref[b : b + 1, :] = rows.reshape(1, shard * 128)

        clipped = R.whole[b, 0:shard, :].astype(F32) * factor
        new_first = R.first_held[b] + (1.0 - BETA_FIRST) * clipped
        new_second = R.second_held[b] + (1.0 - BETA_SECOND) * clipped * clipped
        first_hat = new_first / (1.0 - BETA_FIRST**STEP)
        second_hat = new_second / (1.0 - BETA_SECOND**STEP)
        params = R.own[b]
        store(
            R.new_params,
            params
            - LEARN_RATE
            * (first_hat / (jnp.sqrt(second_hat) + EPS_ADAM) + WEIGHT_DECAY * params),
        )
        store(R.new_first, new_first)
        store(R.new_second, new_second)
    R.params_copy[...] = R.new_params[...].astype(BF16)


def per_device(n_win, n_fsdp, tokens, cotangent, crop_ids, params, first_moment, second_moment):
    ints, marks = constant_tables()
    extent = tokens.shape[1]
    shard = params.shape[1] // 128
    held = round_up(shard, 16)
    padded = round_up(-(-shard // n_win), 16) * n_win
    rows = jax.ShapeDtypeStruct(params.shape, F32)
    cells = jax.ShapeDtypeStruct((extent, SY, SZ * C), BF16)
    inputs = dict(
        tokens=tokens[0],
        cotangent=cotangent[0],
        crop=crop_ids,
        ints=ints,
        marks=marks,
        params=params,
        first=first_moment,
        second=second_moment,
    )
    outputs = dict(
        block_out=cells,
        input_grad=cells,
        grad_norm=jax.ShapeDtypeStruct((1, 1), F32),
        new_params=rows,
        new_first=rows,
        new_second=rows,
        params_copy=jax.ShapeDtypeStruct(params.shape, BF16),
    )
    V = pltpu.VMEM
    edge = V((SHIFT, SY, SZ * C), BF16)
    scratch = dict(
        own=V((2, shard, 128), F32),
        first_held=V((2, shard, 128), F32),
        second_held=V((2, shard, 128), F32),
        gathered=V((n_fsdp, 2, held, 128), BF16),
        edge=edge,
        edge_in=edge,
        edge_back=edge,
        halo=V((C, 896), BF16),
        halo_in=V((C, 896), BF16),
        halo_back=V((C, 896), BF16),
        halo_back_in=V((C, 896), BF16),
        outgoing=V((2, n_fsdp, padded, 128), BF16),
        incoming=V((2, n_fsdp, padded, 128), BF16),
        sums=V((2, padded, 128), BF16),
        parts=V((2, n_win, padded // n_win, 128), BF16),
        whole=V((2, padded, 128), BF16),
        norms=V((n_fsdp, 8, 128), F32),
        select=V((2, 896, 2 * QLANE), BF16),
        place=V((896, QLANE), BF16),
        spread=V((176, 49 * 128), BF16),
        flat=V((FLAT + 8, 128), F32),
        wide=V((3, 384, 128), F32),
        tiles=V((80 * 56, 128), F32),
        square=V((128, 1408), F32),
        tall=V((1408, 128), F32),
        grid=V((C, 17 * 128), BF16),
        grid_two=V((C, 17 * 128), BF16),
        kept=V((SZ, C, 128), F32),
        windows=V((4, C, QLANE), F32),
        deltas=V((4, C, QLANE), F32),
        bars=V((32, QLANE), F32),
    )
    for k, (shape, kind) in WEIGHT_SHAPES.items():
        scratch["w_" + k] = V(shape, kind)
    for k in ("cols", "q_n", "kv_n", "proj_n", "one_n", "two_n"):
        scratch["k_" + k] = V(*WEIGHT_SHAPES[k])
    for k, (shape, kind) in SAVED_SHAPES.items():
        scratch["s_" + k] = V((5, *shape), kind)
    for k, (shape, kind) in GRAD_SHAPES.items():
        scratch["g_" + k] = V(shape, kind)
    copies = 5 * (n_fsdp - 1) + 4 * (n_win - 1) + 4
    scratch["send"] = pltpu.SemaphoreType.DMA((copies,))
    scratch["recv"] = pltpu.SemaphoreType.DMA((copies,))
    names = [*inputs, *outputs, *scratch]
    vmem = pl.BlockSpec(memory_space=pltpu.VMEM)
    smem = pl.BlockSpec(memory_space=pltpu.SMEM)
    results = pl.pallas_call(
        functools.partial(step_kernel, n_win, n_fsdp, names),
        out_shape=tuple(outputs.values()),
        in_specs=[smem if k == "crop" else vmem for k in inputs],
        out_specs=tuple(smem if k == "grad_norm" else vmem for k in outputs),
        scratch_shapes=list(scratch.values()),
        compiler_params=pltpu.CompilerParams(
            collective_id=0 if n_win * n_fsdp > 1 else None,
            has_side_effects=True,
            vmem_limit_bytes=66 * 1024 * 1024 - 2 * 1024 * 1024,
        ),
        name="layer_step",
    )(*inputs.values())
    block_out, input_grad, grad_norm, *states = results
    return (block_out[None], input_grad[None], grad_norm[0, 0], *states)


def solution(mesh):
    data = P("fsdp", "win", None, None)
    state = P(None, "fsdp")
    return jax.shard_map(
        functools.partial(per_device, mesh.shape["win"], mesh.shape["fsdp"]),
        mesh=mesh,
        in_specs=(data, data, P("fsdp", None), state, state, state),
        out_specs=(data, data, P(), state, state, state, state),
        check_vma=False,
    )
```

```python
import functools
from types import SimpleNamespace as Names

import jax
import jax.numpy as jnp
import numpy as np
from jax import lax
from jax.experimental import pallas as pl
from jax.experimental.pallas import tpu as pltpu
from jax.sharding import PartitionSpec as P

C = 96
HEADS = 6
HEAD = 16
HID = 384
WS = 7
SHIFT = 3
SY = 14
SZ = 14
BPAD = 124928
STEP = 5
EPS_NORM = 1e-05
CLIP_LIMIT = 1.0
LEARN_RATE = 0.4
BETA_FIRST = 0.9
BETA_SECOND = 0.999
WEIGHT_DECAY = 0.05
EPS_ADAM = 1e-08
BIG = 1e30
LOG2E = 1.4426950408889634
LN2 = 0.6931471805599453

CELLS = WS**3
KROW = 352
QLANE = 384
FLAT = BPAD // 128
ROW_PROJ = 216
ROW_ONE = 288
ROW_TWO = 576
ROW_TABLE = 864
ROW_TAIL = 966
V_GAIN1, V_BIAS1, V_BQ, V_BV, V_BPROJ, V_GAIN2, V_BIAS2, V_BHID, V_BOUT = (
    0, 96, 192, 288, 384, 480, 576, 672, 1056,
)

F32 = jnp.float32
BF16 = jnp.bfloat16


def nn(a, b):
    return lax.dot_general(a, b, (((1,), (0,)), ((), ())), preferred_element_type=F32)


def nt(a, b):
    return lax.dot_general(a, b, (((1,), (1,)), ((), ())), preferred_element_type=F32)


def iota(shape, dim):
    return lax.broadcasted_iota(jnp.int32, shape, dim)


def roll(x, by):
    by = by % 128
    return x if by == 0 else pltpu.roll(x, by, 1)


def skew(x, by):
    while by > 0:
        some = min(1 << (by.bit_length() - 1), 16)
        x = pltpu.roll(x, 0, 1, stride=some, stride_axis=0)
        by -= some
    return x


def constant_tables():
    t = np.arange(QLANE)
    live = t < CELLS
    z, x, y = t // 49, t % 49 // 7, t % 7
    ints = np.full((8, QLANE), -1, np.int32)
    for s in range(2):
        for wy in range(2):
            cell_y = (y + 7 * wy + SHIFT * s) % SY
            ints[2 * s + wy] = np.where(live, z * 128 + x * 16 + cell_y, -1)
    ints[4] = np.where(live, z * 128 + t % 49, -1)
    ints[5] = np.where(live, x, -1)
    lane = np.arange(128)
    ints[6, :128] = np.where(lane < 49, 13 * (lane // 7) + lane % 7, -1000)
    marks = np.zeros((64, QLANE), np.float32)
    for i in range(7):
        marks[i] = live & (x == i)
        marks[7 + i] = live & (y == i)
        marks[14 + i] = live & (z == i)
        marks[32 + 7 + i] = live & ((i >= 4) != (y >= 4))
        marks[32 + 14 + i] = live & ((i >= 4) != (z >= 4))
    return jnp.asarray(ints), jnp.asarray(marks, BF16)


def unit_copy(pieces, units):
    out = None
    for at, unit in enumerate(units):
        if unit is None:
            continue
        i, g = unit
        moved = roll(pieces[i], 32 * (at - g))
        group = iota(moved.shape, 1) // 32
        base = jnp.zeros_like(moved) if out is None else out
        out = jnp.where(group == at, moved, base)
    return out


def read_matrix(flat, base, rows, width, store):
    units = width // 32
    if units % 4 == 0:
        step = units // 4
        for o in range(step):
            store(0, 1, o, flat[pl.ds(base + o, rows, stride=step), :])
        return
    groups = rows // 4
    loaded = [flat[pl.ds(base + o, groups, stride=units), :] for o in range(units)]
    for j in range(4):
        for p in range(units // 3):
            first = units * j + 3 * p
            store(j, 4, p, unit_copy(loaded, [divmod(first + s, 4) for s in range(3)] + [None]))


def write_matrix(flat, base, rows, width, load):
    units = width // 32
    if units % 4 == 0:
        step = units // 4
        for o in range(step):
            flat[pl.ds(base + o, rows, stride=step), :] = load(0, 1, o)
        return
    groups = rows // 4
    parts = units // 3
    loaded = [load(j, 4, p) for j in range(4) for p in range(parts)]
    for o in range(units):
        flat[pl.ds(base + o, groups, stride=units), :] = unit_copy(
            loaded, [divmod(4 * o + g, 3) for g in range(4)]
        )


def build_selectors(ints, select, place, spread):
    for s in range(2):
        for wy in range(2):
            need = ints[2 * s + wy : 2 * s + wy + 1, :]
            for r in range(7):
                row = iota((128, QLANE), 0) + 128 * r
                select[s, 128 * r : 128 * r + 128, QLANE * wy : QLANE * wy + QLANE] = jnp.where(
                    row == need, 1.0, 0.0
                ).astype(BF16)
    need = ints[4:5, :]
    for r in range(7):
        row = iota((128, QLANE), 0) + 128 * r
        place[128 * r : 128 * r + 128, :] = jnp.where(row == need, 1.0, 0.0).astype(BF16)
    gap = iota((176, 128), 0) - ints[6:7, :128]
    for k in range(49):
        hit = gap == 84 - 13 * (k // 7) - k % 7
        spread[:, 128 * k : 128 * k + 128] = jnp.where(hit, 1.0, 0.0).astype(BF16)


def table_pick(second):
    row = iota((176, 104), 0)
    col = iota((176, 104), 1) - second
    at = 128 * col
    start = 78 * row
    hit = (start >= at) & (start < at + 128) & (row < 169)
    return jnp.where(hit, 1.0, 0.0).astype(BF16)


def table_start():
    row = iota((176, 128), 0)
    return jnp.bitwise_and(78 * row, 127)


def build_table(flat, spread, place, tiles, table):
    rows = flat[ROW_TABLE : ROW_TABLE + 104, :].astype(BF16)
    first = skew(nn(table_pick(0), rows), 50)
    second = skew(nn(table_pick(1), rows), 50)
    lane = iota((176, 128), 1)
    mixed = jnp.where(lane + table_start() < 128, first, second)
    mixed = jnp.where((lane < 78) & (iota((176, 128), 0) < 169), mixed, 0.0)
    turned = jnp.concatenate([mixed, jnp.zeros((80, 128), F32)], axis=0).T
    cube = turned[:80, :176].astype(BF16)
    for k in range(0, 49, 2):
        some = min(2, 49 - k)
        block = nn(cube, spread[:, 128 * k : 128 * k + 128 * some])
        for i in range(some):
            tiles[pl.ds(k + i, 80, stride=56), :] = block[:, 128 * i : 128 * i + 128]

    def gathered(ck, first, last):
        return jnp.concatenate(
            [
                tiles[336 * (cq - ck + 6) : 336 * (cq - ck + 7), :].astype(BF16)
                for cq in range(first, last)
            ],
            axis=1,
        )

    for ck in range(7):
        block = jnp.concatenate(
            [
                nn(gathered(ck, 0, 6), place[0:768, 0:256]),
                nn(gathered(ck, 5, 7), place[640:896, 256:QLANE]),
            ],
            axis=1,
        )
        block = block * LOG2E
        for h in range(HEADS):
            table[h, 49 * ck : 49 * ck + 49, :] = block[56 * h : 56 * h + 49, :]
    for h in range(HEADS):
        table[h, CELLS:KROW, :] = jnp.full((KROW - CELLS, QLANE), -BIG, F32)


def collapse_table(total, spread, place, tiles, flat):
    tiles[...] = jnp.zeros(tiles.shape, F32)
    for ck in range(7):
        lhs = jnp.concatenate(
            [total[h, 49 * ck : 49 * ck + 56, :] for h in range(HEADS)], axis=0
        ).astype(BF16)
        for cq, start, end in ((0, 0, 128), (2, 0, 256), (4, 128, 384), (6, 256, 384)):
            some = min(2, 7 - cq)
            block = nt(lhs[:, start:end], place[128 * cq : 128 * cq + 128 * some, start:end])
            for i in range(some):
                dc = cq + i - ck + 6
                tiles[336 * dc : 336 * dc + 336, :] += block[:, 128 * i : 128 * i + 128]
    lhs = jnp.concatenate(
        [tiles[pl.ds(k, 80, stride=56), :].astype(BF16) for k in range(49)], axis=1
    )
    cube = nt(lhs, spread[...])
    wide = jnp.concatenate([cube, jnp.zeros((80, 80), F32)], axis=1)
    wide = jnp.concatenate([wide, jnp.zeros((48, 256), F32)], axis=0)
    mixed = wide.T[:176, :]
    mixed = skew(mixed, 78)
    fits = iota((176, 128), 1) >= table_start()
    lane = iota((176, 128), 1)
    length = jnp.bitwise_and(lane - table_start(), 127)
    live = (length < 78) & (iota((176, 128), 0) < 169)
    head = jnp.where(fits & live, mixed, 0.0).astype(BF16)
    rest = jnp.where(jnp.logical_not(fits) & live, mixed, 0.0).astype(BF16)

    def tn(a, b):
        return lax.dot_general(a, b, (((0,), (0,)), ((), ())), preferred_element_type=F32)

    return tn(table_pick(0), head) + tn(table_pick(1), rest)


def tail_vector(tail, start, width):
    o, at = divmod(start, 128)
    lane = iota((1, 128), 1)
    out = roll(tail[o : o + 1, :], -at)
    if at + width > 128:
        out = jnp.where(lane < 128 - at, out, roll(tail[o + 1 : o + 2, :], -at))
    return jnp.where(lane < width, out, 0.0)


def prepare(flat, W, wide, spread, place, tiles):
    rows = flat[ROW_TAIL : ROW_TAIL + 16, :]
    lane = iota((9, 128), 1)
    tail = jnp.where(lane < 2, roll(rows[:9], 2), roll(rows[1:10], 2))
    turned = jnp.concatenate([tail, jnp.zeros((119, 128), F32)], axis=0).T
    for o in range(9):
        W.cols[128 * o : 128 * o + 128, :] = jnp.broadcast_to(turned[:, o : o + 1], (128, 128))

    def into(j, step, p, value):
        wide[p, pl.ds(j, value.shape[0], stride=step), :] = value

    def finish(p, bias):
        wide[p, 96:97, :] = bias
        wide[p, 97:128, :] = jnp.zeros((31, 128), F32)

    read_matrix(flat, 0, C, 3 * C, into)
    finish(0, tail_vector(tail, V_BQ, C))
    finish(1, jnp.zeros((1, 128), F32))
    finish(2, tail_vector(tail, V_BV, C))
    W.q_n[...] = wide[0, 0:96, :].astype(BF16)
    for p in range(1, 3):
        W.kv_n[:, 128 * p - 128 : 128 * p] = wide[p, 0:96, :].astype(BF16)
    for p in range(3):
        W.qkv_t[96 * p : 96 * p + 96, :] = wide[p, 0:128, :].T[:96].astype(BF16)

    read_matrix(flat, ROW_PROJ, C, C, into)
    finish(0, tail_vector(tail, V_BPROJ, C))
    W.proj_n[...] = wide[0, 0:96, :].astype(BF16)
    W.proj_t[...] = wide[0, 0:128, :].T[:96].astype(BF16)

    read_matrix(flat, ROW_ONE, C, HID, into)
    for p in range(3):
        finish(p, tail_vector(tail, V_BHID + 128 * p, 128))
        W.one_n[:, 128 * p : 128 * p + 128] = wide[p, 0:96, :].astype(BF16)
        W.one_t[128 * p : 128 * p + 128, :] = wide[p, 0:128, :].T.astype(BF16)

    read_matrix(flat, ROW_TWO, HID, C, into)
    W.two_n[...] = wide[0].astype(BF16)
    for p in range(3):
        W.two_t[:, 128 * p : 128 * p + 128] = wide[0, 128 * p : 128 * p + 128, :].T[:96].astype(
            BF16
        )
    build_table(flat, spread, place, tiles, W.table)


WEIGHT_SHAPES = dict(
    cols=((1152, 128), F32),
    q_n=((96, 128), BF16),
    kv_n=((96, 256), BF16),
    qkv_t=((288, 128), BF16),
    proj_n=((96, 128), BF16),
    proj_t=((96, 128), BF16),
    one_n=((96, 384), BF16),
    one_t=((384, 128), BF16),
    two_n=((384, 128), BF16),
    two_t=((96, 384), BF16),
    table=((HEADS, KROW, QLANE), F32),
)


SAVED_SHAPES = dict(
    normed=((128, QLANE), BF16),
    hat=((96, QLANE), F32),
    scale=((8, QLANE), F32),
    qkv=((288, QLANE), BF16),
    probs=((HEADS, KROW, QLANE), BF16),
    inverse=((8, QLANE), F32),
    attended=((128, QLANE), BF16),
    hat_two=((96, QLANE), F32),
    scale_two=((8, QLANE), F32),
    normed_two=((128, QLANE), BF16),
    slope=((HID, QLANE), BF16),
    active=((HID, QLANE), BF16),
)

GRAD_SHAPES = dict(
    q=((112, 128), F32),
    kv=((2, 112, 128), F32),
    proj=((112, 128), F32),
    one=((112, 384), F32),
    two=((400, 128), F32),
    gain1=((96, 128), F32),
    bias1=((96, 128), F32),
    gain2=((96, 128), F32),
    bias2=((96, 128), F32),
    total=((HEADS, KROW, QLANE), F32),
)


def column(W, start, rows=96):
    part = W.cols[start : start + rows, :]
    return jnp.concatenate([part, part, part], axis=1)


def extended(rows):
    width = rows.shape[1]
    return jnp.concatenate([rows, jnp.ones((16, width), BF16), jnp.zeros((16, width), BF16)], axis=0)


def standardize(x):
    centered = x - jnp.mean(x, axis=0, keepdims=True)
    variance = jnp.mean(centered * centered, axis=0, keepdims=True)
    scale = lax.rsqrt(variance + EPS_NORM)
    return centered * scale, scale


def at_head(h, rows, tail):
    width = rows.shape[1]
    parts = []
    if h > 0:
        parts.append(jnp.zeros((16 * h, width), BF16))
    parts.append(rows)
    if h < HEADS - 1:
        parts.append(jnp.zeros((16 * (HEADS - 1 - h), width), BF16))
    return jnp.concatenate(parts + [tail], axis=0)


def scaled_queries(qkv):
    return (qkv[0:96].astype(F32) * (HEAD**-0.5 * LOG2E)).astype(BF16)


def window_norm(x, S, s):
    hat, scale = standardize(x)
    S.hat[s] = hat
    S.scale[s, 0:1] = scale


def window_forward(x, W, S, s, marks, barred):
    hat = S.hat[s]
    normed = extended((hat * column(W, V_GAIN1) + column(W, V_BIAS1)).astype(BF16))
    S.normed[s] = normed
    qkv = nn(W.qkv_t[...], normed).astype(BF16)
    S.qkv[s] = qkv
    queries = scaled_queries(qkv)
    keys = jnp.concatenate([qkv[96:192], marks[0:32, :]], axis=0).T[:KROW]
    ones = jnp.ones((16, KROW), BF16)

    def pair_scores(p):
        sides = [at_head(h, queries[16 * h : 16 * h + 16], barred) for h in (2 * p, 2 * p + 1)]
        return nn(keys, jnp.concatenate(sides, axis=1))

    parts = []
    coming = pair_scores(0)
    for h in range(HEADS):
        if h % 2 == 0:
            pair = coming
            if h + 2 < HEADS:
                coming = pair_scores(h // 2 + 1)
        scores = pair[:, QLANE * (h % 2) : QLANE * (h % 2) + QLANE] + W.table[h]
        highest = jnp.max(scores, axis=0, keepdims=True)
        probs = jnp.exp2(scores - highest).astype(BF16)
        S.probs[s, h] = probs
        values = jnp.concatenate([qkv[192 + 16 * h : 208 + 16 * h, :KROW], ones], axis=0)
        mixed = nn(values, probs)
        inverse = 1.0 / mixed[16:17]
        S.inverse[s, h : h + 1] = inverse
        parts.append((mixed[:16] * inverse).astype(BF16))
    attended = extended(jnp.concatenate(parts, axis=0))
    S.attended[s] = attended
    branch = nn(W.proj_t[...], attended).astype(BF16)
    middle = x + branch.astype(F32)
    hat, scale = standardize(middle)
    S.hat_two[s] = hat
    S.scale_two[s, 0:1] = scale
    normed_two = extended((hat * column(W, V_GAIN2) + column(W, V_BIAS2)).astype(BF16))
    S.normed_two[s] = normed_two
    hidden = nn(W.one_t[...], normed_two)
    share = 0.5 + 0.5 * lax.erf(hidden * (0.5**0.5))
    active = (hidden * share).astype(BF16)
    S.active[s] = active
    slope = share + hidden * jnp.exp2(hidden * hidden * (-0.5 * LOG2E)) * 0.3989422804014327
    S.slope[s] = slope.astype(BF16)
    return middle + nn(W.two_t[...], active) + column(W, V_BOUT)


def fold(x):
    return x[:, 0:128] + x[:, 128:256] + x[:, 256:384]


def norm_backward(grad, hat, scale, gain):
    scaled = grad * gain
    mean_one = jnp.mean(scaled, axis=0, keepdims=True)
    mean_two = jnp.mean(scaled * hat, axis=0, keepdims=True)
    return scale * (scaled - mean_one - hat * mean_two)


def window_backward(grad, W, S, s, G, marks, barred):
    result = extended(grad.astype(BF16))
    active = S.active[s]
    G.two[...] += nt(jnp.concatenate([active, jnp.ones((16, QLANE), BF16)], axis=0), result)
    hidden = (nn(W.two_n[...], result) * S.slope[s].astype(F32)).astype(BF16)
    G.one[...] += nt(S.normed_two[s, 0:112], hidden)
    d_normed = nn(W.one_n[...], hidden)
    hat = S.hat_two[s]
    G.gain2[...] += fold(d_normed * hat)
    G.bias2[...] += fold(d_normed)
    d_middle = grad + norm_backward(d_normed, hat, S.scale_two[s, 0:1], column(W, V_GAIN2))
    d_branch = extended(d_middle.astype(BF16))
    attended = S.attended[s]
    G.proj[...] += nt(attended[0:112], d_branch)
    d_attended = nn(W.proj_n[...], d_branch).astype(BF16).astype(F32)
    product = d_attended * attended[0:96].astype(F32)
    qkv = S.qkv[s]
    queries = scaled_queries(qkv)
    values = extended(qkv[192:288]).T[:KROW]
    d_both = jnp.zeros((KROW, 256), F32)
    none = jnp.zeros((32, QLANE), BF16)
    blank = jnp.zeros((128, QLANE), BF16)
    row = iota((32, QLANE), 0)
    parts = []

    def head_gradient(h):
        inverse = S.inverse[s, h : h + 1]
        inner = jnp.sum(product[16 * h : 16 * h + 16], axis=0, keepdims=True) * inverse
        high = inner.astype(BF16)
        low = (inner - high.astype(F32)).astype(BF16)
        less = jnp.where(row == 0, -high.astype(F32), jnp.where(row == 1, -low.astype(F32), 0.0))
        rows = (d_attended[16 * h : 16 * h + 16] * inverse).astype(BF16)
        return at_head(h, rows, less.astype(BF16))

    for p in range(HEADS // 2):
        d_outs = [head_gradient(h) for h in (2 * p, 2 * p + 1)]
        d_pair = nn(values, jnp.concatenate(d_outs, axis=1)).astype(BF16)
        for h in (2 * p, 2 * p + 1):
            probs = S.probs[s, h]
            d_scores = probs * d_pair[:, QLANE * (h % 2) : QLANE * (h % 2) + QLANE]
            G.total[h] += d_scores.astype(F32)
            sides = jnp.concatenate(
                [
                    jnp.concatenate(
                        [at_head(h, queries[16 * h : 16 * h + 16], none), blank], axis=0
                    ),
                    jnp.concatenate([blank, d_outs[h % 2]], axis=0),
                ],
                axis=1,
            )
            d_both += nt(jnp.concatenate([d_scores, probs], axis=1), sides)
            parts.append(nn(qkv[96 + 16 * h : 112 + 16 * h, :KROW], d_scores))
    d_queries = (jnp.concatenate(parts, axis=0) * HEAD**-0.5).astype(BF16)
    lane = iota((KROW, 256), 1)
    factor = jnp.where(lane < 96, LN2, jnp.where((lane >= 128) & (lane < 224), 1.0, 0.0))
    d_pair = jnp.where(factor > 0, d_both * factor, 0.0).astype(BF16)
    normed = S.normed[s, 0:112]
    G.q[:, 0:96] += nt(normed, d_queries)
    both = nn(normed[:, :KROW], d_pair)
    for p in range(2):
        G.kv[p] += both[:, 128 * p : 128 * p + 128]
    d_pair = jnp.concatenate([d_pair, jnp.zeros((QLANE - KROW, 256), BF16)], axis=0)
    d_normed = nn(W.q_n[:, 0:96], d_queries) + nt(W.kv_n[...], d_pair)
    hat = S.hat[s]
    G.gain1[...] += fold(d_normed * hat)
    G.bias1[...] += fold(d_normed)
    return d_middle + norm_backward(d_normed, hat, S.scale[s, 0:1], column(W, V_GAIN1))


def finish_gradients(G, flat, wide, spread, place, tiles):
    def qkv_rows(j, step, p):
        if p == 0:
            return G.q[pl.ds(j, 24, stride=4), :]
        return G.kv[p - 1, pl.ds(j, 24, stride=4), :]

    write_matrix(flat, 0, C, 3 * C, qkv_rows)
    write_matrix(flat, ROW_PROJ, C, C, lambda j, step, p: G.proj[pl.ds(j, 24, stride=4), :])
    write_matrix(
        flat, ROW_ONE, C, HID, lambda j, step, p: G.one[0:96, 128 * p : 128 * p + 128]
    )
    write_matrix(flat, ROW_TWO, HID, C, lambda j, step, p: G.two[pl.ds(j, 96, stride=4), :])
    lane = iota((96, 128), 1)
    columns = jnp.zeros((96, 128), F32)
    for at, ref in enumerate([G.gain1, G.bias1, G.gain2, G.bias2]):
        columns = jnp.where(lane == at, jnp.sum(ref[...], axis=1, keepdims=True), columns)
    turned = jnp.concatenate([columns, jnp.zeros((32, 128), F32)], axis=0).T
    sources = [
        (turned[0:1], 3),
        (turned[1:2], 3),
        (G.q[96:97, :], 3),
        (G.kv[1, 96:97, :], 3),
        (G.proj[96:97, :], 3),
        (turned[2:3], 3),
        (turned[3:4], 3),
        (G.one[96:97, 0:128], 4),
        (G.one[96:97, 128:256], 4),
        (G.one[96:97, 256:384], 4),
        (G.two[384:385, :], 3),
    ]
    pieces = [source for source, _ in sources]
    units = [(i, g) for i, (_, count) in enumerate(sources) for g in range(count)]
    tail = jnp.concatenate(
        [unit_copy(pieces, units[4 * o : 4 * o + 4]) for o in range(9)], axis=0
    )
    table = collapse_table(G.total, spread, place, tiles, flat)
    flat[ROW_TABLE:ROW_TAIL, :] = table[0:102]
    none = jnp.zeros((1, 128), F32)
    moved = roll(jnp.concatenate([none, tail, none], axis=0), 126)
    lane = iota((10, 128), 1)
    mixed = jnp.where(lane >= 126, moved[1:11], moved[0:10])
    first = jnp.where(iota((1, 128), 1) >= 126, mixed[0:1], table[102:103])
    flat[ROW_TAIL:FLAT, :] = jnp.concatenate([first, mixed[1:10]], axis=0)


def round_up(value, to):
    return -(-value // to) * to


def take_grid(row_of, square, tall, grid, wrapped):
    for x in range(7):
        square[16 * x : 16 * x + 14, 0 : SZ * C] = row_of(x)
    for i in range(11):
        tall[128 * i : 128 * i + 128, :] = square[:, 128 * i : 128 * i + 128].T
    for z in range(SZ + 3 if wrapped else SZ):
        grid[:, 128 * z : 128 * z + 128] = tall[C * (z % SZ) : C * (z % SZ) + C, :].astype(BF16)


def take_window(grid, select, s, wy, wz):
    rows = grid[:, pl.ds(pl.multiple_of(896 * wz + 384 * s, 128), 896)]
    return nn(rows, select[s, :, pl.ds(pl.multiple_of(QLANE * wy, 128), QLANE)])


def give_grid(windows, select, s, wz, put):
    both = jnp.concatenate([windows[2 * wz], windows[2 * wz + 1]], axis=1).astype(BF16)
    cells = nt(both, select[s])
    for r in range(7):
        put((r + 7 * wz + SHIFT * s) % SZ, cells[:, 128 * r : 128 * r + 128])


def give_rows(tall, square):
    for i in range(11):
        square[:, 128 * i : 128 * i + 128] = tall[128 * i : 128 * i + 128, :].T


def crop_bars(crop, ints, first, total):
    ids = [crop[0, lax.rem(first + a, total)] for a in range(7)]
    at = ints[5:6, :]
    own = jnp.zeros((1, QLANE), jnp.int32)
    for a in range(7):
        own = jnp.where(at == a, ids[a], own)
    row = iota((32, QLANE), 0)
    key = jnp.full((32, QLANE), -1, jnp.int32)
    for a in range(7):
        key = jnp.where(row == a, ids[a], key)
    return jnp.where((row < 7) & (key != own), -BIG, 0.0)


def shift_bars(marks, wy, wz):
    row = iota((32, QLANE), 0)
    factor = jnp.where(row < 14, wy, wz).astype(F32) * -BIG
    return marks[32:64, :].astype(F32) * factor


STAGED = ("params", "tokens", "cotangent", "first_moment", "second_moment")
RESULTS = (
    "block_out", "input_grad", "new_params", "new_first", "new_second", "params_copy",
)


def near_extent(n_win):
    n_x = 1
    while 4 * n_x * n_x <= n_win:
        n_x *= 2
    return n_x


def step_kernel(n_win, n_fsdp, names, *refs):
    held = dict(zip(names, refs))
    R = Names(**held)
    W = Names(**{k: held["w_" + k] for k in WEIGHT_SHAPES})
    S = Names(**{k: held["s_" + k] for k in SAVED_SHAPES})
    G = Names(**{k: held["g_" + k] for k in GRAD_SHAPES})
    tokens, cotangent, crop = R.tokens, R.cotangent, R.crop
    ints, marks = R.ints, R.marks
    select, place, spread = R.select, R.place, R.spread
    flat, wide, tiles = R.flat, R.wide, R.tiles
    square, tall = R.square, R.tall
    send, recv = R.send, R.recv
    shard = FLAT // n_fsdp
    extent = tokens.shape[0]
    total = n_win * extent
    me_win, me_fsdp = lax.axis_index("win"), lax.axis_index("fsdp")
    left, right = lax.rem(me_win + n_win - 1, n_win), lax.rem(me_win + 1, n_win)
    n_x = near_extent(n_win)
    n_z = n_win // n_x
    me_x, me_z = lax.rem(me_win, n_x), me_win // n_x
    me_near = me_fsdp * n_x + me_x
    near = []
    for k in range(1, n_fsdp * n_x):
        f, x = lax.rem(me_fsdp + k // n_x, n_fsdp), lax.rem(me_x + k % n_x, n_x)
        near.append((k, f, x, {"win": me_z * n_x + x, "fsdp": f}))
    far = [(k, {"win": lax.rem(me_z + k, n_z) * n_x + me_x}) for k in range(1, n_z)]
    sides = [{"win": left}, {"win": right}] if n_win > 1 else []
    slots = {}

    def remote(name, src, dst, to):
        slot = slots.setdefault(name, len(slots))
        return pltpu.make_async_remote_copy(
            src_ref=src,
            dst_ref=dst,
            send_sem=send.at[slot],
            recv_sem=recv.at[slot],
            device_id=to,
            device_id_type=pl.DeviceIdType.MESH,
        )

    def start(copies):
        for copy in copies:
            copy.start()
        return copies

    def neighbour(name, src, dst, to):
        if n_win > 1:
            return start([remote(name, src, dst, {"win": to})])
        dst[...] = src[...]
        return []

    def fetch(k):
        at = STAGED.index(k)
        return pltpu.make_async_copy(held["hbm_" + k], held[k], R.local.at[at])

    def flush(k):
        at = len(STAGED) + RESULTS.index(k)
        return pltpu.make_async_copy(held[k], held["hbm_" + k], R.local.at[at])

    def wait(copies):
        for copy in copies:
            copy.wait()

    start([fetch(k) for k in STAGED])
    if n_win * n_fsdp > 1:
        barrier = pltpu.get_barrier_semaphore()
        peers = [peer[-1] for peer in near + far] + sides
        for peer in peers:
            pl.semaphore_signal(
                barrier, inc=1, device_id=peer, device_id_type=pl.DeviceIdType.MESH
            )
    gathered = R.gathered
    fetch("params").wait()
    for b in range(2):
        R.own[b] = R.params[b : b + 1, :].reshape(shard, 128)
        gathered[me_fsdp, b, 0:shard, :] = R.own[b].astype(BF16)
    fetch("cotangent").wait()
    R.edge[...] = cotangent[0:SHIFT]
    build_selectors(ints, select, place, spread)
    square[...] = jnp.zeros(square.shape, F32)
    fetch("tokens").wait()
    take_grid(lambda x: tokens[x].astype(F32), square, tall, R.grid, False)
    windows, deltas = R.windows, R.deltas

    def first_window(w, carry):
        x = take_window(R.grid, select, 0, lax.rem(w, 2), w // 2)
        windows[w] = x
        window_norm(x, S, w)
        return carry

    lax.fori_loop(0, 4, first_window, 0)
    if n_win * n_fsdp > 1:
        pl.semaphore_wait(barrier, len(peers))

    weights_in = []
    for b in range(2):
        mine = gathered.at[me_fsdp, b]
        copies = []
        for k in range(1, n_fsdp):
            to = {"fsdp": lax.rem(me_fsdp + k, n_fsdp)}
            copies.append(remote(("weights", b, k), mine, mine, to))
        weights_in.append(start(copies))
    halo_in = neighbour("halo", R.edge, R.edge_in, left)

    def clear(ref):
        ref[...] = jnp.zeros(ref.shape, ref.dtype)

    for ref in vars(G).values():
        clear(ref)
    wait(halo_in)

    def shifted_cotangent(x):
        return (cotangent[x + SHIFT] if x < 7 - SHIFT else R.edge_in[x - 7 + SHIFT]).astype(F32)

    take_grid(shifted_cotangent, square, tall, R.grid_two, True)

    def spread_weights(b):
        wait(weights_in[b])
        for f in range(n_fsdp):
            flat[shard * f : shard * f + shard, :] = gathered[f, b, 0:shard, :].astype(F32)
        prepare(flat, W, wide, spread, place, tiles)

    spread_weights(0)
    R.bars[...] = crop_bars(crop, ints, me_win * extent, total)

    halo, halo_back = R.halo, R.halo_back
    kept = R.kept
    lane = iota((C, 128), 1)
    slab_parts = [(0, 3), (3, 7)]

    def slab_copy(wz, name, src, dst, to):
        start, end = slab_parts[wz]
        part = pl.ds(start, end - start)
        return remote((name, wz), src.at[part], dst.at[part], {"win": to})

    def pass_slab(wz, name, src, dst, to):
        if n_win > 1:
            slab_copy(wz, name, src, dst, to).start()
        else:
            start, end = slab_parts[wz]
            dst[start:end] = src[start:end]

    def wait_slab(name, src, dst, to):
        if n_win > 1:
            wait([slab_copy(wz, name, src, dst, to) for wz in range(2)])

    def put_kept(z, value):
        kept[z] = value

    def give_slices(wz):
        give_grid(windows, select, 0, wz, put_kept)
        for i in range(*slab_parts[wz]):
            pair = jnp.where(lane < 64, kept[2 * i], roll(kept[2 * i + 1], 64))
            halo[i] = pair.astype(BF16)
        pass_slab(wz, "slab", halo, R.halo_in, left)

    def first_forward(w, carry):
        windows[w] = window_forward(windows[w], W, S, w, marks, R.bars[...].astype(BF16))

        @pl.when(w == 1)
        def _():
            give_slices(0)

        return carry

    lax.fori_loop(0, 4, first_forward, 0)

    give_slices(1)
    first_weights = {}
    for k in ("cols", "q_n", "kv_n", "proj_n", "one_n", "two_n"):
        held["k_" + k][...] = held["w_" + k][...]
        first_weights[k] = held["k_" + k]
    spread_weights(1)
    wait_slab("slab", halo, R.halo_in, left)
    for z in range(SZ + 3):
        pair = R.halo_in[z % SZ // 2].astype(F32)
        if z % SZ % 2 == 0:
            pair = roll(pair, 64)
        joined = jnp.where(lane < 64, roll(kept[z % SZ], -48), pair)
        R.grid[:, 128 * z : 128 * z + 128] = joined.astype(BF16)

    R.bars[...] = crop_bars(crop, ints, me_win * extent + SHIFT, total)

    def give_back(wz):
        give_grid(deltas, select, 1, wz, put_kept)
        for at in range(*slab_parts[wz]):
            i = (at + 2) % 7
            pair = jnp.where(lane < 64, roll(kept[2 * i], 64), kept[2 * i + 1])
            halo_back[at] = pair.astype(BF16)
        pass_slab(wz, "slab_back", halo_back, R.halo_back_in, right)

    def second(w, carry):
        wy, wz = lax.rem(w, 2), w // 2
        bars = (R.bars[...] + shift_bars(marks, wy, wz)).astype(BF16)
        x = take_window(R.grid, select, 1, wy, wz)
        window_norm(x, S, 4)
        windows[w] = window_forward(x, W, S, 4, marks, bars)
        grad = take_window(R.grid_two, select, 1, wy, wz)
        deltas[w] = window_backward(grad, W, S, 4, G, marks, bars)

        @pl.when(w == 1)
        def _():
            give_back(0)

        return carry

    lax.fori_loop(0, 4, second, 0)

    give_back(1)

    def put_tall(z, value):
        tall[C * z : C * z + C, :] = value

    for wz in range(2):
        give_grid(windows, select, 1, wz, put_tall)
    give_rows(tall, square)
    for x in range(7 - SHIFT):
        R.block_out[x + SHIFT] = square[16 * x : 16 * x + 14, 0 : SZ * C].astype(BF16)
    for x in range(SHIFT):
        at = 16 * (x + 7 - SHIFT)
        R.edge[x] = square[at : at + 14, 0 : SZ * C].astype(BF16)
    out_back = neighbour("out_back", R.edge, R.edge_back, right)

    padded = R.outgoing.shape[2]
    piece = padded // n_x

    def scatter(b):
        finish_gradients(G, flat, wide, spread, place, tiles)
        for f in range(n_fsdp):
            R.outgoing[b, f, 0:shard, :] = flat[shard * f : shard * f + shard, :].astype(BF16)
            if padded > shard:
                R.outgoing[b, f, shard:padded, :] = jnp.zeros((padded - shard, 128), BF16)
        start(near_copies(b))

    def rows_of(x):
        return pl.ds(pl.multiple_of(piece * x, 16), piece)

    own = rows_of(me_x)

    def near_copies(b):
        return [
            remote(
                ("near", b, k), R.outgoing.at[b, f, rows_of(x)], R.incoming.at[b, me_near], to
            )
            for k, f, x, to in near
        ]

    def far_copies(b):
        mine = R.parts.at[b, me_z]
        return [remote(("far", b, k), mine, mine, to) for k, to in far]

    def whole_copies(b):
        mine = R.whole.at[b, own]
        return [remote(("whole", b, k), mine, mine, to) for k, f, x, to in near if k < n_x]

    def norm_copies():
        mine = R.norms.at[me_near]
        return [remote(("norm", k), mine, mine, to) for k, f, x, to in near]

    def add_near(b):
        wait(near_copies(b))
        R.incoming[b, me_near] = R.outgoing[b, me_fsdp, own, :]
        total_rows = R.incoming[b, 0].astype(F32)
        for i in range(1, n_fsdp * n_x):
            total_rows += R.incoming[b, i].astype(F32)
        R.parts[b, me_z] = total_rows.astype(BF16)
        start(far_copies(b))

    def add_far(b):
        wait(far_copies(b))
        total_rows = R.parts[b, 0].astype(F32)
        for i in range(1, n_z):
            total_rows += R.parts[b, i].astype(F32)
        R.whole[b, own, :] = total_rows.astype(BF16)
        start(whole_copies(b))
        squares = jnp.sum((total_rows * total_rows).reshape(piece // 8, 8, 128), axis=0)
        if b == 1:
            R.norms[me_near] = squares
        else:
            R.norms[me_near] += squares
            start(norm_copies())

    scatter(1)
    wait_slab("slab_back", halo_back, R.halo_back_in, right)
    for z in range(SZ):
        pair = R.halo_back_in[(z // 2 + 5) % 7].astype(F32)
        if z % 2 == 1:
            pair = roll(pair, 64)
        joined = jnp.where(lane < 48, pair, roll(kept[z], 48))
        R.grid[:, 128 * z : 128 * z + 128] = joined.astype(BF16)
    for ref in vars(G).values():
        clear(ref)
    W0 = Names(**{**vars(W), **first_weights})

    def first_backward(w, carry):
        grad = take_window(R.grid, select, 0, lax.rem(w, 2), w // 2)
        deltas[w] = window_backward(grad, W0, S, w, G, marks, R.bars[...].astype(BF16))

        @pl.when(w == 1)
        def _():
            add_near(1)

        @pl.when(w == 2)
        def _():
            add_far(1)

        return carry

    lax.fori_loop(0, 4, first_backward, 0)
    scatter(0)
    for wz in range(2):
        give_grid(deltas, select, 0, wz, put_tall)
    give_rows(tall, square)
    for x in range(7):
        R.input_grad[x] = square[16 * x : 16 * x + 14, 0 : SZ * C].astype(BF16)
    flush("input_grad").start()
    wait(out_back)
    R.block_out[0:SHIFT] = R.edge_back[...]
    flush("block_out").start()
    add_near(0)
    fetch("first_moment").wait()
    fetch("second_moment").wait()
    for b in range(2):
        R.first_held[b] = BETA_FIRST * R.first_moment[b : b + 1, :].reshape(shard, 128)
        R.second_held[b] = BETA_SECOND * R.second_moment[b : b + 1, :].reshape(shard, 128)
    wait(whole_copies(1))
    add_far(0)
    wait(whole_copies(0))
    wait(norm_copies())
    norm = R.norms[0]
    for i in range(1, n_fsdp * n_x):
        norm += R.norms[i]
    norm = jnp.sum(jnp.sum(norm, axis=0, keepdims=True), axis=1, keepdims=True)
    norm = jnp.broadcast_to(jnp.sqrt(norm), (1, 128))
    R.grad_norm[0, 0] = norm[0, 0]
    factor = jnp.minimum(1.0, CLIP_LIMIT / (norm + 1e-06))[0:1]
    states = []
    for b in range(2):
        clipped = R.whole[b, 0:shard, :].astype(F32) * factor
        new_first = R.first_held[b] + (1.0 - BETA_FIRST) * clipped
        new_second = R.second_held[b] + (1.0 - BETA_SECOND) * clipped * clipped
        first_hat = new_first / (1.0 - BETA_FIRST**STEP)
        second_hat = new_second / (1.0 - BETA_SECOND**STEP)
        params = R.own[b]
        new_params = params - LEARN_RATE * (
            first_hat / (jnp.sqrt(second_hat) + EPS_ADAM) + WEIGHT_DECAY * params
        )
        states.append((new_first, new_second, new_params))

    def store(ref, at):
        for b in range(2):
            ref[b : b + 1, :] = states[b][at].reshape(1, shard * 128)

    store(R.new_first, 0)
    flush("new_first").start()
    store(R.new_second, 1)
    flush("new_second").start()
    store(R.new_params, 2)
    flush("new_params").start()
    R.params_copy[...] = R.new_params[...].astype(BF16)
    flush("params_copy").start()
    wait([flush(k) for k in RESULTS])


def deliver(*refs):
    count = (len(refs) - 1) // 3 + 1
    sources, targets, held, sems = refs[:count], refs[count : 2 * count], refs[2 * count : -1], refs[-1]
    moves = []
    for source, target in zip(sources, targets):
        if source.shape == (1, 1):
            target[0, 0] = source[0, 0]
            continue
        at = len(moves)
        into = pltpu.make_async_copy(source, held[at], sems.at[0, at])
        moves.append((into, pltpu.make_async_copy(held[at], target, sems.at[1, at])))
        into.start()
    for into, out in moves:
        into.wait()
        out.start()
    for into, out in moves:
        out.wait()


def per_device(n_win, n_fsdp, tokens, cotangent, crop_ids, params, first_moment, second_moment):
    ints, marks = constant_tables()
    extent = tokens.shape[1]
    shard = params.shape[1] // 128
    held = round_up(shard, 16)
    n_x = near_extent(n_win)
    n_near, n_z = n_fsdp * n_x, n_win // n_x
    piece = round_up(-(-shard // n_x), 16)
    padded = piece * n_x
    rows = jax.ShapeDtypeStruct(params.shape, F32)
    cells = jax.ShapeDtypeStruct((extent, SY, SZ * C), BF16)
    inputs = dict(
        tokens=tokens[0],
        cotangent=cotangent[0],
        crop=crop_ids,
        ints=ints,
        marks=marks,
        params=params,
        first_moment=first_moment,
        second_moment=second_moment,
    )
    outputs = dict(
        block_out=cells,
        input_grad=cells,
        grad_norm=jax.ShapeDtypeStruct((1, 1), F32),
        new_params=rows,
        new_first=rows,
        new_second=rows,
        params_copy=jax.ShapeDtypeStruct(params.shape, BF16),
    )
    V = pltpu.VMEM
    edge = V((SHIFT, SY, SZ * C), BF16)
    scratch = dict(
        own=V((2, shard, 128), F32),
        first_held=V((2, shard, 128), F32),
        second_held=V((2, shard, 128), F32),
        gathered=V((n_fsdp, 2, held, 128), BF16),
        edge=edge,
        edge_in=edge,
        edge_back=edge,
        halo=V((7, C, 128), BF16),
        halo_in=V((7, C, 128), BF16),
        halo_back=V((7, C, 128), BF16),
        halo_back_in=V((7, C, 128), BF16),
        outgoing=V((2, n_fsdp, padded, 128), BF16),
        incoming=V((2, n_near, piece, 128), BF16),
        parts=V((2, n_z, piece, 128), BF16),
        whole=V((2, padded, 128), BF16),
        norms=V((n_near, 8, 128), F32),
        select=V((2, 896, 2 * QLANE), BF16),
        place=V((896, QLANE), BF16),
        spread=V((176, 49 * 128), BF16),
        flat=V((FLAT + 8, 128), F32),
        wide=V((3, 384, 128), F32),
        tiles=V((80 * 56, 128), F32),
        square=V((128, 1408), F32),
        tall=V((1408, 128), F32),
        grid=V((C, 17 * 128), BF16),
        grid_two=V((C, 17 * 128), BF16),
        kept=V((SZ, C, 128), F32),
        windows=V((4, C, QLANE), F32),
        deltas=V((4, C, QLANE), F32),
        bars=V((32, QLANE), F32),
    )
    for k, (shape, kind) in WEIGHT_SHAPES.items():
        scratch["w_" + k] = V(shape, kind)
    for k in ("cols", "q_n", "kv_n", "proj_n", "one_n", "two_n"):
        scratch["k_" + k] = V(*WEIGHT_SHAPES[k])
    for k, (shape, kind) in SAVED_SHAPES.items():
        scratch["s_" + k] = V((5, *shape), kind)
    for k, (shape, kind) in GRAD_SHAPES.items():
        scratch["g_" + k] = V(shape, kind)
    copies = 2 * (n_fsdp - 1) + 3 * (n_near - 1) + 2 * (n_z - 1) + 2 * (n_x - 1) + 6
    for k in STAGED:
        scratch[k] = V(inputs[k].shape, inputs[k].dtype)
    for k in RESULTS:
        scratch[k] = V(outputs[k].shape, outputs[k].dtype)
    scratch["local"] = pltpu.SemaphoreType.DMA((len(STAGED) + len(RESULTS),))
    scratch["send"] = pltpu.SemaphoreType.DMA((copies,))
    scratch["recv"] = pltpu.SemaphoreType.DMA((copies,))
    outside = {k: "hbm_" + k if k in STAGED + RESULTS else k for k in [*inputs, *outputs]}
    names = [*outside.values(), *scratch]
    vmem = pl.BlockSpec(memory_space=pltpu.VMEM)
    hbm = pl.BlockSpec(memory_space=pltpu.HBM)
    smem = pl.BlockSpec(memory_space=pltpu.SMEM)
    results = pl.pallas_call(
        functools.partial(step_kernel, n_win, n_fsdp, names),
        out_shape=tuple(outputs.values()),
        in_specs=[smem if k == "crop" else hbm if k in STAGED else vmem for k in inputs],
        out_specs=tuple(smem if k == "grad_norm" else hbm for k in outputs),
        scratch_shapes=list(scratch.values()),
        compiler_params=pltpu.CompilerParams(
            collective_id=0 if n_win * n_fsdp > 1 else None,
            has_side_effects=True,
            vmem_limit_bytes=66 * 1024 * 1024 - 2 * 1024 * 1024,
        ),
        name="layer_step",
    )(*inputs.values())
    results = pl.pallas_call(
        deliver,
        out_shape=tuple(outputs.values()),
        in_specs=[smem if k == "grad_norm" else hbm for k in outputs],
        out_specs=tuple(smem if k == "grad_norm" else hbm for k in outputs),
        scratch_shapes=[
            *(V(outputs[k].shape, outputs[k].dtype) for k in RESULTS),
            pltpu.SemaphoreType.DMA((2, len(RESULTS))),
        ],
        name="deliver",
    )(*results)
    block_out, input_grad, grad_norm, *states = results
    return (block_out[None], input_grad[None], grad_norm[0, 0], *states)


def solution(mesh):
    data = P("fsdp", "win", None, None)
    state = P(None, "fsdp")
    return jax.shard_map(
        functools.partial(per_device, mesh.shape["win"], mesh.shape["fsdp"]),
        mesh=mesh,
        in_specs=(data, data, P("fsdp", None), state, state, state),
        out_specs=(data, data, P(), state, state, state, state),
        check_vma=False,
    )
```

```python
import functools
from types import SimpleNamespace as Names

import jax
import jax.numpy as jnp
import numpy as np
from jax import lax
from jax.experimental import pallas as pl
from jax.experimental.pallas import tpu as pltpu
from jax.sharding import PartitionSpec as P

C = 96
HEADS = 6
HEAD = 16
HID = 384
WS = 7
SHIFT = 3
SY = 14
SZ = 14
BPAD = 124928
STEP = 5
EPS_NORM = 1e-05
CLIP_LIMIT = 1.0
LEARN_RATE = 0.4
BETA_FIRST = 0.9
BETA_SECOND = 0.999
WEIGHT_DECAY = 0.05
EPS_ADAM = 1e-08
BIG = 1e30
LOG2E = 1.4426950408889634
LN2 = 0.6931471805599453

CELLS = WS**3
KROW = 352
QLANE = 384
FLAT = BPAD // 128
ROW_PROJ = 216
ROW_ONE = 288
ROW_TWO = 576
ROW_TABLE = 864
ROW_TAIL = 966
V_GAIN1, V_BIAS1, V_BQ, V_BV, V_BPROJ, V_GAIN2, V_BIAS2, V_BHID, V_BOUT = (
    0, 96, 192, 288, 384, 480, 576, 672, 1056,
)

F32 = jnp.float32
BF16 = jnp.bfloat16


def nn(a, b):
    return lax.dot_general(a, b, (((1,), (0,)), ((), ())), preferred_element_type=F32)


def nt(a, b):
    return lax.dot_general(a, b, (((1,), (1,)), ((), ())), preferred_element_type=F32)


def iota(shape, dim):
    return lax.broadcasted_iota(jnp.int32, shape, dim)


def roll(x, by):
    by = by % 128
    return x if by == 0 else pltpu.roll(x, by, 1)


def skew(x, by):
    while by > 0:
        some = min(1 << (by.bit_length() - 1), 16)
        x = pltpu.roll(x, 0, 1, stride=some, stride_axis=0)
        by -= some
    return x


def constant_tables():
    t = np.arange(QLANE)
    live = t < CELLS
    z, x, y = t // 49, t % 49 // 7, t % 7
    ints = np.full((8, QLANE), -1, np.int32)
    for s in range(2):
        for wy in range(2):
            cell_y = (y + 7 * wy + SHIFT * s) % SY
            ints[2 * s + wy] = np.where(live, z * 128 + x * 16 + cell_y, -1)
    ints[4] = np.where(live, z * 128 + t % 49, -1)
    ints[5] = np.where(live, x, -1)
    lane = np.arange(128)
    ints[6, :128] = np.where(lane < 49, 13 * (lane // 7) + lane % 7, -1000)
    marks = np.zeros((64, QLANE), np.float32)
    for i in range(7):
        marks[i] = live & (x == i)
        marks[7 + i] = live & (y == i)
        marks[14 + i] = live & (z == i)
        marks[32 + 7 + i] = live & ((i >= 4) != (y >= 4))
        marks[32 + 14 + i] = live & ((i >= 4) != (z >= 4))
    return jnp.asarray(ints), jnp.asarray(marks, BF16)


def unit_copy(pieces, units):
    out = None
    for at, unit in enumerate(units):
        if unit is None:
            continue
        i, g = unit
        moved = roll(pieces[i], 32 * (at - g))
        group = iota(moved.shape, 1) // 32
        base = jnp.zeros_like(moved) if out is None else out
        out = jnp.where(group == at, moved, base)
    return out


def read_matrix(flat, base, rows, width, store):
    units = width // 32
    if units % 4 == 0:
        step = units // 4
        for o in range(step):
            store(0, 1, o, flat[pl.ds(base + o, rows, stride=step), :])
        return
    groups = rows // 4
    loaded = [flat[pl.ds(base + o, groups, stride=units), :] for o in range(units)]
    for j in range(4):
        for p in range(units // 3):
            first = units * j + 3 * p
            store(j, 4, p, unit_copy(loaded, [divmod(first + s, 4) for s in range(3)] + [None]))


def write_matrix(flat, base, rows, width, load):
    units = width // 32
    if units % 4 == 0:
        step = units // 4
        for o in range(step):
            flat[pl.ds(base + o, rows, stride=step), :] = load(0, 1, o)
        return
    groups = rows // 4
    parts = units // 3
    loaded = [load(j, 4, p) for j in range(4) for p in range(parts)]
    for o in range(units):
        flat[pl.ds(base + o, groups, stride=units), :] = unit_copy(
            loaded, [divmod(4 * o + g, 3) for g in range(4)]
        )


def build_selectors(ints, select, place, spread):
    for s in range(2):
        for wy in range(2):
            need = ints[2 * s + wy : 2 * s + wy + 1, :]
            for r in range(7):
                row = iota((128, QLANE), 0) + 128 * r
                select[s, 128 * r : 128 * r + 128, QLANE * wy : QLANE * wy + QLANE] = jnp.where(
                    row == need, 1.0, 0.0
                ).astype(BF16)
    need = ints[4:5, :]
    for r in range(7):
        row = iota((128, QLANE), 0) + 128 * r
        place[128 * r : 128 * r + 128, :] = jnp.where(row == need, 1.0, 0.0).astype(BF16)
    gap = iota((176, 128), 0) - ints[6:7, :128]
    for k in range(49):
        hit = gap == 84 - 13 * (k // 7) - k % 7
        spread[:, 128 * k : 128 * k + 128] = jnp.where(hit, 1.0, 0.0).astype(BF16)


def table_pick(second):
    row = iota((176, 104), 0)
    col = iota((176, 104), 1) - second
    at = 128 * col
    start = 78 * row
    hit = (start >= at) & (start < at + 128) & (row < 169)
    return jnp.where(hit, 1.0, 0.0).astype(BF16)


def table_start():
    row = iota((176, 128), 0)
    return jnp.bitwise_and(78 * row, 127)


def build_table(flat, spread, place, tiles, table):
    rows = flat[ROW_TABLE : ROW_TABLE + 104, :].astype(BF16)
    first = skew(nn(table_pick(0), rows), 50)
    second = skew(nn(table_pick(1), rows), 50)
    lane = iota((176, 128), 1)
    mixed = jnp.where(lane + table_start() < 128, first, second)
    mixed = jnp.where((lane < 78) & (iota((176, 128), 0) < 169), mixed, 0.0)
    turned = jnp.concatenate([mixed, jnp.zeros((80, 128), F32)], axis=0).T
    cube = turned[:80, :176].astype(BF16)
    for k in range(0, 49, 2):
        some = min(2, 49 - k)
        block = nn(cube, spread[:, 128 * k : 128 * k + 128 * some])
        for i in range(some):
            tiles[pl.ds(k + i, 80, stride=56), :] = block[:, 128 * i : 128 * i + 128]

    def gathered(ck, first, last):
        return jnp.concatenate(
            [
                tiles[336 * (cq - ck + 6) : 336 * (cq - ck + 7), :].astype(BF16)
                for cq in range(first, last)
            ],
            axis=1,
        )

    for ck in range(7):
        block = jnp.concatenate(
            [
                nn(gathered(ck, 0, 6), place[0:768, 0:256]),
                nn(gathered(ck, 5, 7), place[640:896, 256:QLANE]),
            ],
            axis=1,
        )
        block = block * LOG2E
        for h in range(HEADS):
            table[h, 49 * ck : 49 * ck + 49, :] = block[56 * h : 56 * h + 49, :]
    for h in range(HEADS):
        table[h, CELLS:KROW, :] = jnp.full((KROW - CELLS, QLANE), -BIG, F32)


def collapse_table(total, wide_total, spread, place, tiles, flat):
    tiles[...] = jnp.zeros(tiles.shape, F32)
    for h in range(HEADS):
        wide_total[h] = total[h].astype(F32)
    for ck in range(7):
        lhs = jnp.concatenate(
            [wide_total[h, 49 * ck : 49 * ck + 56, :] for h in range(HEADS)], axis=0
        ).astype(BF16)
        for cq, start, end in ((0, 0, 128), (2, 0, 256), (4, 128, 384), (6, 256, 384)):
            some = min(2, 7 - cq)
            block = nt(lhs[:, start:end], place[128 * cq : 128 * cq + 128 * some, start:end])
            for i in range(some):
                dc = cq + i - ck + 6
                tiles[336 * dc : 336 * dc + 336, :] += block[:, 128 * i : 128 * i + 128]
    lhs = jnp.concatenate(
        [tiles[pl.ds(k, 80, stride=56), :].astype(BF16) for k in range(49)], axis=1
    )
    cube = nt(lhs, spread[...])
    wide = jnp.concatenate([cube, jnp.zeros((80, 80), F32)], axis=1)
    wide = jnp.concatenate([wide, jnp.zeros((48, 256), F32)], axis=0)
    mixed = wide.T[:176, :]
    mixed = skew(mixed, 78)
    fits = iota((176, 128), 1) >= table_start()
    lane = iota((176, 128), 1)
    length = jnp.bitwise_and(lane - table_start(), 127)
    live = (length < 78) & (iota((176, 128), 0) < 169)
    head = jnp.where(fits & live, mixed, 0.0).astype(BF16)
    rest = jnp.where(jnp.logical_not(fits) & live, mixed, 0.0).astype(BF16)

    def tn(a, b):
        return lax.dot_general(a, b, (((0,), (0,)), ((), ())), preferred_element_type=F32)

    return tn(table_pick(0), head) + tn(table_pick(1), rest)


def tail_vector(tail, start, width):
    o, at = divmod(start, 128)
    lane = iota((1, 128), 1)
    out = roll(tail[o : o + 1, :], -at)
    if at + width > 128:
        out = jnp.where(lane < 128 - at, out, roll(tail[o + 1 : o + 2, :], -at))
    return jnp.where(lane < width, out, 0.0)


def prepare(flat, W, wide, spread, place, tiles):
    rows = flat[ROW_TAIL : ROW_TAIL + 16, :]
    lane = iota((9, 128), 1)
    tail = jnp.where(lane < 2, roll(rows[:9], 2), roll(rows[1:10], 2))
    turned = jnp.concatenate([tail, jnp.zeros((119, 128), F32)], axis=0).T
    for o in range(9):
        W.cols[128 * o : 128 * o + 128, :] = jnp.broadcast_to(turned[:, o : o + 1], (128, 128))

    def into(j, step, p, value):
        wide[p, pl.ds(j, value.shape[0], stride=step), :] = value

    def finish(p, bias):
        wide[p, 96:97, :] = bias
        wide[p, 97:128, :] = jnp.zeros((31, 128), F32)

    read_matrix(flat, 0, C, 3 * C, into)
    finish(0, tail_vector(tail, V_BQ, C))
    finish(1, jnp.zeros((1, 128), F32))
    finish(2, tail_vector(tail, V_BV, C))
    W.q_n[...] = wide[0, 0:96, :].astype(BF16)
    for p in range(1, 3):
        W.kv_n[:, 128 * p - 128 : 128 * p] = wide[p, 0:96, :].astype(BF16)
    for p in range(3):
        W.qkv_t[96 * p : 96 * p + 96, :] = wide[p, 0:128, :].T[:96].astype(BF16)

    read_matrix(flat, ROW_PROJ, C, C, into)
    finish(0, tail_vector(tail, V_BPROJ, C))
    W.proj_n[...] = wide[0, 0:96, :].astype(BF16)
    W.proj_t[...] = wide[0, 0:128, :].T[:96].astype(BF16)

    read_matrix(flat, ROW_ONE, C, HID, into)
    for p in range(3):
        finish(p, tail_vector(tail, V_BHID + 128 * p, 128))
        W.one_n[:, 128 * p : 128 * p + 128] = wide[p, 0:96, :].astype(BF16)
        W.one_t[128 * p : 128 * p + 128, :] = wide[p, 0:128, :].T.astype(BF16)

    read_matrix(flat, ROW_TWO, HID, C, into)
    W.two_n[...] = wide[0].astype(BF16)
    for p in range(3):
        W.two_t[:, 128 * p : 128 * p + 128] = wide[0, 128 * p : 128 * p + 128, :].T[:96].astype(
            BF16
        )
    build_table(flat, spread, place, tiles, W.table)


WEIGHT_SHAPES = dict(
    cols=((1152, 128), F32),
    q_n=((96, 128), BF16),
    kv_n=((96, 256), BF16),
    qkv_t=((288, 128), BF16),
    proj_n=((96, 128), BF16),
    proj_t=((96, 128), BF16),
    one_n=((96, 384), BF16),
    one_t=((384, 128), BF16),
    two_n=((384, 128), BF16),
    two_t=((96, 384), BF16),
    table=((HEADS, KROW, QLANE), F32),
)


SAVED_SHAPES = dict(
    normed=((128, QLANE), BF16),
    hat=((96, QLANE), F32),
    scale=((8, QLANE), F32),
    qkv=((288, QLANE), BF16),
    probs=((HEADS, KROW, QLANE), BF16),
    inverse=((8, QLANE), F32),
    attended=((128, QLANE), BF16),
    hat_two=((96, QLANE), F32),
    scale_two=((8, QLANE), F32),
    normed_two=((128, QLANE), BF16),
    slope=((HID, QLANE), BF16),
    active=((HID, QLANE), BF16),
)

GRAD_SHAPES = dict(
    q=((112, 128), F32),
    kv=((2, 112, 128), F32),
    proj=((112, 128), F32),
    one=((112, 384), F32),
    two=((400, 128), F32),
    gain1=((96, 128), F32),
    bias1=((96, 128), F32),
    gain2=((96, 128), F32),
    bias2=((96, 128), F32),
    total=((HEADS, KROW, QLANE), BF16),
)


def column(W, start, rows=96):
    part = W.cols[start : start + rows, :]
    return jnp.concatenate([part, part, part], axis=1)


def extended(rows):
    width = rows.shape[1]
    return jnp.concatenate([rows, jnp.ones((16, width), BF16), jnp.zeros((16, width), BF16)], axis=0)


def standardize(x):
    centered = x - jnp.mean(x, axis=0, keepdims=True)
    variance = jnp.mean(centered * centered, axis=0, keepdims=True)
    scale = lax.rsqrt(variance + EPS_NORM)
    return centered * scale, scale


def at_head(h, rows, tail):
    width = rows.shape[1]
    parts = []
    if h > 0:
        parts.append(jnp.zeros((16 * h, width), BF16))
    parts.append(rows)
    if h < HEADS - 1:
        parts.append(jnp.zeros((16 * (HEADS - 1 - h), width), BF16))
    return jnp.concatenate(parts + [tail], axis=0)


def scaled_queries(qkv):
    return (qkv[0:96].astype(F32) * (HEAD**-0.5 * LOG2E)).astype(BF16)


def window_norm(x, S, s):
    hat, scale = standardize(x)
    S.hat[s] = hat
    S.scale[s, 0:1] = scale


def window_forward(x, W, S, s, marks, barred):
    hat = S.hat[s]
    normed = extended((hat * column(W, V_GAIN1) + column(W, V_BIAS1)).astype(BF16))
    S.normed[s] = normed
    qkv = nn(W.qkv_t[...], normed).astype(BF16)
    S.qkv[s] = qkv
    queries = scaled_queries(qkv)
    keys = jnp.concatenate([qkv[96:192], marks[0:32, :]], axis=0).T[:KROW]
    ones = jnp.ones((16, KROW), BF16)

    def pair_scores(p):
        sides = [at_head(h, queries[16 * h : 16 * h + 16], barred) for h in (2 * p, 2 * p + 1)]
        return nn(keys, jnp.concatenate(sides, axis=1))

    parts = []
    coming = pair_scores(0)
    for h in range(HEADS):
        if h % 2 == 0:
            pair = coming
            if h + 2 < HEADS:
                coming = pair_scores(h // 2 + 1)
        scores = pair[:, QLANE * (h % 2) : QLANE * (h % 2) + QLANE] + W.table[h]
        highest = jnp.max(scores, axis=0, keepdims=True)
        probs = jnp.exp2(scores - highest).astype(BF16)
        S.probs[s, h] = probs
        values = jnp.concatenate([qkv[192 + 16 * h : 208 + 16 * h, :KROW], ones], axis=0)
        mixed = nn(values, probs)
        inverse = 1.0 / mixed[16:17]
        S.inverse[s, h : h + 1] = inverse
        parts.append((mixed[:16] * inverse).astype(BF16))
    attended = extended(jnp.concatenate(parts, axis=0))
    S.attended[s] = attended
    branch = nn(W.proj_t[...], attended).astype(BF16)
    middle = x + branch.astype(F32)
    hat, scale = standardize(middle)
    S.hat_two[s] = hat
    S.scale_two[s, 0:1] = scale
    normed_two = extended((hat * column(W, V_GAIN2) + column(W, V_BIAS2)).astype(BF16))
    S.normed_two[s] = normed_two
    hidden = nn(W.one_t[...], normed_two)
    share = 0.5 + 0.5 * lax.erf(hidden * (0.5**0.5))
    active = (hidden * share).astype(BF16)
    S.active[s] = active
    slope = share + hidden * jnp.exp2(hidden * hidden * (-0.5 * LOG2E)) * 0.3989422804014327
    S.slope[s] = slope.astype(BF16)
    return middle + nn(W.two_t[...], active) + column(W, V_BOUT)


def fold(x):
    return x[:, 0:128] + x[:, 128:256] + x[:, 256:384]


def norm_backward(grad, hat, scale, gain):
    scaled = grad * gain
    mean_one = jnp.mean(scaled, axis=0, keepdims=True)
    mean_two = jnp.mean(scaled * hat, axis=0, keepdims=True)
    return scale * (scaled - mean_one - hat * mean_two)


def window_backward(grad, W, S, s, G, marks, barred):
    result = extended(grad.astype(BF16))
    active = S.active[s]
    G.two[...] += nt(jnp.concatenate([active, jnp.ones((16, QLANE), BF16)], axis=0), result)
    hidden = (nn(W.two_n[...], result) * S.slope[s].astype(F32)).astype(BF16)
    G.one[...] += nt(S.normed_two[s, 0:112], hidden)
    d_normed = nn(W.one_n[...], hidden)
    hat = S.hat_two[s]
    G.gain2[...] += fold(d_normed * hat)
    G.bias2[...] += fold(d_normed)
    d_middle = grad + norm_backward(d_normed, hat, S.scale_two[s, 0:1], column(W, V_GAIN2))
    d_branch = extended(d_middle.astype(BF16))
    attended = S.attended[s]
    G.proj[...] += nt(attended[0:112], d_branch)
    d_attended = nn(W.proj_n[...], d_branch).astype(BF16).astype(F32)
    product = d_attended * attended[0:96].astype(F32)
    qkv = S.qkv[s]
    queries = scaled_queries(qkv)
    values = extended(qkv[192:288]).T[:KROW]
    row = iota((32, QLANE), 0)
    parts, d_keys, d_values = [], [], []

    def head_gradient(h):
        inverse = S.inverse[s, h : h + 1]
        inner = jnp.sum(product[16 * h : 16 * h + 16], axis=0, keepdims=True) * inverse
        high = inner.astype(BF16)
        low = (inner - high.astype(F32)).astype(BF16)
        less = jnp.where(row == 0, -high.astype(F32), jnp.where(row == 1, -low.astype(F32), 0.0))
        rows = (d_attended[16 * h : 16 * h + 16] * inverse).astype(BF16)
        return rows, at_head(h, rows, less.astype(BF16))

    def pair_gradient(p):
        d_outs = [head_gradient(h) for h in (2 * p, 2 * p + 1)]
        product = nn(values, jnp.concatenate([d_out for _, d_out in d_outs], axis=1))
        return d_outs, product.astype(BF16)

    def head_products(h, d_scores, rows, probs):
        d_keys.append(nt(queries[16 * h : 16 * h + 16], d_scores))
        d_values.append(nt(rows, probs))
        parts.append(nn(qkv[96 + 16 * h : 112 + 16 * h, :KROW], d_scores))

    late = []
    coming = pair_gradient(0)
    for p in range(HEADS // 2):
        d_outs, d_pair = coming
        if p + 1 < HEADS // 2:
            coming = pair_gradient(p + 1)
        for h in (2 * p, 2 * p + 1):
            probs = S.probs[s, h]
            d_scores = probs * d_pair[:, QLANE * (h % 2) : QLANE * (h % 2) + QLANE]
            G.total[h] += d_scores
            late.append((h, d_scores, d_outs[h % 2][0], probs))
            if len(late) > 6:
                head_products(*late.pop(0))
    for held in late:
        head_products(*held)
    d_queries = (jnp.concatenate(parts, axis=0) * HEAD**-0.5).astype(BF16)
    gap = jnp.zeros((32, QLANE), BF16)
    tokens_gap = jnp.zeros((96, QLANE - KROW), F32)

    def side(rows, factor):
        rows = jnp.concatenate(rows, axis=0) * factor
        return jnp.concatenate([rows, tokens_gap], axis=1).astype(BF16)

    d_pair = jnp.concatenate([side(d_keys, LN2), gap, side(d_values, 1.0), gap], axis=0)
    normed = S.normed[s, 0:112]
    G.q[:, 0:96] += nt(normed, d_queries)
    both = nt(normed, d_pair)
    for p in range(2):
        G.kv[p] += both[:, 128 * p : 128 * p + 128]
    d_normed = nn(W.q_n[:, 0:96], d_queries) + nn(W.kv_n[...], d_pair)
    hat = S.hat[s]
    G.gain1[...] += fold(d_normed * hat)
    G.bias1[...] += fold(d_normed)
    return d_middle + norm_backward(d_normed, hat, S.scale[s, 0:1], column(W, V_GAIN1))


def finish_gradients(G, wide_total, flat, wide, spread, place, tiles):
    def qkv_rows(j, step, p):
        if p == 0:
            return G.q[pl.ds(j, 24, stride=4), :]
        return G.kv[p - 1, pl.ds(j, 24, stride=4), :]

    write_matrix(flat, 0, C, 3 * C, qkv_rows)
    write_matrix(flat, ROW_PROJ, C, C, lambda j, step, p: G.proj[pl.ds(j, 24, stride=4), :])
    write_matrix(
        flat, ROW_ONE, C, HID, lambda j, step, p: G.one[0:96, 128 * p : 128 * p + 128]
    )
    write_matrix(flat, ROW_TWO, HID, C, lambda j, step, p: G.two[pl.ds(j, 96, stride=4), :])
    lane = iota((96, 128), 1)
    columns = jnp.zeros((96, 128), F32)
    for at, ref in enumerate([G.gain1, G.bias1, G.gain2, G.bias2]):
        columns = jnp.where(lane == at, jnp.sum(ref[...], axis=1, keepdims=True), columns)
    turned = jnp.concatenate([columns, jnp.zeros((32, 128), F32)], axis=0).T
    sources = [
        (turned[0:1], 3),
        (turned[1:2], 3),
        (G.q[96:97, :], 3),
        (G.kv[1, 96:97, :], 3),
        (G.proj[96:97, :], 3),
        (turned[2:3], 3),
        (turned[3:4], 3),
        (G.one[96:97, 0:128], 4),
        (G.one[96:97, 128:256], 4),
        (G.one[96:97, 256:384], 4),
        (G.two[384:385, :], 3),
    ]
    pieces = [source for source, _ in sources]
    units = [(i, g) for i, (_, count) in enumerate(sources) for g in range(count)]
    tail = jnp.concatenate(
        [unit_copy(pieces, units[4 * o : 4 * o + 4]) for o in range(9)], axis=0
    )
    table = collapse_table(G.total, wide_total, spread, place, tiles, flat)
    flat[ROW_TABLE:ROW_TAIL, :] = table[0:102]
    none = jnp.zeros((1, 128), F32)
    moved = roll(jnp.concatenate([none, tail, none], axis=0), 126)
    lane = iota((10, 128), 1)
    mixed = jnp.where(lane >= 126, moved[1:11], moved[0:10])
    first = jnp.where(iota((1, 128), 1) >= 126, mixed[0:1], table[102:103])
    flat[ROW_TAIL:FLAT, :] = jnp.concatenate([first, mixed[1:10]], axis=0)


def round_up(value, to):
    return -(-value // to) * to


def take_grid(row_of, square, tall, grid, wrapped):
    for x in range(7):
        square[16 * x : 16 * x + 14, 0 : SZ * C] = row_of(x)
    for i in range(11):
        tall[128 * i : 128 * i + 128, :] = square[:, 128 * i : 128 * i + 128].T
    for z in range(SZ + 3 if wrapped else SZ):
        grid[:, 128 * z : 128 * z + 128] = tall[C * (z % SZ) : C * (z % SZ) + C, :].astype(BF16)


def take_window(grid, select, s, wy, wz):
    rows = grid[:, pl.ds(pl.multiple_of(896 * wz + 384 * s, 128), 896)]
    return nn(rows, select[s, :, pl.ds(pl.multiple_of(QLANE * wy, 128), QLANE)])


def give_grid(windows, select, s, wz, put):
    both = jnp.concatenate([windows[2 * wz], windows[2 * wz + 1]], axis=1).astype(BF16)
    cells = nt(both, select[s])
    for r in range(7):
        put((r + 7 * wz + SHIFT * s) % SZ, cells[:, 128 * r : 128 * r + 128])


def give_rows(tall, square):
    for i in range(11):
        square[:, 128 * i : 128 * i + 128] = tall[128 * i : 128 * i + 128, :].T


def crop_bars(crop, ints, first, total):
    ids = [crop[0, lax.rem(first + a, total)] for a in range(7)]
    at = ints[5:6, :]
    own = jnp.zeros((1, QLANE), jnp.int32)
    for a in range(7):
        own = jnp.where(at == a, ids[a], own)
    row = iota((32, QLANE), 0)
    key = jnp.full((32, QLANE), -1, jnp.int32)
    for a in range(7):
        key = jnp.where(row == a, ids[a], key)
    return jnp.where((row < 7) & (key != own), -BIG, 0.0)


def shift_bars(marks, wy, wz):
    row = iota((32, QLANE), 0)
    factor = jnp.where(row < 14, wy, wz).astype(F32) * -BIG
    return marks[32:64, :].astype(F32) * factor


STAGED = ("params", "tokens", "cotangent", "first_moment", "second_moment")
RESULTS = (
    "block_out", "input_grad", "new_params", "new_first", "new_second", "params_copy",
)


def near_extent(n_win):
    n_x = 1
    while 4 * n_x * n_x <= n_win:
        n_x *= 2
    return n_x


def step_kernel(n_win, n_fsdp, names, *refs):
    held = dict(zip(names, refs))
    R = Names(**held)
    W = Names(**{k: held["w_" + k] for k in WEIGHT_SHAPES})
    S = Names(**{k: held["s_" + k] for k in SAVED_SHAPES})
    G = Names(**{k: held["g_" + k] for k in GRAD_SHAPES})
    tokens, cotangent, crop = R.tokens, R.cotangent, R.crop
    ints, marks = R.ints, R.marks
    select, place, spread = R.select, R.place, R.spread
    flat, wide, tiles = R.flat, R.wide, R.tiles
    square, tall = R.square, R.tall
    send, recv = R.send, R.recv
    shard = FLAT // n_fsdp
    extent = tokens.shape[0]
    total = n_win * extent
    me_win, me_fsdp = lax.axis_index("win"), lax.axis_index("fsdp")
    left, right = lax.rem(me_win + n_win - 1, n_win), lax.rem(me_win + 1, n_win)
    n_x = near_extent(n_win)
    n_z = n_win // n_x
    me_x, me_z = lax.rem(me_win, n_x), me_win // n_x
    me_near = me_fsdp * n_x + me_x
    near = []
    for k in range(1, n_fsdp * n_x):
        f, x = lax.rem(me_fsdp + k // n_x, n_fsdp), lax.rem(me_x + k % n_x, n_x)
        near.append((k, f, x, {"win": me_z * n_x + x, "fsdp": f}))
    far = [(k, {"win": lax.rem(me_z + k, n_z) * n_x + me_x}) for k in range(1, n_z)]
    sides = [{"win": left}, {"win": right}] if n_win > 1 else []
    slots = {}

    def remote(name, src, dst, to):
        slot = slots.setdefault(name, len(slots))
        return pltpu.make_async_remote_copy(
            src_ref=src,
            dst_ref=dst,
            send_sem=send.at[slot],
            recv_sem=recv.at[slot],
            device_id=to,
            device_id_type=pl.DeviceIdType.MESH,
        )

    def start(copies):
        for copy in copies:
            copy.start()
        return copies

    def neighbour(name, src, dst, to):
        if n_win > 1:
            return start([remote(name, src, dst, {"win": to})])
        dst[...] = src[...]
        return []

    def fetch(k):
        at = STAGED.index(k)
        return pltpu.make_async_copy(held["hbm_" + k], held[k], R.local.at[at])

    def flush(k):
        at = len(STAGED) + RESULTS.index(k)
        return pltpu.make_async_copy(held[k], held["hbm_" + k], R.local.at[at])

    def wait(copies):
        for copy in copies:
            copy.wait()

    start([fetch(k) for k in STAGED])
    if n_win * n_fsdp > 1:
        barrier = pltpu.get_barrier_semaphore()
        peers = [peer[-1] for peer in near + far] + sides
        for peer in peers:
            pl.semaphore_signal(
                barrier, inc=1, device_id=peer, device_id_type=pl.DeviceIdType.MESH
            )
    gathered = R.gathered
    fetch("params").wait()
    for b in range(2):
        R.own[b] = R.params[b : b + 1, :].reshape(shard, 128)
        gathered[me_fsdp, b, 0:shard, :] = R.own[b].astype(BF16)
    fetch("cotangent").wait()
    R.edge[...] = cotangent[0:SHIFT]
    build_selectors(ints, select, place, spread)
    square[...] = jnp.zeros(square.shape, F32)
    fetch("tokens").wait()
    take_grid(lambda x: tokens[x].astype(F32), square, tall, R.grid, False)
    windows, deltas = R.windows, R.deltas

    def first_window(w, carry):
        x = take_window(R.grid, select, 0, lax.rem(w, 2), w // 2)
        windows[w] = x
        window_norm(x, S, w)
        return carry

    lax.fori_loop(0, 4, first_window, 0)
    if n_win * n_fsdp > 1:
        pl.semaphore_wait(barrier, len(peers))

    weights_in = []
    for b in range(2):
        mine = gathered.at[me_fsdp, b]
        copies = []
        for k in range(1, n_fsdp):
            to = {"fsdp": lax.rem(me_fsdp + k, n_fsdp)}
            copies.append(remote(("weights", b, k), mine, mine, to))
        weights_in.append(start(copies))
    halo_in = neighbour("halo", R.edge, R.edge_in, left)

    def clear(ref):
        ref[...] = jnp.zeros(ref.shape, ref.dtype)

    for ref in vars(G).values():
        clear(ref)
    wait(halo_in)

    def shifted_cotangent(x):
        return (cotangent[x + SHIFT] if x < 7 - SHIFT else R.edge_in[x - 7 + SHIFT]).astype(F32)

    take_grid(shifted_cotangent, square, tall, R.grid_two, True)

    def spread_weights(b):
        wait(weights_in[b])
        for f in range(n_fsdp):
            flat[shard * f : shard * f + shard, :] = gathered[f, b, 0:shard, :].astype(F32)
        prepare(flat, W, wide, spread, place, tiles)

    spread_weights(0)
    R.bars[...] = crop_bars(crop, ints, me_win * extent, total)

    halo, halo_back = R.halo, R.halo_back
    kept = R.kept
    lane = iota((C, 128), 1)
    slab_parts = [(0, 3), (3, 7)]

    def slab_copy(wz, name, src, dst, to):
        begin, end = slab_parts[wz]
        part = pl.ds(begin, end - begin)
        return remote((name, wz), src.at[part], dst.at[part], {"win": to})

    def pass_slab(wz, name, src, dst, to):
        if n_win > 1:
            start([slab_copy(wz, name, src, dst, to)])
        else:
            begin, end = slab_parts[wz]
            dst[begin:end] = src[begin:end]

    def wait_slab(name, src, dst, to):
        if n_win > 1:
            wait([slab_copy(wz, name, src, dst, to) for wz in range(2)])

    def put_kept(z, value):
        kept[z] = value

    def give_slices(wz):
        give_grid(windows, select, 0, wz, put_kept)
        for i in range(*slab_parts[wz]):
            pair = jnp.where(lane < 64, kept[2 * i], roll(kept[2 * i + 1], 64))
            halo[i] = pair.astype(BF16)
        pass_slab(wz, "slab", halo, R.halo_in, left)

    def first_forward(w, carry):
        windows[w] = window_forward(windows[w], W, S, w, marks, R.bars[...].astype(BF16))

        @pl.when(w == 1)
        def _():
            give_slices(0)

        return carry

    lax.fori_loop(0, 4, first_forward, 0)

    give_slices(1)
    first_weights = {}
    for k in ("cols", "q_n", "kv_n", "proj_n", "one_n", "two_n"):
        held["k_" + k][...] = held["w_" + k][...]
        first_weights[k] = held["k_" + k]
    spread_weights(1)
    wait_slab("slab", halo, R.halo_in, left)
    for z in range(SZ + 3):
        pair = R.halo_in[z % SZ // 2].astype(F32)
        if z % SZ % 2 == 0:
            pair = roll(pair, 64)
        joined = jnp.where(lane < 64, roll(kept[z % SZ], -48), pair)
        R.grid[:, 128 * z : 128 * z + 128] = joined.astype(BF16)

    R.bars[...] = crop_bars(crop, ints, me_win * extent + SHIFT, total)

    def give_back(wz):
        give_grid(deltas, select, 1, wz, put_kept)
        for at in range(*slab_parts[wz]):
            i = (at + 2) % 7
            pair = jnp.where(lane < 64, roll(kept[2 * i], 64), kept[2 * i + 1])
            halo_back[at] = pair.astype(BF16)
        pass_slab(wz, "slab_back", halo_back, R.halo_back_in, right)

    def second(w, carry):
        wy, wz = lax.rem(w, 2), w // 2
        bars = (R.bars[...] + shift_bars(marks, wy, wz)).astype(BF16)
        x = take_window(R.grid, select, 1, wy, wz)
        window_norm(x, S, 4)
        windows[w] = window_forward(x, W, S, 4, marks, bars)
        grad = take_window(R.grid_two, select, 1, wy, wz)
        deltas[w] = window_backward(grad, W, S, 4, G, marks, bars)

        @pl.when(w == 1)
        def _():
            give_back(0)

        return carry

    lax.fori_loop(0, 4, second, 0)

    give_back(1)

    def put_tall(z, value):
        tall[C * z : C * z + C, :] = value

    for wz in range(2):
        give_grid(windows, select, 1, wz, put_tall)
    give_rows(tall, square)
    for x in range(7 - SHIFT):
        R.block_out[x + SHIFT] = square[16 * x : 16 * x + 14, 0 : SZ * C].astype(BF16)
    for x in range(SHIFT):
        at = 16 * (x + 7 - SHIFT)
        R.edge[x] = square[at : at + 14, 0 : SZ * C].astype(BF16)
    out_back = neighbour("out_back", R.edge, R.edge_back, right)

    padded = R.outgoing.shape[2]
    piece = padded // n_x

    def scatter(b):
        finish_gradients(G, R.wide_total, flat, wide, spread, place, tiles)
        for f in range(n_fsdp):
            R.outgoing[b, f, 0:shard, :] = flat[shard * f : shard * f + shard, :].astype(BF16)
            if padded > shard:
                R.outgoing[b, f, shard:padded, :] = jnp.zeros((padded - shard, 128), BF16)
        start(near_copies(b))

    def rows_of(x):
        return pl.ds(pl.multiple_of(piece * x, 16), piece)

    own = rows_of(me_x)

    def near_copies(b):
        return [
            remote(
                ("near", b, k), R.outgoing.at[b, f, rows_of(x)], R.incoming.at[b, me_near], to
            )
            for k, f, x, to in near
        ]

    def far_copies(b):
        mine = R.parts.at[b, me_z]
        return [remote(("far", b, k), mine, mine, to) for k, to in far]

    def whole_copies(b):
        mine = R.whole.at[b, own]
        return [remote(("whole", b, k), mine, mine, to) for k, f, x, to in near if k < n_x]

    def norm_copies():
        mine = R.norms.at[me_near]
        return [remote(("norm", k), mine, mine, to) for k, f, x, to in near]

    def add_near(b):
        wait(near_copies(b))
        R.incoming[b, me_near] = R.outgoing[b, me_fsdp, own, :]
        total_rows = R.incoming[b, 0].astype(F32)
        for i in range(1, n_fsdp * n_x):
            total_rows += R.incoming[b, i].astype(F32)
        R.parts[b, me_z] = total_rows.astype(BF16)
        start(far_copies(b))

    def add_far(b):
        wait(far_copies(b))
        total_rows = R.parts[b, 0].astype(F32)
        for i in range(1, n_z):
            total_rows += R.parts[b, i].astype(F32)
        R.whole[b, own, :] = total_rows.astype(BF16)
        start(whole_copies(b))
        squares = jnp.sum((total_rows * total_rows).reshape(piece // 8, 8, 128), axis=0)
        if b == 1:
            R.norms[me_near] = squares
        else:
            R.norms[me_near] += squares
            start(norm_copies())

    scatter(1)
    wait_slab("slab_back", halo_back, R.halo_back_in, right)
    for z in range(SZ):
        pair = R.halo_back_in[(z // 2 + 5) % 7].astype(F32)
        if z % 2 == 1:
            pair = roll(pair, 64)
        joined = jnp.where(lane < 48, pair, roll(kept[z], 48))
        R.grid[:, 128 * z : 128 * z + 128] = joined.astype(BF16)
    for ref in vars(G).values():
        clear(ref)
    W0 = Names(**{**vars(W), **first_weights})

    def first_backward(w, carry):
        grad = take_window(R.grid, select, 0, lax.rem(w, 2), w // 2)
        deltas[w] = window_backward(grad, W0, S, w, G, marks, R.bars[...].astype(BF16))

        @pl.when(w == 1)
        def _():
            add_near(1)

        @pl.when(w == 2)
        def _():
            add_far(1)

        return carry

    lax.fori_loop(0, 4, first_backward, 0)
    scatter(0)
    for wz in range(2):
        give_grid(deltas, select, 0, wz, put_tall)
    give_rows(tall, square)
    for x in range(7):
        R.input_grad[x] = square[16 * x : 16 * x + 14, 0 : SZ * C].astype(BF16)
    flush("input_grad").start()
    wait(out_back)
    R.block_out[0:SHIFT] = R.edge_back[...]
    flush("block_out").start()
    add_near(0)
    fetch("first_moment").wait()
    fetch("second_moment").wait()
    for b in range(2):
        R.first_held[b] = BETA_FIRST * R.first_moment[b : b + 1, :].reshape(shard, 128)
        R.second_held[b] = BETA_SECOND * R.second_moment[b : b + 1, :].reshape(shard, 128)
    wait(whole_copies(1))
    add_far(0)
    wait(whole_copies(0))
    wait(norm_copies())
    norm = R.norms[0]
    for i in range(1, n_fsdp * n_x):
        norm += R.norms[i]
    norm = jnp.sum(jnp.sum(norm, axis=0, keepdims=True), axis=1, keepdims=True)
    norm = jnp.broadcast_to(jnp.sqrt(norm), (1, 128))
    R.grad_norm[0, 0] = norm[0, 0]
    factor = jnp.minimum(1.0, CLIP_LIMIT / (norm + 1e-06))[0:1]
    states = []
    for b in range(2):
        clipped = R.whole[b, 0:shard, :].astype(F32) * factor
        new_first = R.first_held[b] + (1.0 - BETA_FIRST) * clipped
        new_second = R.second_held[b] + (1.0 - BETA_SECOND) * clipped * clipped
        first_hat = new_first / (1.0 - BETA_FIRST**STEP)
        second_hat = new_second / (1.0 - BETA_SECOND**STEP)
        params = R.own[b]
        new_params = params - LEARN_RATE * (
            first_hat / (jnp.sqrt(second_hat) + EPS_ADAM) + WEIGHT_DECAY * params
        )
        states.append((new_first, new_second, new_params))

    def store(ref, at):
        for b in range(2):
            ref[b : b + 1, :] = states[b][at].reshape(1, shard * 128)

    store(R.new_first, 0)
    flush("new_first").start()
    store(R.new_second, 1)
    flush("new_second").start()
    store(R.new_params, 2)
    flush("new_params").start()
    R.params_copy[...] = R.new_params[...].astype(BF16)
    flush("params_copy").start()
    wait([flush(k) for k in RESULTS])


def deliver(*refs):
    count = (len(refs) - 1) // 3 + 1
    sources, targets, held, sems = refs[:count], refs[count : 2 * count], refs[2 * count : -1], refs[-1]
    moves = []
    for source, target in zip(sources, targets):
        if source.shape == (1, 1):
            target[0, 0] = source[0, 0]
            continue
        at = len(moves)
        into = pltpu.make_async_copy(source, held[at], sems.at[0, at])
        moves.append((into, pltpu.make_async_copy(held[at], target, sems.at[1, at])))
        into.start()
    for into, out in moves:
        into.wait()
        out.start()
    for into, out in moves:
        out.wait()


def per_device(n_win, n_fsdp, tokens, cotangent, crop_ids, params, first_moment, second_moment):
    ints, marks = constant_tables()
    extent = tokens.shape[1]
    shard = params.shape[1] // 128
    held = round_up(shard, 16)
    n_x = near_extent(n_win)
    n_near, n_z = n_fsdp * n_x, n_win // n_x
    piece = round_up(-(-shard // n_x), 16)
    padded = piece * n_x
    rows = jax.ShapeDtypeStruct(params.shape, F32)
    cells = jax.ShapeDtypeStruct((extent, SY, SZ * C), BF16)
    inputs = dict(
        tokens=tokens[0],
        cotangent=cotangent[0],
        crop=crop_ids,
        ints=ints,
        marks=marks,
        params=params,
        first_moment=first_moment,
        second_moment=second_moment,
    )
    outputs = dict(
        block_out=cells,
        input_grad=cells,
        grad_norm=jax.ShapeDtypeStruct((1, 1), F32),
        new_params=rows,
        new_first=rows,
        new_second=rows,
        params_copy=jax.ShapeDtypeStruct(params.shape, BF16),
    )
    V = pltpu.VMEM
    edge = V((SHIFT, SY, SZ * C), BF16)
    scratch = dict(
        own=V((2, shard, 128), F32),
        first_held=V((2, shard, 128), F32),
        second_held=V((2, shard, 128), F32),
        gathered=V((n_fsdp, 2, held, 128), BF16),
        edge=edge,
        edge_in=edge,
        edge_back=edge,
        halo=V((7, C, 128), BF16),
        halo_in=V((7, C, 128), BF16),
        halo_back=V((7, C, 128), BF16),
        halo_back_in=V((7, C, 128), BF16),
        outgoing=V((2, n_fsdp, padded, 128), BF16),
        incoming=V((2, n_near, piece, 128), BF16),
        parts=V((2, n_z, piece, 128), BF16),
        whole=V((2, padded, 128), BF16),
        norms=V((n_near, 8, 128), F32),
        select=V((2, 896, 2 * QLANE), BF16),
        place=V((896, QLANE), BF16),
        spread=V((176, 49 * 128), BF16),
        flat=V((FLAT + 8, 128), F32),
        wide=V((3, 384, 128), F32),
        tiles=V((80 * 56, 128), F32),
        square=V((128, 1408), F32),
        tall=V((1408, 128), F32),
        grid=V((C, 17 * 128), BF16),
        grid_two=V((C, 17 * 128), BF16),
        kept=V((SZ, C, 128), F32),
        windows=V((4, C, QLANE), F32),
        deltas=V((4, C, QLANE), F32),
        bars=V((32, QLANE), F32),
        wide_total=V((HEADS, KROW, QLANE), F32),
    )
    for k, (shape, kind) in WEIGHT_SHAPES.items():
        scratch["w_" + k] = V(shape, kind)
    for k in ("cols", "q_n", "kv_n", "proj_n", "one_n", "two_n"):
        scratch["k_" + k] = V(*WEIGHT_SHAPES[k])
    for k, (shape, kind) in SAVED_SHAPES.items():
        scratch["s_" + k] = V((5, *shape), kind)
    for k, (shape, kind) in GRAD_SHAPES.items():
        scratch["g_" + k] = V(shape, kind)
    copies = 2 * (n_fsdp - 1) + 3 * (n_near - 1) + 2 * (n_z - 1) + 2 * (n_x - 1) + 6
    for k in STAGED:
        scratch[k] = V(inputs[k].shape, inputs[k].dtype)
    for k in RESULTS:
        scratch[k] = V(outputs[k].shape, outputs[k].dtype)
    scratch["local"] = pltpu.SemaphoreType.DMA((len(STAGED) + len(RESULTS),))
    scratch["send"] = pltpu.SemaphoreType.DMA((copies,))
    scratch["recv"] = pltpu.SemaphoreType.DMA((copies,))
    outside = {k: "hbm_" + k if k in STAGED + RESULTS else k for k in [*inputs, *outputs]}
    names = [*outside.values(), *scratch]
    vmem = pl.BlockSpec(memory_space=pltpu.VMEM)
    hbm = pl.BlockSpec(memory_space=pltpu.HBM)
    smem = pl.BlockSpec(memory_space=pltpu.SMEM)
    results = pl.pallas_call(
        functools.partial(step_kernel, n_win, n_fsdp, names),
        out_shape=tuple(outputs.values()),
        in_specs=[smem if k == "crop" else hbm if k in STAGED else vmem for k in inputs],
        out_specs=tuple(smem if k == "grad_norm" else hbm for k in outputs),
        scratch_shapes=list(scratch.values()),
        compiler_params=pltpu.CompilerParams(
            collective_id=0 if n_win * n_fsdp > 1 else None,
            has_side_effects=True,
            vmem_limit_bytes=66 * 1024 * 1024 - 2 * 1024 * 1024,
        ),
        name="layer_step",
    )(*inputs.values())
    results = pl.pallas_call(
        deliver,
        out_shape=tuple(outputs.values()),
        in_specs=[smem if k == "grad_norm" else hbm for k in outputs],
        out_specs=tuple(smem if k == "grad_norm" else hbm for k in outputs),
        scratch_shapes=[
            *(V(outputs[k].shape, outputs[k].dtype) for k in RESULTS),
            pltpu.SemaphoreType.DMA((2, len(RESULTS))),
        ],
        name="deliver",
    )(*results)
    block_out, input_grad, grad_norm, *states = results
    return (block_out[None], input_grad[None], grad_norm[0, 0], *states)


def solution(mesh):
    data = P("fsdp", "win", None, None)
    state = P(None, "fsdp")
    return jax.shard_map(
        functools.partial(per_device, mesh.shape["win"], mesh.shape["fsdp"]),
        mesh=mesh,
        in_specs=(data, data, P("fsdp", None), state, state, state),
        out_specs=(data, data, P(), state, state, state, state),
        check_vma=False,
    )
```

```python
import functools
from types import SimpleNamespace as Names

import jax
import jax.numpy as jnp
import numpy as np
from jax import lax
from jax.experimental import pallas as pl
from jax.experimental.pallas import tpu as pltpu
from jax.sharding import PartitionSpec as P

C = 96
HEADS = 6
HEAD = 16
HID = 384
WS = 7
SHIFT = 3
SY = 14
SZ = 14
BPAD = 124928
STEP = 5
EPS_NORM = 1e-05
CLIP_LIMIT = 1.0
LEARN_RATE = 0.4
BETA_FIRST = 0.9
BETA_SECOND = 0.999
WEIGHT_DECAY = 0.05
EPS_ADAM = 1e-08
BIG = 1e30
LOG2E = 1.4426950408889634
LN2 = 0.6931471805599453

CELLS = WS**3
KROW = 352
QLANE = 384
FLAT = BPAD // 128
ROW_PROJ = 216
ROW_ONE = 288
ROW_TWO = 576
ROW_TABLE = 864
ROW_TAIL = 966
V_GAIN1, V_BIAS1, V_BQ, V_BV, V_BPROJ, V_GAIN2, V_BIAS2, V_BHID, V_BOUT = (
    0, 96, 192, 288, 384, 480, 576, 672, 1056,
)

F32 = jnp.float32
BF16 = jnp.bfloat16


def nn(a, b):
    return lax.dot_general(a, b, (((1,), (0,)), ((), ())), preferred_element_type=F32)


def nt(a, b):
    return lax.dot_general(a, b, (((1,), (1,)), ((), ())), preferred_element_type=F32)


def iota(shape, dim):
    return lax.broadcasted_iota(jnp.int32, shape, dim)


def roll(x, by):
    by = by % 128
    return x if by == 0 else pltpu.roll(x, by, 1)


def skew(x, by):
    while by > 0:
        some = min(1 << (by.bit_length() - 1), 16)
        x = pltpu.roll(x, 0, 1, stride=some, stride_axis=0)
        by -= some
    return x


def constant_tables():
    t = np.arange(QLANE)
    live = t < CELLS
    z, x, y = t // 49, t % 49 // 7, t % 7
    ints = np.full((8, QLANE), -1, np.int32)
    for s in range(2):
        for wy in range(2):
            cell_y = (y + 7 * wy + SHIFT * s) % SY
            ints[2 * s + wy] = np.where(live, z * 128 + x * 16 + cell_y, -1)
    ints[4] = np.where(live, z * 128 + t % 49, -1)
    ints[5] = np.where(live, x, -1)
    lane = np.arange(128)
    ints[6, :128] = np.where(lane < 49, 13 * (lane // 7) + lane % 7, -1000)
    marks = np.zeros((64, QLANE), np.float32)
    for i in range(7):
        marks[i] = live & (x == i)
        marks[7 + i] = live & (y == i)
        marks[14 + i] = live & (z == i)
        marks[32 + 7 + i] = live & ((i >= 4) != (y >= 4))
        marks[32 + 14 + i] = live & ((i >= 4) != (z >= 4))
    return jnp.asarray(ints), jnp.asarray(marks, BF16)


def unit_copy(pieces, units):
    out = None
    for at, unit in enumerate(units):
        if unit is None:
            continue
        i, g = unit
        moved = roll(pieces[i], 32 * (at - g))
        group = iota(moved.shape, 1) // 32
        base = jnp.zeros_like(moved) if out is None else out
        out = jnp.where(group == at, moved, base)
    return out


def read_matrix(flat, base, rows, width, store):
    units = width // 32
    if units % 4 == 0:
        step = units // 4
        for o in range(step):
            store(0, 1, o, flat[pl.ds(base + o, rows, stride=step), :])
        return
    groups = rows // 4
    loaded = [flat[pl.ds(base + o, groups, stride=units), :] for o in range(units)]
    for j in range(4):
        for p in range(units // 3):
            first = units * j + 3 * p
            store(j, 4, p, unit_copy(loaded, [divmod(first + s, 4) for s in range(3)] + [None]))


def write_matrix(flat, base, rows, width, load):
    units = width // 32
    if units % 4 == 0:
        step = units // 4
        for o in range(step):
            flat[pl.ds(base + o, rows, stride=step), :] = load(0, 1, o)
        return
    groups = rows // 4
    parts = units // 3
    loaded = [load(j, 4, p) for j in range(4) for p in range(parts)]
    for o in range(units):
        flat[pl.ds(base + o, groups, stride=units), :] = unit_copy(
            loaded, [divmod(4 * o + g, 3) for g in range(4)]
        )


def build_selectors(ints, select, place, spread):
    for s in range(2):
        for wy in range(2):
            need = ints[2 * s + wy : 2 * s + wy + 1, :]
            for r in range(7):
                row = iota((128, QLANE), 0) + 128 * r
                select[s, 128 * r : 128 * r + 128, QLANE * wy : QLANE * wy + QLANE] = jnp.where(
                    row == need, 1.0, 0.0
                ).astype(BF16)
    need = ints[4:5, :]
    for r in range(7):
        row = iota((128, QLANE), 0) + 128 * r
        place[128 * r : 128 * r + 128, :] = jnp.where(row == need, 1.0, 0.0).astype(BF16)
    gap = iota((176, 128), 0) - ints[6:7, :128]
    for k in range(49):
        hit = gap == 84 - 13 * (k // 7) - k % 7
        spread[:, 128 * k : 128 * k + 128] = jnp.where(hit, 1.0, 0.0).astype(BF16)


def table_pick(second):
    row = iota((176, 104), 0)
    col = iota((176, 104), 1) - second
    at = 128 * col
    start = 78 * row
    hit = (start >= at) & (start < at + 128) & (row < 169)
    return jnp.where(hit, 1.0, 0.0).astype(BF16)


def table_start():
    row = iota((176, 128), 0)
    return jnp.bitwise_and(78 * row, 127)


def build_table(flat, spread, place, tiles, table):
    rows = flat[ROW_TABLE : ROW_TABLE + 104, :].astype(BF16)
    first = skew(nn(table_pick(0), rows), 50)
    second = skew(nn(table_pick(1), rows), 50)
    lane = iota((176, 128), 1)
    mixed = jnp.where(lane + table_start() < 128, first, second)
    mixed = jnp.where((lane < 78) & (iota((176, 128), 0) < 169), mixed, 0.0)
    turned = jnp.concatenate([mixed, jnp.zeros((80, 128), F32)], axis=0).T
    cube = turned[:80, :176].astype(BF16)
    for k in range(0, 49, 2):
        some = min(2, 49 - k)
        block = nn(cube, spread[:, 128 * k : 128 * k + 128 * some])
        for i in range(some):
            tiles[pl.ds(k + i, 80, stride=56), :] = block[:, 128 * i : 128 * i + 128]

    def gathered(ck, first, last):
        return jnp.concatenate(
            [
                tiles[336 * (cq - ck + 6) : 336 * (cq - ck + 7), :].astype(BF16)
                for cq in range(first, last)
            ],
            axis=1,
        )

    for ck in range(7):
        block = jnp.concatenate(
            [
                nn(gathered(ck, 0, 6), place[0:768, 0:256]),
                nn(gathered(ck, 5, 7), place[640:896, 256:QLANE]),
            ],
            axis=1,
        )
        block = block * LOG2E
        for h in range(HEADS):
            table[h, 49 * ck : 49 * ck + 49, :] = block[56 * h : 56 * h + 49, :]
    for h in range(HEADS):
        table[h, CELLS:KROW, :] = jnp.full((KROW - CELLS, QLANE), -BIG, F32)


def collapse_table(total, wide_total, spread, place, tiles, flat):
    tiles[...] = jnp.zeros(tiles.shape, F32)
    for h in range(HEADS):
        wide_total[h] = total[h].astype(F32)
    for ck in range(7):
        lhs = jnp.concatenate(
            [wide_total[h, 49 * ck : 49 * ck + 56, :] for h in range(HEADS)], axis=0
        ).astype(BF16)
        for cq, start, end in ((0, 0, 128), (2, 0, 256), (4, 128, 384), (6, 256, 384)):
            some = min(2, 7 - cq)
            block = nt(lhs[:, start:end], place[128 * cq : 128 * cq + 128 * some, start:end])
            for i in range(some):
                dc = cq + i - ck + 6
                tiles[336 * dc : 336 * dc + 336, :] += block[:, 128 * i : 128 * i + 128]
    lhs = jnp.concatenate(
        [tiles[pl.ds(k, 80, stride=56), :].astype(BF16) for k in range(49)], axis=1
    )
    cube = nt(lhs, spread[...])
    wide = jnp.concatenate([cube, jnp.zeros((80, 80), F32)], axis=1)
    wide = jnp.concatenate([wide, jnp.zeros((48, 256), F32)], axis=0)
    mixed = wide.T[:176, :]
    mixed = skew(mixed, 78)
    fits = iota((176, 128), 1) >= table_start()
    lane = iota((176, 128), 1)
    length = jnp.bitwise_and(lane - table_start(), 127)
    live = (length < 78) & (iota((176, 128), 0) < 169)
    head = jnp.where(fits & live, mixed, 0.0).astype(BF16)
    rest = jnp.where(jnp.logical_not(fits) & live, mixed, 0.0).astype(BF16)

    def tn(a, b):
        return lax.dot_general(a, b, (((0,), (0,)), ((), ())), preferred_element_type=F32)

    return tn(table_pick(0), head) + tn(table_pick(1), rest)


def tail_vector(tail, start, width):
    o, at = divmod(start, 128)
    lane = iota((1, 128), 1)
    out = roll(tail[o : o + 1, :], -at)
    if at + width > 128:
        out = jnp.where(lane < 128 - at, out, roll(tail[o + 1 : o + 2, :], -at))
    return jnp.where(lane < width, out, 0.0)


def prepare(flat, W, wide, spread, place, tiles):
    rows = flat[ROW_TAIL : ROW_TAIL + 16, :]
    lane = iota((9, 128), 1)
    tail = jnp.where(lane < 2, roll(rows[:9], 2), roll(rows[1:10], 2))
    turned = jnp.concatenate([tail, jnp.zeros((119, 128), F32)], axis=0).T
    for o in range(9):
        W.cols[128 * o : 128 * o + 128, :] = jnp.broadcast_to(turned[:, o : o + 1], (128, 128))

    def into(j, step, p, value):
        wide[p, pl.ds(j, value.shape[0], stride=step), :] = value

    def finish(p, bias):
        wide[p, 96:97, :] = bias
        wide[p, 97:128, :] = jnp.zeros((31, 128), F32)

    read_matrix(flat, 0, C, 3 * C, into)
    finish(0, tail_vector(tail, V_BQ, C))
    finish(1, jnp.zeros((1, 128), F32))
    finish(2, tail_vector(tail, V_BV, C))
    W.q_n[...] = wide[0, 0:96, :].astype(BF16)
    for p in range(1, 3):
        W.kv_n[:, 128 * p - 128 : 128 * p] = wide[p, 0:96, :].astype(BF16)
    for p in range(3):
        W.qkv_t[96 * p : 96 * p + 96, :] = wide[p, 0:128, :].T[:96].astype(BF16)

    read_matrix(flat, ROW_PROJ, C, C, into)
    finish(0, tail_vector(tail, V_BPROJ, C))
    W.proj_n[...] = wide[0, 0:96, :].astype(BF16)
    W.proj_t[...] = wide[0, 0:128, :].T[:96].astype(BF16)

    read_matrix(flat, ROW_ONE, C, HID, into)
    for p in range(3):
        finish(p, tail_vector(tail, V_BHID + 128 * p, 128))
        W.one_n[:, 128 * p : 128 * p + 128] = wide[p, 0:96, :].astype(BF16)
        W.one_t[128 * p : 128 * p + 128, :] = wide[p, 0:128, :].T.astype(BF16)

    read_matrix(flat, ROW_TWO, HID, C, into)
    W.two_n[...] = wide[0].astype(BF16)
    for p in range(3):
        W.two_t[:, 128 * p : 128 * p + 128] = wide[0, 128 * p : 128 * p + 128, :].T[:96].astype(
            BF16
        )
    build_table(flat, spread, place, tiles, W.table)


WEIGHT_SHAPES = dict(
    cols=((1152, 128), F32),
    q_n=((96, 128), BF16),
    kv_n=((96, 256), BF16),
    qkv_t=((288, 128), BF16),
    proj_n=((96, 128), BF16),
    proj_t=((96, 128), BF16),
    one_n=((96, 384), BF16),
    one_t=((384, 128), BF16),
    two_n=((384, 128), BF16),
    two_t=((96, 384), BF16),
    table=((HEADS, KROW, QLANE), F32),
)


SAVED_SHAPES = dict(
    normed=((128, QLANE), BF16),
    hat=((96, QLANE), F32),
    scale=((8, QLANE), F32),
    qkv=((288, QLANE), BF16),
    probs=((HEADS, KROW, QLANE), BF16),
    inverse=((8, QLANE), F32),
    attended=((128, QLANE), BF16),
    hat_two=((96, QLANE), F32),
    scale_two=((8, QLANE), F32),
    normed_two=((128, QLANE), BF16),
    slope=((HID, QLANE), BF16),
    active=((HID, QLANE), BF16),
)

GRAD_SHAPES = dict(
    q=((112, 128), F32),
    kv=((2, 112, 128), F32),
    proj=((112, 128), F32),
    one=((112, 384), F32),
    two=((400, 128), F32),
    gain1=((96, 128), F32),
    bias1=((96, 128), F32),
    gain2=((96, 128), F32),
    bias2=((96, 128), F32),
    total=((HEADS, KROW, QLANE), BF16),
)


def column(W, start, rows=96):
    part = W.cols[start : start + rows, :]
    return jnp.concatenate([part, part, part], axis=1)


def extended(rows):
    width = rows.shape[1]
    return jnp.concatenate([rows, jnp.ones((16, width), BF16), jnp.zeros((16, width), BF16)], axis=0)


def standardize(x):
    centered = x - jnp.mean(x, axis=0, keepdims=True)
    variance = jnp.mean(centered * centered, axis=0, keepdims=True)
    scale = lax.rsqrt(variance + EPS_NORM)
    return centered * scale, scale


def at_head(h, rows, tail):
    width = rows.shape[1]
    parts = []
    if h > 0:
        parts.append(jnp.zeros((16 * h, width), BF16))
    parts.append(rows)
    if h < HEADS - 1:
        parts.append(jnp.zeros((16 * (HEADS - 1 - h), width), BF16))
    return jnp.concatenate(parts + [tail], axis=0)


def scaled_queries(qkv):
    return (qkv[0:96].astype(F32) * (HEAD**-0.5 * LOG2E)).astype(BF16)


def window_norm(x, S, s):
    hat, scale = standardize(x)
    S.hat[s] = hat
    S.scale[s, 0:1] = scale


def window_forward(x, W, S, s, marks, barred):
    hat = S.hat[s]
    normed = extended((hat * column(W, V_GAIN1) + column(W, V_BIAS1)).astype(BF16))
    S.normed[s] = normed
    qkv = nn(W.qkv_t[...], normed).astype(BF16)
    S.qkv[s] = qkv
    queries = scaled_queries(qkv)
    keys = jnp.concatenate([qkv[96:192], marks[0:32, :]], axis=0).T[:KROW]
    ones = jnp.ones((16, KROW), BF16)

    def pair_scores(p):
        sides = [at_head(h, queries[16 * h : 16 * h + 16], barred) for h in (2 * p, 2 * p + 1)]
        return nn(keys, jnp.concatenate(sides, axis=1))

    parts = []
    coming = pair_scores(0)
    for h in range(HEADS):
        if h % 2 == 0:
            pair = coming
            if h + 2 < HEADS:
                coming = pair_scores(h // 2 + 1)
        scores = pair[:, QLANE * (h % 2) : QLANE * (h % 2) + QLANE] + W.table[h]
        highest = jnp.max(scores, axis=0, keepdims=True)
        probs = jnp.exp2(scores - highest).astype(BF16)
        S.probs[s, h] = probs
        values = jnp.concatenate([qkv[192 + 16 * h : 208 + 16 * h, :KROW], ones], axis=0)
        mixed = nn(values, probs)
        inverse = 1.0 / mixed[16:17]
        S.inverse[s, h : h + 1] = inverse
        parts.append((mixed[:16] * inverse).astype(BF16))
    attended = extended(jnp.concatenate(parts, axis=0))
    S.attended[s] = attended
    branch = nn(W.proj_t[...], attended).astype(BF16)
    middle = x + branch.astype(F32)
    hat, scale = standardize(middle)
    S.hat_two[s] = hat
    S.scale_two[s, 0:1] = scale
    normed_two = extended((hat * column(W, V_GAIN2) + column(W, V_BIAS2)).astype(BF16))
    S.normed_two[s] = normed_two
    hidden = nn(W.one_t[...], normed_two)
    share = 0.5 + 0.5 * lax.erf(hidden * (0.5**0.5))
    active = (hidden * share).astype(BF16)
    S.active[s] = active
    slope = share + hidden * jnp.exp2(hidden * hidden * (-0.5 * LOG2E)) * 0.3989422804014327
    S.slope[s] = slope.astype(BF16)
    return middle + nn(W.two_t[...], active) + column(W, V_BOUT)


def fold(x):
    return x[:, 0:128] + x[:, 128:256] + x[:, 256:384]


def norm_backward(grad, hat, scale, gain):
    scaled = grad * gain
    mean_one = jnp.mean(scaled, axis=0, keepdims=True)
    mean_two = jnp.mean(scaled * hat, axis=0, keepdims=True)
    return scale * (scaled - mean_one - hat * mean_two)


def window_backward(grad, W, S, s, G, marks, barred):
    result = extended(grad.astype(BF16))
    active = S.active[s]
    G.two[...] += nt(jnp.concatenate([active, jnp.ones((16, QLANE), BF16)], axis=0), result)
    hidden = (nn(W.two_n[...], result) * S.slope[s].astype(F32)).astype(BF16)
    G.one[...] += nt(S.normed_two[s, 0:112], hidden)
    d_normed = nn(W.one_n[...], hidden)
    hat = S.hat_two[s]
    G.gain2[...] += fold(d_normed * hat)
    G.bias2[...] += fold(d_normed)
    d_middle = grad + norm_backward(d_normed, hat, S.scale_two[s, 0:1], column(W, V_GAIN2))
    d_branch = extended(d_middle.astype(BF16))
    attended = S.attended[s]
    G.proj[...] += nt(attended[0:112], d_branch)
    d_attended = nn(W.proj_n[...], d_branch).astype(BF16).astype(F32)
    product = d_attended * attended[0:96].astype(F32)
    qkv = S.qkv[s]
    queries = scaled_queries(qkv)
    values = extended(qkv[192:288]).T[:KROW]
    row = iota((32, QLANE), 0)
    parts, d_keys, d_values = [], [], []

    def head_gradient(h):
        inverse = S.inverse[s, h : h + 1]
        inner = jnp.sum(product[16 * h : 16 * h + 16], axis=0, keepdims=True) * inverse
        high = inner.astype(BF16)
        low = (inner - high.astype(F32)).astype(BF16)
        less = jnp.where(row == 0, -high.astype(F32), jnp.where(row == 1, -low.astype(F32), 0.0))
        rows = (d_attended[16 * h : 16 * h + 16] * inverse).astype(BF16)
        return rows, at_head(h, rows, less.astype(BF16))

    def pair_gradient(p):
        d_outs = [head_gradient(h) for h in (2 * p, 2 * p + 1)]
        product = nn(values, jnp.concatenate([d_out for _, d_out in d_outs], axis=1))
        return d_outs, product.astype(BF16)

    def head_products(h, d_scores, rows, probs):
        d_keys.append(nt(queries[16 * h : 16 * h + 16], d_scores))
        d_values.append(nt(rows, probs))
        parts.append(nn(qkv[96 + 16 * h : 112 + 16 * h, :KROW], d_scores))

    late = []
    coming = pair_gradient(0)
    for p in range(HEADS // 2):
        d_outs, d_pair = coming
        if p + 1 < HEADS // 2:
            coming = pair_gradient(p + 1)
        for h in (2 * p, 2 * p + 1):
            probs = S.probs[s, h]
            d_scores = probs * d_pair[:, QLANE * (h % 2) : QLANE * (h % 2) + QLANE]
            G.total[h] += d_scores
            late.append((h, d_scores, d_outs[h % 2][0], probs))
            if len(late) > 6:
                head_products(*late.pop(0))
    for held in late:
        head_products(*held)
    d_queries = (jnp.concatenate(parts, axis=0) * HEAD**-0.5).astype(BF16)
    gap = jnp.zeros((32, QLANE), BF16)
    tokens_gap = jnp.zeros((96, QLANE - KROW), F32)

    def side(rows, factor):
        rows = jnp.concatenate(rows, axis=0) * factor
        return jnp.concatenate([rows, tokens_gap], axis=1).astype(BF16)

    d_pair = jnp.concatenate([side(d_keys, LN2), gap, side(d_values, 1.0), gap], axis=0)
    normed = S.normed[s, 0:112]
    G.q[:, 0:96] += nt(normed, d_queries)
    both = nt(normed, d_pair)
    for p in range(2):
        G.kv[p] += both[:, 128 * p : 128 * p + 128]
    d_normed = nn(W.q_n[:, 0:96], d_queries) + nn(W.kv_n[...], d_pair)
    hat = S.hat[s]
    G.gain1[...] += fold(d_normed * hat)
    G.bias1[...] += fold(d_normed)
    return d_middle + norm_backward(d_normed, hat, S.scale[s, 0:1], column(W, V_GAIN1))


def finish_gradients(G, matrices_done, wide_total, flat, wide, spread, place, tiles):
    def qkv_rows(j, step, p):
        if p == 0:
            return G.q[pl.ds(j, 24, stride=4), :]
        return G.kv[p - 1, pl.ds(j, 24, stride=4), :]

    write_matrix(flat, 0, C, 3 * C, qkv_rows)
    write_matrix(flat, ROW_PROJ, C, C, lambda j, step, p: G.proj[pl.ds(j, 24, stride=4), :])
    write_matrix(
        flat, ROW_ONE, C, HID, lambda j, step, p: G.one[0:96, 128 * p : 128 * p + 128]
    )
    write_matrix(flat, ROW_TWO, HID, C, lambda j, step, p: G.two[pl.ds(j, 96, stride=4), :])
    matrices_done()
    lane = iota((96, 128), 1)
    columns = jnp.zeros((96, 128), F32)
    for at, ref in enumerate([G.gain1, G.bias1, G.gain2, G.bias2]):
        columns = jnp.where(lane == at, jnp.sum(ref[...], axis=1, keepdims=True), columns)
    turned = jnp.concatenate([columns, jnp.zeros((32, 128), F32)], axis=0).T
    sources = [
        (turned[0:1], 3),
        (turned[1:2], 3),
        (G.q[96:97, :], 3),
        (G.kv[1, 96:97, :], 3),
        (G.proj[96:97, :], 3),
        (turned[2:3], 3),
        (turned[3:4], 3),
        (G.one[96:97, 0:128], 4),
        (G.one[96:97, 128:256], 4),
        (G.one[96:97, 256:384], 4),
        (G.two[384:385, :], 3),
    ]
    pieces = [source for source, _ in sources]
    units = [(i, g) for i, (_, count) in enumerate(sources) for g in range(count)]
    tail = jnp.concatenate(
        [unit_copy(pieces, units[4 * o : 4 * o + 4]) for o in range(9)], axis=0
    )
    table = collapse_table(G.total, wide_total, spread, place, tiles, flat)
    flat[ROW_TABLE:ROW_TAIL, :] = table[0:102]
    none = jnp.zeros((1, 128), F32)
    moved = roll(jnp.concatenate([none, tail, none], axis=0), 126)
    lane = iota((10, 128), 1)
    mixed = jnp.where(lane >= 126, moved[1:11], moved[0:10])
    first = jnp.where(iota((1, 128), 1) >= 126, mixed[0:1], table[102:103])
    flat[ROW_TAIL:FLAT, :] = jnp.concatenate([first, mixed[1:10]], axis=0)


def round_up(value, to):
    return -(-value // to) * to


def take_grid(row_of, square, tall, grid, wrapped):
    for x in range(7):
        square[16 * x : 16 * x + 14, 0 : SZ * C] = row_of(x)
    for i in range(11):
        tall[128 * i : 128 * i + 128, :] = square[:, 128 * i : 128 * i + 128].T
    for z in range(SZ + 3 if wrapped else SZ):
        grid[:, 128 * z : 128 * z + 128] = tall[C * (z % SZ) : C * (z % SZ) + C, :].astype(BF16)


def take_window(grid, select, s, wy, wz):
    rows = grid[:, pl.ds(pl.multiple_of(896 * wz + 384 * s, 128), 896)]
    return nn(rows, select[s, :, pl.ds(pl.multiple_of(QLANE * wy, 128), QLANE)])


def give_grid(windows, select, s, wz, put):
    both = jnp.concatenate([windows[2 * wz], windows[2 * wz + 1]], axis=1).astype(BF16)
    cells = nt(both, select[s])
    for r in range(7):
        put((r + 7 * wz + SHIFT * s) % SZ, cells[:, 128 * r : 128 * r + 128])


def give_rows(tall, square):
    for i in range(11):
        square[:, 128 * i : 128 * i + 128] = tall[128 * i : 128 * i + 128, :].T


def crop_bars(crop, ints, first, total):
    ids = [crop[0, lax.rem(first + a, total)] for a in range(7)]
    at = ints[5:6, :]
    own = jnp.zeros((1, QLANE), jnp.int32)
    for a in range(7):
        own = jnp.where(at == a, ids[a], own)
    row = iota((32, QLANE), 0)
    key = jnp.full((32, QLANE), -1, jnp.int32)
    for a in range(7):
        key = jnp.where(row == a, ids[a], key)
    return jnp.where((row < 7) & (key != own), -BIG, 0.0)


def shift_bars(marks, wy, wz):
    row = iota((32, QLANE), 0)
    factor = jnp.where(row < 14, wy, wz).astype(F32) * -BIG
    return marks[32:64, :].astype(F32) * factor


STAGED = ("params", "tokens", "cotangent")
RESULTS = ("block_out", "input_grad", "grads")
TAKEN = ("block_out", "input_grad", "grads", "params", "first_moment", "second_moment")
GIVEN = ("block_out", "input_grad", "new_params", "new_first", "new_second", "params_copy")


def near_extent(n_win):
    n_x = 1
    while 4 * n_x * n_x <= n_win:
        n_x *= 2
    return n_x


def step_kernel(n_win, n_fsdp, names, *refs):
    held = dict(zip(names, refs))
    R = Names(**held)
    W = Names(**{k: held["w_" + k] for k in WEIGHT_SHAPES})
    S = Names(**{k: held["s_" + k] for k in SAVED_SHAPES})
    G = Names(**{k: held["g_" + k] for k in GRAD_SHAPES})
    tokens, cotangent, crop = R.tokens, R.cotangent, R.crop
    ints, marks = R.ints, R.marks
    select, place, spread = R.select, R.place, R.spread
    flat, wide, tiles = R.flat, R.wide, R.tiles
    square, tall = R.square, R.tall
    send, recv = R.send, R.recv
    shard = FLAT // n_fsdp
    extent = tokens.shape[0]
    total = n_win * extent
    me_win, me_fsdp = lax.axis_index("win"), lax.axis_index("fsdp")
    left, right = lax.rem(me_win + n_win - 1, n_win), lax.rem(me_win + 1, n_win)
    n_x = near_extent(n_win)
    n_z = n_win // n_x
    me_x, me_z = lax.rem(me_win, n_x), me_win // n_x
    me_near = me_fsdp * n_x + me_x
    near = []
    for k in range(1, n_fsdp * n_x):
        f, x = lax.rem(me_fsdp + k // n_x, n_fsdp), lax.rem(me_x + k % n_x, n_x)
        near.append((k, f, x, {"win": me_z * n_x + x, "fsdp": f}))
    far = [(k, {"win": lax.rem(me_z + k, n_z) * n_x + me_x}) for k in range(1, n_z)]
    sides = [{"win": left}, {"win": right}] if n_win > 1 else []
    slots = {}

    def remote(name, src, dst, to):
        slot = slots.setdefault(name, len(slots))
        return pltpu.make_async_remote_copy(
            src_ref=src,
            dst_ref=dst,
            send_sem=send.at[slot],
            recv_sem=recv.at[slot],
            device_id=to,
            device_id_type=pl.DeviceIdType.MESH,
        )

    def start(copies):
        for copy in copies:
            copy.start()
        return copies

    def neighbour(name, src, dst, to):
        if n_win > 1:
            return start([remote(name, src, dst, {"win": to})])
        dst[...] = src[...]
        return []

    def fetch(k):
        at = STAGED.index(k)
        return pltpu.make_async_copy(held["hbm_" + k], held[k], R.local.at[at])

    def flush(k):
        at = len(STAGED) + RESULTS.index(k)
        return pltpu.make_async_copy(held[k], held["hbm_" + k], R.local.at[at])

    def wait(copies):
        for copy in copies:
            copy.wait()

    start([fetch(k) for k in STAGED])
    if n_win * n_fsdp > 1:
        barrier = pltpu.get_barrier_semaphore()
        peers = [peer[-1] for peer in near + far] + sides
        for peer in peers:
            pl.semaphore_signal(
                barrier, inc=1, device_id=peer, device_id_type=pl.DeviceIdType.MESH
            )
    gathered = R.gathered
    fetch("params").wait()
    for b in range(2):
        rows = R.params[b : b + 1, :].reshape(shard, 128)
        gathered[me_fsdp, b, 0:shard, :] = rows.astype(BF16)
    fetch("cotangent").wait()
    R.edge[...] = cotangent[0:SHIFT]
    build_selectors(ints, select, place, spread)
    square[...] = jnp.zeros(square.shape, F32)
    fetch("tokens").wait()
    take_grid(lambda x: tokens[x].astype(F32), square, tall, R.grid, False)
    windows, deltas = R.windows, R.deltas

    def first_window(w, carry):
        x = take_window(R.grid, select, 0, lax.rem(w, 2), w // 2)
        windows[w] = x
        window_norm(x, S, w)
        return carry

    lax.fori_loop(0, 4, first_window, 0)
    if n_win * n_fsdp > 1:
        pl.semaphore_wait(barrier, len(peers))

    weights_in = []
    for b in range(2):
        mine = gathered.at[me_fsdp, b]
        copies = []
        for k in range(1, n_fsdp):
            to = {"fsdp": lax.rem(me_fsdp + k, n_fsdp)}
            copies.append(remote(("weights", b, k), mine, mine, to))
        weights_in.append(start(copies))
    halo_in = neighbour("halo", R.edge, R.edge_in, left)

    def clear(ref):
        ref[...] = jnp.zeros(ref.shape, ref.dtype)

    for ref in vars(G).values():
        clear(ref)
    wait(halo_in)

    def shifted_cotangent(x):
        return (cotangent[x + SHIFT] if x < 7 - SHIFT else R.edge_in[x - 7 + SHIFT]).astype(F32)

    take_grid(shifted_cotangent, square, tall, R.grid_two, True)

    def spread_weights(b):
        wait(weights_in[b])
        for f in range(n_fsdp):
            flat[shard * f : shard * f + shard, :] = gathered[f, b, 0:shard, :].astype(F32)
        prepare(flat, W, wide, spread, place, tiles)

    spread_weights(0)
    R.bars[...] = crop_bars(crop, ints, me_win * extent, total)

    halo, halo_back = R.halo, R.halo_back
    kept = R.kept
    lane = iota((C, 128), 1)
    slab_parts = [(0, 3), (3, 7)]

    def slab_copy(wz, name, src, dst, to):
        begin, end = slab_parts[wz]
        part = pl.ds(begin, end - begin)
        return remote((name, wz), src.at[part], dst.at[part], {"win": to})

    def pass_slab(wz, name, src, dst, to):
        if n_win > 1:
            start([slab_copy(wz, name, src, dst, to)])
        else:
            begin, end = slab_parts[wz]
            dst[begin:end] = src[begin:end]

    def wait_slab(name, src, dst, to):
        if n_win > 1:
            wait([slab_copy(wz, name, src, dst, to) for wz in range(2)])

    def put_kept(z, value):
        kept[z] = value

    def give_slices(wz):
        give_grid(windows, select, 0, wz, put_kept)
        for i in range(*slab_parts[wz]):
            pair = jnp.where(lane < 64, kept[2 * i], roll(kept[2 * i + 1], 64))
            halo[i] = pair.astype(BF16)
        pass_slab(wz, "slab", halo, R.halo_in, left)

    def first_forward(w, carry):
        windows[w] = window_forward(windows[w], W, S, w, marks, R.bars[...].astype(BF16))

        @pl.when(w == 1)
        def _():
            give_slices(0)

        return carry

    lax.fori_loop(0, 4, first_forward, 0)

    give_slices(1)
    first_weights = {}
    for k in ("cols", "q_n", "kv_n", "proj_n", "one_n", "two_n"):
        held["k_" + k][...] = held["w_" + k][...]
        first_weights[k] = held["k_" + k]
    spread_weights(1)
    wait_slab("slab", halo, R.halo_in, left)
    for z in range(SZ + 3):
        pair = R.halo_in[z % SZ // 2].astype(F32)
        if z % SZ % 2 == 0:
            pair = roll(pair, 64)
        joined = jnp.where(lane < 64, roll(kept[z % SZ], -48), pair)
        R.grid[:, 128 * z : 128 * z + 128] = joined.astype(BF16)

    R.bars[...] = crop_bars(crop, ints, me_win * extent + SHIFT, total)

    def give_back(wz):
        give_grid(deltas, select, 1, wz, put_kept)
        for at in range(*slab_parts[wz]):
            i = (at + 2) % 7
            pair = jnp.where(lane < 64, roll(kept[2 * i], 64), kept[2 * i + 1])
            halo_back[at] = pair.astype(BF16)
        pass_slab(wz, "slab_back", halo_back, R.halo_back_in, right)

    def second(w, carry):
        wy, wz = lax.rem(w, 2), w // 2
        bars = (R.bars[...] + shift_bars(marks, wy, wz)).astype(BF16)
        x = take_window(R.grid, select, 1, wy, wz)
        window_norm(x, S, 4)
        windows[w] = window_forward(x, W, S, 4, marks, bars)
        grad = take_window(R.grid_two, select, 1, wy, wz)
        deltas[w] = window_backward(grad, W, S, 4, G, marks, bars)

        @pl.when(w == 1)
        def _():
            give_back(0)

        return carry

    lax.fori_loop(0, 4, second, 0)

    give_back(1)

    def put_tall(z, value):
        tall[C * z : C * z + C, :] = value

    for wz in range(2):
        give_grid(windows, select, 1, wz, put_tall)
    give_rows(tall, square)
    for x in range(7 - SHIFT):
        R.block_out[x + SHIFT] = square[16 * x : 16 * x + 14, 0 : SZ * C].astype(BF16)
    for x in range(SHIFT):
        at = 16 * (x + 7 - SHIFT)
        R.edge[x] = square[at : at + 14, 0 : SZ * C].astype(BF16)
    out_back = neighbour("out_back", R.edge, R.edge_back, right)

    padded = R.outgoing.shape[2]
    piece = padded // n_x

    def scatter(b):
        early = ROW_TABLE // shard

        def send(first, last):
            for f in range(first, last):
                R.outgoing[b, f, 0:shard, :] = flat[shard * f : shard * f + shard, :].astype(BF16)
                if padded > shard:
                    R.outgoing[b, f, shard:padded, :] = jnp.zeros((padded - shard, 128), BF16)
            for (k, f, x, to), copy in zip(near, near_copies(b)):
                pl.when((f >= first) & (f < last))(copy.start)

        finish_gradients(
            G, lambda: send(0, early), R.wide_total, flat, wide, spread, place, tiles
        )
        send(early, n_fsdp)

    def rows_of(x):
        return pl.ds(pl.multiple_of(piece * x, 16), piece)

    own = rows_of(me_x)

    def near_copies(b):
        return [
            remote(
                ("near", b, k), R.outgoing.at[b, f, rows_of(x)], R.incoming.at[b, me_near], to
            )
            for k, f, x, to in near
        ]

    def far_copies(b):
        mine = R.parts.at[b, me_z]
        return [remote(("far", b, k), mine, mine, to) for k, to in far]

    def whole_copies(b):
        mine = R.grads.at[b, own]
        return [remote(("whole", b, k), mine, mine, to) for k, f, x, to in near if k < n_x]

    def norm_copies():
        mine = R.norms.at[me_near]
        return [remote(("norm", k), mine, mine, to) for k, f, x, to in near]

    def add_near(b):
        wait(near_copies(b))
        R.incoming[b, me_near] = R.outgoing[b, me_fsdp, own, :]
        total_rows = R.incoming[b, 0].astype(F32)
        for i in range(1, n_fsdp * n_x):
            total_rows += R.incoming[b, i].astype(F32)
        R.parts[b, me_z] = total_rows.astype(BF16)
        start(far_copies(b))

    def add_far(b):
        wait(far_copies(b))
        total_rows = R.parts[b, 0].astype(F32)
        for i in range(1, n_z):
            total_rows += R.parts[b, i].astype(F32)
        R.grads[b, own, :] = total_rows.astype(BF16)
        start(whole_copies(b))
        squares = jnp.sum((total_rows * total_rows).reshape(piece // 8, 8, 128), axis=0)
        if b == 1:
            R.norms[me_near] = squares
        else:
            R.norms[me_near] += squares
            start(norm_copies())

    scatter(1)
    wait_slab("slab_back", halo_back, R.halo_back_in, right)
    for z in range(SZ):
        pair = R.halo_back_in[(z // 2 + 5) % 7].astype(F32)
        if z % 2 == 1:
            pair = roll(pair, 64)
        joined = jnp.where(lane < 48, pair, roll(kept[z], 48))
        R.grid[:, 128 * z : 128 * z + 128] = joined.astype(BF16)
    for ref in vars(G).values():
        clear(ref)
    W0 = Names(**{**vars(W), **first_weights})

    def first_backward(w, carry):
        grad = take_window(R.grid, select, 0, lax.rem(w, 2), w // 2)
        deltas[w] = window_backward(grad, W0, S, w, G, marks, R.bars[...].astype(BF16))

        @pl.when(w == 1)
        def _():
            add_near(1)

        @pl.when(w == 2)
        def _():
            add_far(1)

        return carry

    lax.fori_loop(0, 4, first_backward, 0)
    scatter(0)
    for wz in range(2):
        give_grid(deltas, select, 0, wz, put_tall)
    give_rows(tall, square)
    for x in range(7):
        R.input_grad[x] = square[16 * x : 16 * x + 14, 0 : SZ * C].astype(BF16)
    flush("input_grad").start()
    wait(out_back)
    R.block_out[0:SHIFT] = R.edge_back[...]
    flush("block_out").start()
    add_near(0)
    wait(whole_copies(1))
    add_far(0)
    wait(whole_copies(0))
    wait(norm_copies())
    norm = R.norms[0]
    for i in range(1, n_fsdp * n_x):
        norm += R.norms[i]
    norm = jnp.sum(jnp.sum(norm, axis=0, keepdims=True), axis=1, keepdims=True)
    norm = jnp.broadcast_to(jnp.sqrt(norm), (1, 128))
    R.grad_norm[0, 0] = norm[0, 0]
    flush("grads").start()
    wait([flush(k) for k in RESULTS])


def optimizer_kernel(names, *refs):
    R = Names(**dict(zip(names, refs)))
    held = vars(R)
    n = R.params.shape[1]

    def move(i, k, out):
        ends = (held[k], held["out_" + k]) if out else (held["in_" + k], held[k])
        return pltpu.make_async_copy(*ends, R.local.at[i])

    coming = {k: move(i, k, False) for i, k in enumerate(TAKEN)}
    going = {k: move(len(TAKEN) + i, k, True) for i, k in enumerate(GIVEN)}
    for copy in coming.values():
        copy.start()
    for k in ("block_out", "input_grad"):
        coming[k].wait()
        going[k].start()
    for k in TAKEN[2:]:
        coming[k].wait()
    R.out_grad_norm[0, 0] = R.grad_norm[0, 0]
    norm = jnp.full((1, 128), R.grad_norm[0, 0], F32)
    factor = jnp.minimum(1.0, CLIP_LIMIT / (norm + 1e-06))
    states = []
    for b in range(2):

        def rows(ref):
            return ref[b : b + 1, :].reshape(n // 128, 128)

        params = rows(R.params)
        clipped = R.grads[b, 0 : n // 128, :].astype(F32) * factor
        new_first = BETA_FIRST * rows(R.first_moment) + (1.0 - BETA_FIRST) * clipped
        new_second = (
            BETA_SECOND * rows(R.second_moment) + (1.0 - BETA_SECOND) * clipped * clipped
        )
        first_hat = new_first / (1.0 - BETA_FIRST**STEP)
        second_hat = new_second / (1.0 - BETA_SECOND**STEP)
        new_params = params - LEARN_RATE * (
            first_hat / (jnp.sqrt(second_hat) + EPS_ADAM) + WEIGHT_DECAY * params
        )
        states.append((new_params, new_first, new_second))
    for at, k in enumerate(GIVEN[2:5]):
        for b in range(2):
            held[k][b : b + 1, :] = states[b][at].reshape(1, n)
        going[k].start()
    R.params_copy[...] = R.new_params[...].astype(BF16)
    going["params_copy"].start()
    for copy in going.values():
        copy.wait()


def per_device(n_win, n_fsdp, tokens, cotangent, crop_ids, params, first_moment, second_moment):
    ints, marks = constant_tables()
    extent = tokens.shape[1]
    shard = params.shape[1] // 128
    held = round_up(shard, 16)
    n_x = near_extent(n_win)
    n_near, n_z = n_fsdp * n_x, n_win // n_x
    piece = round_up(-(-shard // n_x), 16)
    padded = piece * n_x
    rows = jax.ShapeDtypeStruct(params.shape, F32)
    cells = jax.ShapeDtypeStruct((extent, SY, SZ * C), BF16)
    inputs = dict(
        tokens=tokens[0],
        cotangent=cotangent[0],
        crop=crop_ids,
        ints=ints,
        marks=marks,
        params=params,
    )
    outputs = dict(
        block_out=cells,
        input_grad=cells,
        grad_norm=jax.ShapeDtypeStruct((1, 1), F32),
        grads=jax.ShapeDtypeStruct((2, padded, 128), BF16),
    )
    V = pltpu.VMEM
    edge = V((SHIFT, SY, SZ * C), BF16)
    scratch = dict(
        gathered=V((n_fsdp, 2, held, 128), BF16),
        edge=edge,
        edge_in=edge,
        edge_back=edge,
        halo=V((7, C, 128), BF16),
        halo_in=V((7, C, 128), BF16),
        halo_back=V((7, C, 128), BF16),
        halo_back_in=V((7, C, 128), BF16),
        outgoing=V((2, n_fsdp, padded, 128), BF16),
        incoming=V((2, n_near, piece, 128), BF16),
        parts=V((2, n_z, piece, 128), BF16),
        norms=V((n_near, 8, 128), F32),
        select=V((2, 896, 2 * QLANE), BF16),
        place=V((896, QLANE), BF16),
        spread=V((176, 49 * 128), BF16),
        flat=V((FLAT + 8, 128), F32),
        wide=V((3, 384, 128), F32),
        tiles=V((80 * 56, 128), F32),
        square=V((128, 1408), F32),
        tall=V((1408, 128), F32),
        grid=V((C, 17 * 128), BF16),
        grid_two=V((C, 17 * 128), BF16),
        kept=V((SZ, C, 128), F32),
        windows=V((4, C, QLANE), F32),
        deltas=V((4, C, QLANE), F32),
        bars=V((32, QLANE), F32),
        wide_total=V((HEADS, KROW, QLANE), F32),
    )
    for k, (shape, kind) in WEIGHT_SHAPES.items():
        scratch["w_" + k] = V(shape, kind)
    for k in ("cols", "q_n", "kv_n", "proj_n", "one_n", "two_n"):
        scratch["k_" + k] = V(*WEIGHT_SHAPES[k])
    for k, (shape, kind) in SAVED_SHAPES.items():
        scratch["s_" + k] = V((5, *shape), kind)
    for k, (shape, kind) in GRAD_SHAPES.items():
        scratch["g_" + k] = V(shape, kind)
    copies = 2 * (n_fsdp - 1) + 3 * (n_near - 1) + 2 * (n_z - 1) + 2 * (n_x - 1) + 6
    for k in STAGED:
        scratch[k] = V(inputs[k].shape, inputs[k].dtype)
    for k in RESULTS:
        scratch[k] = V(outputs[k].shape, outputs[k].dtype)
    scratch["local"] = pltpu.SemaphoreType.DMA((len(STAGED) + len(RESULTS),))
    scratch["send"] = pltpu.SemaphoreType.DMA((copies,))
    scratch["recv"] = pltpu.SemaphoreType.DMA((copies,))
    outside = {k: "hbm_" + k if k in STAGED + RESULTS else k for k in [*inputs, *outputs]}
    names = [*outside.values(), *scratch]
    vmem = pl.BlockSpec(memory_space=pltpu.VMEM)
    hbm = pl.BlockSpec(memory_space=pltpu.HBM)
    smem = pl.BlockSpec(memory_space=pltpu.SMEM)
    results = pl.pallas_call(
        functools.partial(step_kernel, n_win, n_fsdp, names),
        out_shape=tuple(outputs.values()),
        in_specs=[smem if k == "crop" else hbm if k in STAGED else vmem for k in inputs],
        out_specs=tuple(smem if k == "grad_norm" else hbm for k in outputs),
        scratch_shapes=list(scratch.values()),
        compiler_params=pltpu.CompilerParams(
            collective_id=0 if n_win * n_fsdp > 1 else None,
            has_side_effects=True,
            vmem_limit_bytes=66 * 1024 * 1024 - 2 * 1024 * 1024,
        ),
        name="layer_step",
    )(*inputs.values())
    taken = dict(zip(outputs, results))
    taken.update(params=params, first_moment=first_moment, second_moment=second_moment)
    given = dict(
        block_out=cells,
        input_grad=cells,
        grad_norm=outputs["grad_norm"],
        new_params=rows,
        new_first=rows,
        new_second=rows,
        params_copy=jax.ShapeDtypeStruct(params.shape, BF16),
    )
    inside = {k: V(taken[k].shape, taken[k].dtype) for k in TAKEN}
    inside.update({k: V(given[k].shape, given[k].dtype) for k in GIVEN})
    inside["local"] = pltpu.SemaphoreType.DMA((len(TAKEN) + len(GIVEN),))
    names = [k if k == "grad_norm" else "in_" + k for k in taken]
    names += ["out_" + k for k in given] + [*inside]
    results = pl.pallas_call(
        functools.partial(optimizer_kernel, names),
        out_shape=tuple(given.values()),
        in_specs=[smem if k == "grad_norm" else hbm for k in taken],
        out_specs=tuple(smem if k == "grad_norm" else hbm for k in given),
        scratch_shapes=list(inside.values()),
        name="optimizer",
    )(*taken.values())
    block_out, input_grad, grad_norm, *states = results
    return (block_out[None], input_grad[None], grad_norm[0, 0], *states)


def solution(mesh):
    data = P("fsdp", "win", None, None)
    state = P(None, "fsdp")
    return jax.shard_map(
        functools.partial(per_device, mesh.shape["win"], mesh.shape["fsdp"]),
        mesh=mesh,
        in_specs=(data, data, P("fsdp", None), state, state, state),
        out_specs=(data, data, P(), state, state, state, state),
        check_vma=False,
    )
```

```python
import functools
from types import SimpleNamespace as Names

import jax
import jax.numpy as jnp
import numpy as np
from jax import lax
from jax.experimental import pallas as pl
from jax.experimental.pallas import tpu as pltpu
from jax.sharding import PartitionSpec as P

C = 96
HEADS = 6
HEAD = 16
HID = 384
WS = 7
SHIFT = 3
SY = 14
SZ = 14
BPAD = 124928
STEP = 5
EPS_NORM = 1e-05
CLIP_LIMIT = 1.0
LEARN_RATE = 0.4
BETA_FIRST = 0.9
BETA_SECOND = 0.999
WEIGHT_DECAY = 0.05
EPS_ADAM = 1e-08
BIG = 1e30
LOG2E = 1.4426950408889634
LN2 = 0.6931471805599453

CELLS = WS**3
KROW = 352
QLANE = 384
FLAT = BPAD // 128
ROW_PROJ = 216
ROW_ONE = 288
ROW_TWO = 576
ROW_TABLE = 864
ROW_TAIL = 966
V_GAIN1, V_BIAS1, V_BQ, V_BV, V_BPROJ, V_GAIN2, V_BIAS2, V_BHID, V_BOUT = (
    0, 96, 192, 288, 384, 480, 576, 672, 1056,
)

F32 = jnp.float32
BF16 = jnp.bfloat16


def nn(a, b):
    return lax.dot_general(a, b, (((1,), (0,)), ((), ())), preferred_element_type=F32)


def nt(a, b):
    return lax.dot_general(a, b, (((1,), (1,)), ((), ())), preferred_element_type=F32)


def iota(shape, dim):
    return lax.broadcasted_iota(jnp.int32, shape, dim)


def roll(x, by):
    by = by % 128
    return x if by == 0 else pltpu.roll(x, by, 1)


def skew(x, by):
    while by > 0:
        some = min(1 << (by.bit_length() - 1), 16)
        x = pltpu.roll(x, 0, 1, stride=some, stride_axis=0)
        by -= some
    return x


def constant_tables():
    t = np.arange(QLANE)
    live = t < CELLS
    z, x, y = t // 49, t % 49 // 7, t % 7
    ints = np.full((8, QLANE), -1, np.int32)
    for s in range(2):
        for wy in range(2):
            cell_y = (y + 7 * wy + SHIFT * s) % SY
            ints[2 * s + wy] = np.where(live, z * 128 + x * 16 + cell_y, -1)
    ints[4] = np.where(live, z * 128 + t % 49, -1)
    ints[5] = np.where(live, x, -1)
    lane = np.arange(128)
    ints[6, :128] = np.where(lane < 49, 13 * (lane // 7) + lane % 7, -1000)
    marks = np.zeros((64, QLANE), np.float32)
    for i in range(7):
        marks[i] = live & (x == i)
        marks[7 + i] = live & (y == i)
        marks[14 + i] = live & (z == i)
        marks[32 + 7 + i] = live & ((i >= 4) != (y >= 4))
        marks[32 + 14 + i] = live & ((i >= 4) != (z >= 4))
    return jnp.asarray(ints), jnp.asarray(marks, BF16)


def unit_copy(pieces, units):
    out = None
    for at, unit in enumerate(units):
        if unit is None:
            continue
        i, g = unit
        moved = roll(pieces[i], 32 * (at - g))
        group = iota(moved.shape, 1) // 32
        base = jnp.zeros_like(moved) if out is None else out
        out = jnp.where(group == at, moved, base)
    return out


def read_matrix(flat, base, rows, width, store):
    units = width // 32
    if units % 4 == 0:
        step = units // 4
        for o in range(step):
            store(0, 1, o, flat[pl.ds(base + o, rows, stride=step), :])
        return
    groups = rows // 4
    loaded = [flat[pl.ds(base + o, groups, stride=units), :] for o in range(units)]
    for j in range(4):
        for p in range(units // 3):
            first = units * j + 3 * p
            store(j, 4, p, unit_copy(loaded, [divmod(first + s, 4) for s in range(3)] + [None]))


def write_matrix(flat, base, rows, width, load):
    units = width // 32
    if units % 4 == 0:
        step = units // 4
        for o in range(step):
            flat[pl.ds(base + o, rows, stride=step), :] = load(0, 1, o)
        return
    groups = rows // 4
    parts = units // 3
    loaded = [load(j, 4, p) for j in range(4) for p in range(parts)]
    for o in range(units):
        flat[pl.ds(base + o, groups, stride=units), :] = unit_copy(
            loaded, [divmod(4 * o + g, 3) for g in range(4)]
        )


def build_selectors(ints, select, place, spread):
    for s in range(2):
        for wy in range(2):
            need = ints[2 * s + wy : 2 * s + wy + 1, :]
            for r in range(7):
                row = iota((128, QLANE), 0) + 128 * r
                select[s, 128 * r : 128 * r + 128, QLANE * wy : QLANE * wy + QLANE] = jnp.where(
                    row == need, 1.0, 0.0
                ).astype(BF16)
    need = ints[4:5, :]
    for r in range(7):
        row = iota((128, QLANE), 0) + 128 * r
        place[128 * r : 128 * r + 128, :] = jnp.where(row == need, 1.0, 0.0).astype(BF16)
    gap = iota((176, 128), 0) - ints[6:7, :128]
    for k in range(49):
        hit = gap == 84 - 13 * (k // 7) - k % 7
        spread[:, 128 * k : 128 * k + 128] = jnp.where(hit, 1.0, 0.0).astype(BF16)


def table_pick(second):
    row = iota((176, 104), 0)
    col = iota((176, 104), 1) - second
    at = 128 * col
    start = 78 * row
    hit = (start >= at) & (start < at + 128) & (row < 169)
    return jnp.where(hit, 1.0, 0.0).astype(BF16)


def table_start():
    row = iota((176, 128), 0)
    return jnp.bitwise_and(78 * row, 127)


def build_table(flat, spread, place, tiles, table):
    rows = flat[ROW_TABLE : ROW_TABLE + 104, :].astype(BF16)
    first = skew(nn(table_pick(0), rows), 50)
    second = skew(nn(table_pick(1), rows), 50)
    lane = iota((176, 128), 1)
    mixed = jnp.where(lane + table_start() < 128, first, second)
    mixed = jnp.where((lane < 78) & (iota((176, 128), 0) < 169), mixed, 0.0)
    turned = jnp.concatenate([mixed, jnp.zeros((80, 128), F32)], axis=0).T
    cube = turned[:80, :176].astype(BF16)
    for k in range(0, 49, 2):
        some = min(2, 49 - k)
        block = nn(cube, spread[:, 128 * k : 128 * k + 128 * some])
        for i in range(some):
            tiles[pl.ds(k + i, 80, stride=56), :] = block[:, 128 * i : 128 * i + 128]

    def gathered(ck, first, last):
        return jnp.concatenate(
            [
                tiles[336 * (cq - ck + 6) : 336 * (cq - ck + 7), :].astype(BF16)
                for cq in range(first, last)
            ],
            axis=1,
        )

    for ck in range(7):
        block = jnp.concatenate(
            [
                nn(gathered(ck, 0, 6), place[0:768, 0:256]),
                nn(gathered(ck, 5, 7), place[640:896, 256:QLANE]),
            ],
            axis=1,
        )
        block = block * LOG2E
        for h in range(HEADS):
            table[h, 49 * ck : 49 * ck + 49, :] = block[56 * h : 56 * h + 49, :]
    for h in range(HEADS):
        table[h, CELLS:KROW, :] = jnp.full((KROW - CELLS, QLANE), -BIG, F32)


def collapse_table(total, wide_total, spread, place, tiles, flat):
    tiles[...] = jnp.zeros(tiles.shape, F32)
    for h in range(HEADS):
        wide_total[h] = total[h].astype(F32)
    for ck in range(7):
        lhs = jnp.concatenate(
            [wide_total[h, 49 * ck : 49 * ck + 56, :] for h in range(HEADS)], axis=0
        ).astype(BF16)
        for cq, start, end in ((0, 0, 128), (2, 0, 256), (4, 128, 384), (6, 256, 384)):
            some = min(2, 7 - cq)
            block = nt(lhs[:, start:end], place[128 * cq : 128 * cq + 128 * some, start:end])
            for i in range(some):
                dc = cq + i - ck + 6
                tiles[336 * dc : 336 * dc + 336, :] += block[:, 128 * i : 128 * i + 128]
    lhs = jnp.concatenate(
        [tiles[pl.ds(k, 80, stride=56), :].astype(BF16) for k in range(49)], axis=1
    )
    cube = nt(lhs, spread[...])
    wide = jnp.concatenate([cube, jnp.zeros((80, 80), F32)], axis=1)
    wide = jnp.concatenate([wide, jnp.zeros((48, 256), F32)], axis=0)
    mixed = wide.T[:176, :]
    mixed = skew(mixed, 78)
    fits = iota((176, 128), 1) >= table_start()
    lane = iota((176, 128), 1)
    length = jnp.bitwise_and(lane - table_start(), 127)
    live = (length < 78) & (iota((176, 128), 0) < 169)
    head = jnp.where(fits & live, mixed, 0.0).astype(BF16)
    rest = jnp.where(jnp.logical_not(fits) & live, mixed, 0.0).astype(BF16)

    def tn(a, b):
        return lax.dot_general(a, b, (((0,), (0,)), ((), ())), preferred_element_type=F32)

    return tn(table_pick(0), head) + tn(table_pick(1), rest)


def tail_vector(tail, start, width):
    o, at = divmod(start, 128)
    lane = iota((1, 128), 1)
    out = roll(tail[o : o + 1, :], -at)
    if at + width > 128:
        out = jnp.where(lane < 128 - at, out, roll(tail[o + 1 : o + 2, :], -at))
    return jnp.where(lane < width, out, 0.0)


def prepare(flat, W, wide, spread, place, tiles):
    rows = flat[ROW_TAIL : ROW_TAIL + 16, :]
    lane = iota((9, 128), 1)
    tail = jnp.where(lane < 2, roll(rows[:9], 2), roll(rows[1:10], 2))
    turned = jnp.concatenate([tail, jnp.zeros((119, 128), F32)], axis=0).T
    for o in range(9):
        W.cols[128 * o : 128 * o + 128, :] = jnp.broadcast_to(turned[:, o : o + 1], (128, 128))

    def into(j, step, p, value):
        wide[p, pl.ds(j, value.shape[0], stride=step), :] = value

    def finish(p, bias):
        wide[p, 96:97, :] = bias
        wide[p, 97:128, :] = jnp.zeros((31, 128), F32)

    read_matrix(flat, 0, C, 3 * C, into)
    finish(0, tail_vector(tail, V_BQ, C))
    finish(1, jnp.zeros((1, 128), F32))
    finish(2, tail_vector(tail, V_BV, C))
    W.q_n[...] = wide[0, 0:96, :].astype(BF16)
    for p in range(1, 3):
        W.kv_n[:, 128 * p - 128 : 128 * p] = wide[p, 0:96, :].astype(BF16)
    for p in range(3):
        W.qkv_t[96 * p : 96 * p + 96, :] = wide[p, 0:128, :].T[:96].astype(BF16)

    read_matrix(flat, ROW_PROJ, C, C, into)
    finish(0, tail_vector(tail, V_BPROJ, C))
    W.proj_n[...] = wide[0, 0:96, :].astype(BF16)
    W.proj_t[...] = wide[0, 0:128, :].T[:96].astype(BF16)

    read_matrix(flat, ROW_ONE, C, HID, into)
    for p in range(3):
        finish(p, tail_vector(tail, V_BHID + 128 * p, 128))
        W.one_n[:, 128 * p : 128 * p + 128] = wide[p, 0:96, :].astype(BF16)
        W.one_t[128 * p : 128 * p + 128, :] = wide[p, 0:128, :].T.astype(BF16)

    read_matrix(flat, ROW_TWO, HID, C, into)
    W.two_n[...] = wide[0].astype(BF16)
    for p in range(3):
        W.two_t[:, 128 * p : 128 * p + 128] = wide[0, 128 * p : 128 * p + 128, :].T[:96].astype(
            BF16
        )
    build_table(flat, spread, place, tiles, W.table)


WEIGHT_SHAPES = dict(
    cols=((1152, 128), F32),
    q_n=((96, 128), BF16),
    kv_n=((96, 256), BF16),
    qkv_t=((288, 128), BF16),
    proj_n=((96, 128), BF16),
    proj_t=((96, 128), BF16),
    one_n=((96, 384), BF16),
    one_t=((384, 128), BF16),
    two_n=((384, 128), BF16),
    two_t=((96, 384), BF16),
    table=((HEADS, KROW, QLANE), F32),
)


SAVED_SHAPES = dict(
    normed=((128, QLANE), BF16),
    hat=((96, QLANE), F32),
    scale=((8, QLANE), F32),
    qkv=((288, QLANE), BF16),
    probs=((HEADS, KROW, QLANE), BF16),
    inverse=((8, QLANE), F32),
    attended=((128, QLANE), BF16),
    hat_two=((96, QLANE), F32),
    scale_two=((8, QLANE), F32),
    normed_two=((128, QLANE), BF16),
    slope=((HID, QLANE), BF16),
    active=((HID, QLANE), BF16),
)

GRAD_SHAPES = dict(
    q=((112, 128), F32),
    kv=((2, 112, 128), F32),
    proj=((112, 128), F32),
    one=((112, 384), F32),
    two=((400, 128), F32),
    gain1=((96, 128), F32),
    bias1=((96, 128), F32),
    gain2=((96, 128), F32),
    bias2=((96, 128), F32),
    total=((HEADS, KROW, QLANE), BF16),
)


def column(W, start, rows=96):
    part = W.cols[start : start + rows, :]
    return jnp.concatenate([part, part, part], axis=1)


def extended(rows):
    width = rows.shape[1]
    return jnp.concatenate([rows, jnp.ones((16, width), BF16), jnp.zeros((16, width), BF16)], axis=0)


def standardize(x):
    centered = x - jnp.mean(x, axis=0, keepdims=True)
    variance = jnp.mean(centered * centered, axis=0, keepdims=True)
    scale = lax.rsqrt(variance + EPS_NORM)
    return centered * scale, scale


def at_head(h, rows, tail):
    width = rows.shape[1]
    parts = []
    if h > 0:
        parts.append(jnp.zeros((16 * h, width), BF16))
    parts.append(rows)
    if h < HEADS - 1:
        parts.append(jnp.zeros((16 * (HEADS - 1 - h), width), BF16))
    return jnp.concatenate(parts + [tail], axis=0)


def scaled_queries(qkv):
    return (qkv[0:96].astype(F32) * (HEAD**-0.5 * LOG2E)).astype(BF16)


def window_norm(x, S, s):
    hat, scale = standardize(x)
    S.hat[s] = hat
    S.scale[s, 0:1] = scale


def window_forward(x, W, S, s, marks, barred):
    hat = S.hat[s]
    normed = extended((hat * column(W, V_GAIN1) + column(W, V_BIAS1)).astype(BF16))
    S.normed[s] = normed
    qkv = nn(W.qkv_t[...], normed).astype(BF16)
    S.qkv[s] = qkv
    queries = scaled_queries(qkv)
    keys = jnp.concatenate([qkv[96:192], marks[0:32, :]], axis=0).T[:KROW]
    ones = jnp.ones((16, KROW), BF16)

    def pair_scores(p):
        sides = [at_head(h, queries[16 * h : 16 * h + 16], barred) for h in (2 * p, 2 * p + 1)]
        return nn(keys, jnp.concatenate(sides, axis=1))

    parts, late = [], []

    def head_values(h, probs):
        values = jnp.concatenate([qkv[192 + 16 * h : 208 + 16 * h, :KROW], ones], axis=0)
        mixed = nn(values, probs)
        inverse = 1.0 / mixed[16:17]
        S.inverse[s, h : h + 1] = inverse
        parts.append((mixed[:16] * inverse).astype(BF16))

    coming = pair_scores(0)
    for h in range(HEADS):
        if h % 2 == 0:
            pair = coming
            if h + 2 < HEADS:
                coming = pair_scores(h // 2 + 1)
        scores = pair[:, QLANE * (h % 2) : QLANE * (h % 2) + QLANE] + W.table[h]
        highest = jnp.max(scores, axis=0, keepdims=True)
        probs = jnp.exp2(scores - highest).astype(BF16)
        S.probs[s, h] = probs
        late.append((h, probs))
        if len(late) > 1:
            head_values(*late.pop(0))
    head_values(*late.pop(0))
    attended = extended(jnp.concatenate(parts, axis=0))
    S.attended[s] = attended
    branch = nn(W.proj_t[...], attended).astype(BF16)
    middle = x + branch.astype(F32)
    hat, scale = standardize(middle)
    S.hat_two[s] = hat
    S.scale_two[s, 0:1] = scale
    normed_two = extended((hat * column(W, V_GAIN2) + column(W, V_BIAS2)).astype(BF16))
    S.normed_two[s] = normed_two
    hidden = nn(W.one_t[...], normed_two)
    share = 0.5 + 0.5 * lax.erf(hidden * (0.5**0.5))
    active = (hidden * share).astype(BF16)
    S.active[s] = active
    slope = share + hidden * jnp.exp2(hidden * hidden * (-0.5 * LOG2E)) * 0.3989422804014327
    S.slope[s] = slope.astype(BF16)
    return middle + nn(W.two_t[...], active) + column(W, V_BOUT)


def fold(x):
    return x[:, 0:128] + x[:, 128:256] + x[:, 256:384]


def norm_backward(grad, hat, scale, gain):
    scaled = grad * gain
    mean_one = jnp.mean(scaled, axis=0, keepdims=True)
    mean_two = jnp.mean(scaled * hat, axis=0, keepdims=True)
    return scale * (scaled - mean_one - hat * mean_two)


def window_backward(grad, W, S, s, G, marks, barred):
    result = extended(grad.astype(BF16))
    active = S.active[s]
    G.two[...] += nt(jnp.concatenate([active, jnp.ones((16, QLANE), BF16)], axis=0), result)
    hidden = (nn(W.two_n[...], result) * S.slope[s].astype(F32)).astype(BF16)
    G.one[...] += nt(S.normed_two[s, 0:112], hidden)
    d_normed = nn(W.one_n[...], hidden)
    hat = S.hat_two[s]
    G.gain2[...] += fold(d_normed * hat)
    G.bias2[...] += fold(d_normed)
    d_middle = grad + norm_backward(d_normed, hat, S.scale_two[s, 0:1], column(W, V_GAIN2))
    d_branch = extended(d_middle.astype(BF16))
    attended = S.attended[s]
    G.proj[...] += nt(attended[0:112], d_branch)
    d_attended = nn(W.proj_n[...], d_branch).astype(BF16).astype(F32)
    product = d_attended * attended[0:96].astype(F32)
    qkv = S.qkv[s]
    queries = scaled_queries(qkv)
    values = extended(qkv[192:288]).T[:KROW]
    row = iota((32, QLANE), 0)
    parts, d_keys, d_values = [], [], []

    def head_gradient(h):
        inverse = S.inverse[s, h : h + 1]
        inner = jnp.sum(product[16 * h : 16 * h + 16], axis=0, keepdims=True) * inverse
        high = inner.astype(BF16)
        low = (inner - high.astype(F32)).astype(BF16)
        less = jnp.where(row == 0, -high.astype(F32), jnp.where(row == 1, -low.astype(F32), 0.0))
        rows = (d_attended[16 * h : 16 * h + 16] * inverse).astype(BF16)
        return rows, at_head(h, rows, less.astype(BF16))

    def pair_gradient(p):
        d_outs = [head_gradient(h) for h in (2 * p, 2 * p + 1)]
        product = nn(values, jnp.concatenate([d_out for _, d_out in d_outs], axis=1))
        return d_outs, product.astype(BF16)

    def head_products(h, d_scores, rows, probs):
        d_keys.append(nt(queries[16 * h : 16 * h + 16], d_scores))
        d_values.append(nt(rows, probs))
        parts.append(nn(qkv[96 + 16 * h : 112 + 16 * h, :KROW], d_scores))

    late = []
    coming = pair_gradient(0)
    for p in range(HEADS // 2):
        d_outs, d_pair = coming
        if p + 1 < HEADS // 2:
            coming = pair_gradient(p + 1)
        for h in (2 * p, 2 * p + 1):
            probs = S.probs[s, h]
            d_scores = probs * d_pair[:, QLANE * (h % 2) : QLANE * (h % 2) + QLANE]
            G.total[h] += d_scores
            late.append((h, d_scores, d_outs[h % 2][0], probs))
            if len(late) > 6:
                head_products(*late.pop(0))
    for held in late:
        head_products(*held)
    d_queries = (jnp.concatenate(parts, axis=0) * HEAD**-0.5).astype(BF16)
    gap = jnp.zeros((32, QLANE), BF16)
    tokens_gap = jnp.zeros((96, QLANE - KROW), F32)

    def side(rows, factor):
        rows = jnp.concatenate(rows, axis=0) * factor
        return jnp.concatenate([rows, tokens_gap], axis=1).astype(BF16)

    d_pair = jnp.concatenate([side(d_keys, LN2), gap, side(d_values, 1.0), gap], axis=0)
    normed = S.normed[s, 0:112]
    G.q[:, 0:96] += nt(normed, d_queries)
    both = nt(normed, d_pair)
    for p in range(2):
        G.kv[p] += both[:, 128 * p : 128 * p + 128]
    d_normed = nn(W.q_n[:, 0:96], d_queries) + nn(W.kv_n[...], d_pair)
    hat = S.hat[s]
    G.gain1[...] += fold(d_normed * hat)
    G.bias1[...] += fold(d_normed)
    return d_middle + norm_backward(d_normed, hat, S.scale[s, 0:1], column(W, V_GAIN1))


def finish_gradients(G, matrices_done, wide_total, flat, wide, spread, place, tiles):
    def qkv_rows(j, step, p):
        if p == 0:
            return G.q[pl.ds(j, 24, stride=4), :]
        return G.kv[p - 1, pl.ds(j, 24, stride=4), :]

    write_matrix(flat, 0, C, 3 * C, qkv_rows)
    write_matrix(flat, ROW_PROJ, C, C, lambda j, step, p: G.proj[pl.ds(j, 24, stride=4), :])
    write_matrix(
        flat, ROW_ONE, C, HID, lambda j, step, p: G.one[0:96, 128 * p : 128 * p + 128]
    )
    write_matrix(flat, ROW_TWO, HID, C, lambda j, step, p: G.two[pl.ds(j, 96, stride=4), :])
    matrices_done()
    lane = iota((96, 128), 1)
    columns = jnp.zeros((96, 128), F32)
    for at, ref in enumerate([G.gain1, G.bias1, G.gain2, G.bias2]):
        columns = jnp.where(lane == at, jnp.sum(ref[...], axis=1, keepdims=True), columns)
    turned = jnp.concatenate([columns, jnp.zeros((32, 128), F32)], axis=0).T
    sources = [
        (turned[0:1], 3),
        (turned[1:2], 3),
        (G.q[96:97, :], 3),
        (G.kv[1, 96:97, :], 3),
        (G.proj[96:97, :], 3),
        (turned[2:3], 3),
        (turned[3:4], 3),
        (G.one[96:97, 0:128], 4),
        (G.one[96:97, 128:256], 4),
        (G.one[96:97, 256:384], 4),
        (G.two[384:385, :], 3),
    ]
    pieces = [source for source, _ in sources]
    units = [(i, g) for i, (_, count) in enumerate(sources) for g in range(count)]
    tail = jnp.concatenate(
        [unit_copy(pieces, units[4 * o : 4 * o + 4]) for o in range(9)], axis=0
    )
    table = collapse_table(G.total, wide_total, spread, place, tiles, flat)
    flat[ROW_TABLE:ROW_TAIL, :] = table[0:102]
    none = jnp.zeros((1, 128), F32)
    moved = roll(jnp.concatenate([none, tail, none], axis=0), 126)
    lane = iota((10, 128), 1)
    mixed = jnp.where(lane >= 126, moved[1:11], moved[0:10])
    first = jnp.where(iota((1, 128), 1) >= 126, mixed[0:1], table[102:103])
    flat[ROW_TAIL:FLAT, :] = jnp.concatenate([first, mixed[1:10]], axis=0)


def round_up(value, to):
    return -(-value // to) * to


def take_grid(row_of, square, tall, grid, wrapped):
    for x in range(7):
        square[16 * x : 16 * x + 14, 0 : SZ * C] = row_of(x)
    for i in range(11):
        tall[128 * i : 128 * i + 128, :] = square[:, 128 * i : 128 * i + 128].T
    for z in range(SZ + 3 if wrapped else SZ):
        grid[:, 128 * z : 128 * z + 128] = tall[C * (z % SZ) : C * (z % SZ) + C, :].astype(BF16)


def take_window(grid, select, s, wy, wz):
    rows = grid[:, pl.ds(pl.multiple_of(896 * wz + 384 * s, 128), 896)]
    return nn(rows, select[s, :, pl.ds(pl.multiple_of(QLANE * wy, 128), QLANE)])


def give_grid(windows, select, s, wz, put):
    both = jnp.concatenate([windows[2 * wz], windows[2 * wz + 1]], axis=1).astype(BF16)
    cells = nt(both, select[s])
    for r in range(7):
        put((r + 7 * wz + SHIFT * s) % SZ, cells[:, 128 * r : 128 * r + 128])


def give_rows(tall, square):
    for i in range(11):
        square[:, 128 * i : 128 * i + 128] = tall[128 * i : 128 * i + 128, :].T


def crop_bars(crop, ints, first, total):
    ids = [crop[0, lax.rem(first + a, total)] for a in range(7)]
    at = ints[5:6, :]
    own = jnp.zeros((1, QLANE), jnp.int32)
    for a in range(7):
        own = jnp.where(at == a, ids[a], own)
    row = iota((32, QLANE), 0)
    key = jnp.full((32, QLANE), -1, jnp.int32)
    for a in range(7):
        key = jnp.where(row == a, ids[a], key)
    return jnp.where((row < 7) & (key != own), -BIG, 0.0)


def shift_bars(marks, wy, wz):
    row = iota((32, QLANE), 0)
    factor = jnp.where(row < 14, wy, wz).astype(F32) * -BIG
    return marks[32:64, :].astype(F32) * factor


STAGED = ("params", "tokens", "cotangent")
RESULTS = ("block_out", "input_grad", "grads")
TAKEN = ("block_out", "input_grad", "grads", "params", "first_moment", "second_moment")
GIVEN = ("block_out", "input_grad", "new_params", "new_first", "new_second", "params_copy")


def near_extent(n_win):
    n_x = 1
    while 4 * n_x * n_x <= n_win:
        n_x *= 2
    return n_x


def step_kernel(n_win, n_fsdp, names, *refs):
    held = dict(zip(names, refs))
    R = Names(**held)
    W = Names(**{k: held["w_" + k] for k in WEIGHT_SHAPES})
    S = Names(**{k: held["s_" + k] for k in SAVED_SHAPES})
    G = Names(**{k: held["g_" + k] for k in GRAD_SHAPES})
    tokens, cotangent, crop = R.tokens, R.cotangent, R.crop
    ints, marks = R.ints, R.marks
    select, place, spread = R.select, R.place, R.spread
    flat, wide, tiles = R.flat, R.wide, R.tiles
    square, tall = R.square, R.tall
    send, recv = R.send, R.recv
    shard = FLAT // n_fsdp
    extent = tokens.shape[0]
    total = n_win * extent
    me_win, me_fsdp = lax.axis_index("win"), lax.axis_index("fsdp")
    left, right = lax.rem(me_win + n_win - 1, n_win), lax.rem(me_win + 1, n_win)
    n_x = near_extent(n_win)
    n_z = n_win // n_x
    me_x, me_z = lax.rem(me_win, n_x), me_win // n_x
    me_near = me_fsdp * n_x + me_x
    near = []
    for k in range(1, n_fsdp * n_x):
        f, x = lax.rem(me_fsdp + k // n_x, n_fsdp), lax.rem(me_x + k % n_x, n_x)
        near.append((k, f, x, {"win": me_z * n_x + x, "fsdp": f}))
    far = [(k, {"win": lax.rem(me_z + k, n_z) * n_x + me_x}) for k in range(1, n_z)]
    sides = [{"win": left}, {"win": right}] if n_win > 1 else []
    slots = {}

    def remote(name, src, dst, to):
        slot = slots.setdefault(name, len(slots))
        return pltpu.make_async_remote_copy(
            src_ref=src,
            dst_ref=dst,
            send_sem=send.at[slot],
            recv_sem=recv.at[slot],
            device_id=to,
            device_id_type=pl.DeviceIdType.MESH,
        )

    def start(copies):
        for copy in copies:
            copy.start()
        return copies

    def neighbour(name, src, dst, to):
        if n_win > 1:
            return start([remote(name, src, dst, {"win": to})])
        dst[...] = src[...]
        return []

    def fetch(k):
        at = STAGED.index(k)
        return pltpu.make_async_copy(held["hbm_" + k], held[k], R.local.at[at])

    def flush(k):
        at = len(STAGED) + RESULTS.index(k)
        return pltpu.make_async_copy(held[k], held["hbm_" + k], R.local.at[at])

    def wait(copies):
        for copy in copies:
            copy.wait()

    start([fetch(k) for k in STAGED])
    if n_win * n_fsdp > 1:
        barrier = pltpu.get_barrier_semaphore()
        peers = [peer[-1] for peer in near + far] + sides
        for peer in peers:
            pl.semaphore_signal(
                barrier, inc=1, device_id=peer, device_id_type=pl.DeviceIdType.MESH
            )
    gathered = R.gathered
    fetch("params").wait()
    for b in range(2):
        rows = R.params[b : b + 1, :].reshape(shard, 128)
        gathered[me_fsdp, b, 0:shard, :] = rows.astype(BF16)
    fetch("cotangent").wait()
    R.edge[...] = cotangent[0:SHIFT]
    build_selectors(ints, select, place, spread)
    if n_win * n_fsdp > 1:
        pl.semaphore_wait(barrier, len(peers))

    weights_in = []
    for b in range(2):
        mine = gathered.at[me_fsdp, b]
        copies = []
        for k in range(1, n_fsdp):
            to = {"fsdp": lax.rem(me_fsdp + k, n_fsdp)}
            copies.append(remote(("weights", b, k), mine, mine, to))
        weights_in.append(start(copies))
    halo_in = neighbour("halo", R.edge, R.edge_in, left)
    square[...] = jnp.zeros(square.shape, F32)
    fetch("tokens").wait()
    take_grid(lambda x: tokens[x].astype(F32), square, tall, R.grid, False)
    windows, deltas = R.windows, R.deltas

    def first_window(w, carry):
        x = take_window(R.grid, select, 0, lax.rem(w, 2), w // 2)
        windows[w] = x
        window_norm(x, S, w)
        return carry

    lax.fori_loop(0, 4, first_window, 0)

    def clear(ref):
        ref[...] = jnp.zeros(ref.shape, ref.dtype)

    for ref in vars(G).values():
        clear(ref)
    wait(halo_in)

    def shifted_cotangent(x):
        return (cotangent[x + SHIFT] if x < 7 - SHIFT else R.edge_in[x - 7 + SHIFT]).astype(F32)

    take_grid(shifted_cotangent, square, tall, R.grid_two, True)

    def spread_weights(b):
        wait(weights_in[b])
        for f in range(n_fsdp):
            flat[shard * f : shard * f + shard, :] = gathered[f, b, 0:shard, :].astype(F32)
        prepare(flat, W, wide, spread, place, tiles)

    spread_weights(0)
    R.bars[...] = crop_bars(crop, ints, me_win * extent, total)

    halo, halo_back = R.halo, R.halo_back
    kept = R.kept
    lane = iota((C, 128), 1)
    slab_parts = [(0, 3), (3, 7)]

    def slab_copy(wz, name, src, dst, to):
        begin, end = slab_parts[wz]
        part = pl.ds(begin, end - begin)
        return remote((name, wz), src.at[part], dst.at[part], {"win": to})

    def pass_slab(wz, name, src, dst, to):
        if n_win > 1:
            start([slab_copy(wz, name, src, dst, to)])
        else:
            begin, end = slab_parts[wz]
            dst[begin:end] = src[begin:end]

    def wait_slab(name, src, dst, to):
        if n_win > 1:
            wait([slab_copy(wz, name, src, dst, to) for wz in range(2)])

    def put_kept(z, value):
        kept[z] = value

    def give_slices(wz):
        give_grid(windows, select, 0, wz, put_kept)
        for i in range(*slab_parts[wz]):
            pair = jnp.where(lane < 64, kept[2 * i], roll(kept[2 * i + 1], 64))
            halo[i] = pair.astype(BF16)
        pass_slab(wz, "slab", halo, R.halo_in, left)

    def first_forward(w, carry):
        windows[w] = window_forward(windows[w], W, S, w, marks, R.bars[...].astype(BF16))

        @pl.when(w == 1)
        def _():
            give_slices(0)

        return carry

    lax.fori_loop(0, 4, first_forward, 0)

    give_slices(1)
    first_weights = {}
    for k in ("cols", "q_n", "kv_n", "proj_n", "one_n", "two_n"):
        held["k_" + k][...] = held["w_" + k][...]
        first_weights[k] = held["k_" + k]
    spread_weights(1)
    wait_slab("slab", halo, R.halo_in, left)
    for z in range(SZ + 3):
        pair = R.halo_in[z % SZ // 2].astype(F32)
        if z % SZ % 2 == 0:
            pair = roll(pair, 64)
        joined = jnp.where(lane < 64, roll(kept[z % SZ], -48), pair)
        R.grid[:, 128 * z : 128 * z + 128] = joined.astype(BF16)

    R.bars[...] = crop_bars(crop, ints, me_win * extent + SHIFT, total)

    def give_back(wz):
        give_grid(deltas, select, 1, wz, put_kept)
        for at in range(*slab_parts[wz]):
            i = (at + 2) % 7
            pair = jnp.where(lane < 64, roll(kept[2 * i], 64), kept[2 * i + 1])
            halo_back[at] = pair.astype(BF16)
        pass_slab(wz, "slab_back", halo_back, R.halo_back_in, right)

    def second(w, carry):
        wy, wz = lax.rem(w, 2), w // 2
        bars = (R.bars[...] + shift_bars(marks, wy, wz)).astype(BF16)
        x = take_window(R.grid, select, 1, wy, wz)
        window_norm(x, S, 4)
        windows[w] = window_forward(x, W, S, 4, marks, bars)
        grad = take_window(R.grid_two, select, 1, wy, wz)
        deltas[w] = window_backward(grad, W, S, 4, G, marks, bars)

        @pl.when(w == 1)
        def _():
            give_back(0)

        return carry

    lax.fori_loop(0, 4, second, 0)

    give_back(1)

    def put_tall(z, value):
        tall[C * z : C * z + C, :] = value

    for wz in range(2):
        give_grid(windows, select, 1, wz, put_tall)
    give_rows(tall, square)
    for x in range(7 - SHIFT):
        R.block_out[x + SHIFT] = square[16 * x : 16 * x + 14, 0 : SZ * C].astype(BF16)
    for x in range(SHIFT):
        at = 16 * (x + 7 - SHIFT)
        R.edge[x] = square[at : at + 14, 0 : SZ * C].astype(BF16)
    out_back = neighbour("out_back", R.edge, R.edge_back, right)

    padded = R.outgoing.shape[2]
    piece = padded // n_x

    def scatter(b):
        early = ROW_TABLE // shard

        def send(first, last):
            for f in range(first, last):
                R.outgoing[b, f, 0:shard, :] = flat[shard * f : shard * f + shard, :].astype(BF16)
                if padded > shard:
                    R.outgoing[b, f, shard:padded, :] = jnp.zeros((padded - shard, 128), BF16)
            for (k, f, x, to), copy in zip(near, near_copies(b)):
                pl.when((f >= first) & (f < last))(copy.start)

        finish_gradients(
            G, lambda: send(0, early), R.wide_total, flat, wide, spread, place, tiles
        )
        send(early, n_fsdp)

    def rows_of(x):
        return pl.ds(pl.multiple_of(piece * x, 16), piece)

    own = rows_of(me_x)

    def near_copies(b):
        return [
            remote(
                ("near", b, k), R.outgoing.at[b, f, rows_of(x)], R.incoming.at[b, me_near], to
            )
            for k, f, x, to in near
        ]

    def far_copies(b):
        mine = R.parts.at[b, me_z]
        return [remote(("far", b, k), mine, mine, to) for k, to in far]

    def whole_copies(b):
        mine = R.grads.at[b, own]
        return [remote(("whole", b, k), mine, mine, to) for k, f, x, to in near if k < n_x]

    def norm_copies():
        mine = R.norms.at[me_near]
        return [remote(("norm", k), mine, mine, to) for k, f, x, to in near]

    def add_near(b):
        wait(near_copies(b))
        R.incoming[b, me_near] = R.outgoing[b, me_fsdp, own, :]
        total_rows = R.incoming[b, 0].astype(F32)
        for i in range(1, n_fsdp * n_x):
            total_rows += R.incoming[b, i].astype(F32)
        R.parts[b, me_z] = total_rows.astype(BF16)
        start(far_copies(b))

    def add_far(b):
        wait(far_copies(b))
        total_rows = R.parts[b, 0].astype(F32)
        for i in range(1, n_z):
            total_rows += R.parts[b, i].astype(F32)
        R.grads[b, own, :] = total_rows.astype(BF16)
        start(whole_copies(b))
        squares = jnp.sum((total_rows * total_rows).reshape(piece // 8, 8, 128), axis=0)
        if b == 1:
            R.norms[me_near] = squares
        else:
            R.norms[me_near] += squares
            start(norm_copies())

    scatter(1)
    wait_slab("slab_back", halo_back, R.halo_back_in, right)
    for z in range(SZ):
        pair = R.halo_back_in[(z // 2 + 5) % 7].astype(F32)
        if z % 2 == 1:
            pair = roll(pair, 64)
        joined = jnp.where(lane < 48, pair, roll(kept[z], 48))
        R.grid[:, 128 * z : 128 * z + 128] = joined.astype(BF16)
    for ref in vars(G).values():
        clear(ref)
    W0 = Names(**{**vars(W), **first_weights})

    def first_backward(w, carry):
        grad = take_window(R.grid, select, 0, lax.rem(w, 2), w // 2)
        deltas[w] = window_backward(grad, W0, S, w, G, marks, R.bars[...].astype(BF16))

        @pl.when(w == 1)
        def _():
            add_near(1)

        @pl.when(w == 2)
        def _():
            add_far(1)

        return carry

    lax.fori_loop(0, 4, first_backward, 0)
    scatter(0)
    for wz in range(2):
        give_grid(deltas, select, 0, wz, put_tall)
    give_rows(tall, square)
    for x in range(7):
        R.input_grad[x] = square[16 * x : 16 * x + 14, 0 : SZ * C].astype(BF16)
    flush("input_grad").start()
    wait(out_back)
    R.block_out[0:SHIFT] = R.edge_back[...]
    flush("block_out").start()
    add_near(0)
    wait(whole_copies(1))
    add_far(0)
    wait(whole_copies(0))
    wait(norm_copies())
    norm = R.norms[0]
    for i in range(1, n_fsdp * n_x):
        norm += R.norms[i]
    norm = jnp.sum(jnp.sum(norm, axis=0, keepdims=True), axis=1, keepdims=True)
    norm = jnp.broadcast_to(jnp.sqrt(norm), (1, 128))
    R.grad_norm[0, 0] = norm[0, 0]
    flush("grads").start()
    wait([flush(k) for k in RESULTS])


def optimizer_kernel(names, *refs):
    R = Names(**dict(zip(names, refs)))
    held = vars(R)
    n = R.params.shape[1]

    def move(i, k, out):
        ends = (held[k], held["out_" + k]) if out else (held["in_" + k], held[k])
        return pltpu.make_async_copy(*ends, R.local.at[i])

    coming = {k: move(i, k, False) for i, k in enumerate(TAKEN)}
    going = {k: move(len(TAKEN) + i, k, True) for i, k in enumerate(GIVEN)}
    for copy in coming.values():
        copy.start()
    for k in ("block_out", "input_grad"):
        coming[k].wait()
        going[k].start()
    for k in TAKEN[2:]:
        coming[k].wait()
    R.out_grad_norm[0, 0] = R.grad_norm[0, 0]
    norm = jnp.full((1, 128), R.grad_norm[0, 0], F32)
    factor = jnp.minimum(1.0, CLIP_LIMIT / (norm + 1e-06))
    states = []
    for b in range(2):

        def rows(ref):
            return ref[b : b + 1, :].reshape(n // 128, 128)

        params = rows(R.params)
        clipped = R.grads[b, 0 : n // 128, :].astype(F32) * factor
        new_first = BETA_FIRST * rows(R.first_moment) + (1.0 - BETA_FIRST) * clipped
        new_second = (
            BETA_SECOND * rows(R.second_moment) + (1.0 - BETA_SECOND) * clipped * clipped
        )
        first_hat = new_first / (1.0 - BETA_FIRST**STEP)
        second_hat = new_second / (1.0 - BETA_SECOND**STEP)
        new_params = params - LEARN_RATE * (
            first_hat / (jnp.sqrt(second_hat) + EPS_ADAM) + WEIGHT_DECAY * params
        )
        states.append((new_params, new_first, new_second))
    for at, k in enumerate(GIVEN[2:5]):
        for b in range(2):
            held[k][b : b + 1, :] = states[b][at].reshape(1, n)
        going[k].start()
    R.params_copy[...] = R.new_params[...].astype(BF16)
    going["params_copy"].start()
    for copy in going.values():
        copy.wait()


def per_device(n_win, n_fsdp, tokens, cotangent, crop_ids, params, first_moment, second_moment):
    ints, marks = constant_tables()
    extent = tokens.shape[1]
    shard = params.shape[1] // 128
    held = round_up(shard, 16)
    n_x = near_extent(n_win)
    n_near, n_z = n_fsdp * n_x, n_win // n_x
    piece = round_up(-(-shard // n_x), 16)
    padded = piece * n_x
    rows = jax.ShapeDtypeStruct(params.shape, F32)
    cells = jax.ShapeDtypeStruct((extent, SY, SZ * C), BF16)
    inputs = dict(
        tokens=tokens[0],
        cotangent=cotangent[0],
        crop=crop_ids,
        ints=ints,
        marks=marks,
        params=params,
    )
    outputs = dict(
        block_out=cells,
        input_grad=cells,
        grad_norm=jax.ShapeDtypeStruct((1, 1), F32),
        grads=jax.ShapeDtypeStruct((2, padded, 128), BF16),
    )
    V = pltpu.VMEM
    edge = V((SHIFT, SY, SZ * C), BF16)
    scratch = dict(
        gathered=V((n_fsdp, 2, held, 128), BF16),
        edge=edge,
        edge_in=edge,
        edge_back=edge,
        halo=V((7, C, 128), BF16),
        halo_in=V((7, C, 128), BF16),
        halo_back=V((7, C, 128), BF16),
        halo_back_in=V((7, C, 128), BF16),
        outgoing=V((2, n_fsdp, padded, 128), BF16),
        incoming=V((2, n_near, piece, 128), BF16),
        parts=V((2, n_z, piece, 128), BF16),
        norms=V((n_near, 8, 128), F32),
        select=V((2, 896, 2 * QLANE), BF16),
        place=V((896, QLANE), BF16),
        spread=V((176, 49 * 128), BF16),
        flat=V((FLAT + 8, 128), F32),
        wide=V((3, 384, 128), F32),
        tiles=V((80 * 56, 128), F32),
        square=V((128, 1408), F32),
        tall=V((1408, 128), F32),
        grid=V((C, 17 * 128), BF16),
        grid_two=V((C, 17 * 128), BF16),
        kept=V((SZ, C, 128), F32),
        windows=V((4, C, QLANE), F32),
        deltas=V((4, C, QLANE), F32),
        bars=V((32, QLANE), F32),
        wide_total=V((HEADS, KROW, QLANE), F32),
    )
    for k, (shape, kind) in WEIGHT_SHAPES.items():
        scratch["w_" + k] = V(shape, kind)
    for k in ("cols", "q_n", "kv_n", "proj_n", "one_n", "two_n"):
        scratch["k_" + k] = V(*WEIGHT_SHAPES[k])
    for k, (shape, kind) in SAVED_SHAPES.items():
        scratch["s_" + k] = V((5, *shape), kind)
    for k, (shape, kind) in GRAD_SHAPES.items():
        scratch["g_" + k] = V(shape, kind)
    copies = 2 * (n_fsdp - 1) + 3 * (n_near - 1) + 2 * (n_z - 1) + 2 * (n_x - 1) + 6
    for k in STAGED:
        scratch[k] = V(inputs[k].shape, inputs[k].dtype)
    for k in RESULTS:
        scratch[k] = V(outputs[k].shape, outputs[k].dtype)
    scratch["local"] = pltpu.SemaphoreType.DMA((len(STAGED) + len(RESULTS),))
    scratch["send"] = pltpu.SemaphoreType.DMA((copies,))
    scratch["recv"] = pltpu.SemaphoreType.DMA((copies,))
    outside = {k: "hbm_" + k if k in STAGED + RESULTS else k for k in [*inputs, *outputs]}
    names = [*outside.values(), *scratch]
    vmem = pl.BlockSpec(memory_space=pltpu.VMEM)
    hbm = pl.BlockSpec(memory_space=pltpu.HBM)
    smem = pl.BlockSpec(memory_space=pltpu.SMEM)
    results = pl.pallas_call(
        functools.partial(step_kernel, n_win, n_fsdp, names),
        out_shape=tuple(outputs.values()),
        in_specs=[smem if k == "crop" else hbm if k in STAGED else vmem for k in inputs],
        out_specs=tuple(smem if k == "grad_norm" else hbm for k in outputs),
        scratch_shapes=list(scratch.values()),
        compiler_params=pltpu.CompilerParams(
            collective_id=0 if n_win * n_fsdp > 1 else None,
            has_side_effects=True,
            vmem_limit_bytes=66 * 1024 * 1024 - 2 * 1024 * 1024,
        ),
        name="layer_step",
    )(*inputs.values())
    taken = dict(zip(outputs, results))
    taken.update(params=params, first_moment=first_moment, second_moment=second_moment)
    given = dict(
        block_out=cells,
        input_grad=cells,
        grad_norm=outputs["grad_norm"],
        new_params=rows,
        new_first=rows,
        new_second=rows,
        params_copy=jax.ShapeDtypeStruct(params.shape, BF16),
    )
    inside = {k: V(taken[k].shape, taken[k].dtype) for k in TAKEN}
    inside.update({k: V(given[k].shape, given[k].dtype) for k in GIVEN})
    inside["local"] = pltpu.SemaphoreType.DMA((len(TAKEN) + len(GIVEN),))
    names = [k if k == "grad_norm" else "in_" + k for k in taken]
    names += ["out_" + k for k in given] + [*inside]
    results = pl.pallas_call(
        functools.partial(optimizer_kernel, names),
        out_shape=tuple(given.values()),
        in_specs=[smem if k == "grad_norm" else hbm for k in taken],
        out_specs=tuple(smem if k == "grad_norm" else hbm for k in given),
        scratch_shapes=list(inside.values()),
        name="optimizer",
    )(*taken.values())
    block_out, input_grad, grad_norm, *states = results
    return (block_out[None], input_grad[None], grad_norm[0, 0], *states)


def solution(mesh):
    data = P("fsdp", "win", None, None)
    state = P(None, "fsdp")
    return jax.shard_map(
        functools.partial(per_device, mesh.shape["win"], mesh.shape["fsdp"]),
        mesh=mesh,
        in_specs=(data, data, P("fsdp", None), state, state, state),
        out_specs=(data, data, P(), state, state, state, state),
        check_vma=False,
    )
```
